32 devices in a mesh: dp: 8 (over y, x, core), tensor: 4 (over z).
Axes of the slice: x: 2, y: 2, z: 4, core: 2. Of those that a mesh axis runs over, the one named last changes fastest.
Arguments:
- tokens: bfloat16 [8192, 768], P(('dp', 'tensor')), may hold values from -6 to 6
- segments: int32 [8, 1024], P('dp'), may hold values from 0 to 15, never falling along the last dimension, each value on 1 to 128 neighbouring positions
- mask_grad: float32 [8192, 150], P(('dp', 'tensor')), may hold values from -6 to 6
- gain_one: float32 [768], P('dp'), may hold values from 0.5 to 1.5
- attend_weight: float32 [768, 2304], P('dp', 'tensor'), may hold values from -0.21875 to 0.21875
- output_weight: float32 [768, 768], P('tensor', 'dp'), may hold values from -0.875 to 0.875
- gain_two: float32 [768], P('dp'), may hold values from 0.5 to 1.5
- up_weight: float32 [768, 3072], P('dp', 'tensor'), may hold values from -0.21875 to 0.21875
- down_weight: float32 [3072, 768], P('tensor', 'dp'), may hold values from -0.109375 to 0.109375
- patch_weight: float32 [768, 768], P('dp', 'tensor'), may hold values from -0.21875 to 0.21875
- class_weight: float32 [768, 768], P('dp', 'tensor'), may hold values from -0.21875 to 0.21875
- class_embed: float32 [150, 768], P(None, 'dp'), may hold values from -6 to 6
- mean_gain_one: float32 [768], P('dp'), may hold values from -12.675879002262526 to 12.675879002262526
- mean_attend_weight: float32 [768, 2304], P('dp', 'tensor'), may hold values from -8.8731153 to 8.8731153
- mean_output_weight: float32 [768, 768], P('tensor', 'dp'), may hold values from -1.774623 to 1.774623
- mean_gain_two: float32 [768], P('dp'), may hold values from -5.0703516 to 5.0703516
- mean_up_weight: float32 [768, 3072], P('dp', 'tensor'), may hold values from -2.5351758 to 2.5351758
- mean_down_weight: float32 [3072, 768], P('tensor', 'dp'), may hold values from -5.0703516 to 5.0703516
- mean_patch_weight: float32 [768, 768], P('dp', 'tensor'), may hold values from -11.408291 to 11.408291
- mean_class_weight: float32 [768, 768], P('dp', 'tensor'), may hold values from -11.154774 to 11.154774
- mean_class_embed: float32 [150, 768], P(None, 'dp'), may hold values from -0.9126633 to 0.9126633
- square_gain_one: float32 [768], P('dp'), may hold values from 19.456 to 1950.72
- square_attend_weight: float32 [768, 2304], P('dp', 'tensor'), may hold values from 9.53344 to 955.8528
- square_output_weight: float32 [768, 768], P('tensor', 'dp'), may hold values from 0.3813376 to 38.23411
- square_gain_two: float32 [768], P('dp'), may hold values from 3.11296 to 312.1152
- square_up_weight: float32 [768, 3072], P('dp', 'tensor'), may hold values from 0.77824 to 78.0288
- square_down_weight: float32 [3072, 768], P('tensor', 'dp'), may hold values from 3.11296 to 312.1152
- square_patch_weight: float32 [768, 768], P('dp', 'tensor'), may hold values from 15.75936 to 1580.0832
- square_class_weight: float32 [768, 768], P('dp', 'tensor'), may hold values from 15.0667264 to 1510.6376
- square_class_embed: float32 [150, 768], P(None, 'dp'), may hold values from 0.1008599 to 10.1125325
Outputs:
- masks: float32 [8192, 150], P(('dp', 'tensor'))
- token_grad: float32 [8192, 768], P(('dp', 'tensor'))
- update_gain_one: float32 [768], P('dp')
- update_attend_weight: float32 [768, 2304], P('dp', 'tensor')
- update_output_weight: float32 [768, 768], P('tensor', 'dp')
- update_gain_two: float32 [768], P('dp')
- update_up_weight: float32 [768, 3072], P('dp', 'tensor')
- update_down_weight: float32 [3072, 768], P('tensor', 'dp')
- update_patch_weight: float32 [768, 768], P('dp', 'tensor')
- update_class_weight: float32 [768, 768], P('dp', 'tensor')
- update_class_embed: float32 [150, 768], P(None, 'dp')
- updated_mean_gain_one: float32 [768], P('dp')
- updated_mean_attend_weight: float32 [768, 2304], P('dp', 'tensor')
- updated_mean_output_weight: float32 [768, 768], P('tensor', 'dp')
- updated_mean_gain_two: float32 [768], P('dp')
- updated_mean_up_weight: float32 [768, 3072], P('dp', 'tensor')
- updated_mean_down_weight: float32 [3072, 768], P('tensor', 'dp')
- updated_mean_patch_weight: float32 [768, 768], P('dp', 'tensor')
- updated_mean_class_weight: float32 [768, 768], P('dp', 'tensor')
- updated_mean_class_embed: float32 [150, 768], P(None, 'dp')
The draws below stay inside these ranges and needn't reach their ends.
Inputs may be any that keep to these rules, and one draw needn't show every extreme that they name: `segments`: in each row the numbers never fall; each image holds 1 to 128 tokens and some image exactly 128.
All inputs are finite; a program needn't handle non-finite values.
Results may differ from the reference program's by a relative error of at most 0.018.
Values may be sent and summed in bfloat16 or wider, within the bound.
A program may use at most 128 MiB of HBM per device.

```python
import math
import jax
import jax.numpy as jnp
import numpy as np
from jax import lax

D = 768
HEADS = 12
HD = 64
FF = 3072
NCLS = 150
SEQ = 1024
PATCH = 128
NSEQ = 8
TOKENS = 8192


def first_moment(key, number, extent, factor):
    drawn_key = jax.random.fold_in(key, number)
    spread_scale = 0.07 * factor * math.sqrt(TOKENS)
    base = jnp.clip(jax.random.normal(drawn_key, extent, jnp.float32), -4.0, 4.0)
    return base * spread_scale


def second_moment(key, number, extent, factor):
    drawn_key = jax.random.fold_in(key, number)
    level = jax.random.uniform(drawn_key, extent, jnp.float32, 0.0, 1.0)
    ratio = jnp.clip(jnp.exp(math.log(0.1) + math.log(100.0) * level), 0.1, 10.0)
    return ratio * (0.0952 * factor * factor * TOKENS)


def draw_mean_gain_one(key, part):
    return first_moment(key, 101, (D,), 0.5)


def draw_mean_attend_weight(key, part):
    return first_moment(key, 102, (D, 3 * D), 0.35)


def draw_mean_output_weight(key, part):
    return first_moment(key, 103, (D, D), 0.07)


def draw_mean_gain_two(key, part):
    return first_moment(key, 104, (D,), 0.2)


def draw_mean_up_weight(key, part):
    return first_moment(key, 105, (D, FF), 0.1)


def draw_mean_down_weight(key, part):
    return first_moment(key, 106, (FF, D), 0.2)


def draw_mean_patch_weight(key, part):
    return first_moment(key, 107, (D, D), 0.45)


def draw_mean_class_weight(key, part):
    return first_moment(key, 108, (D, D), 0.44)


def draw_mean_class_embed(key, part):
    return first_moment(key, 109, (NCLS, D), 0.036)


def draw_square_gain_one(key, part):
    return second_moment(key, 201, (D,), 0.5)


def draw_square_attend_weight(key, part):
    return second_moment(key, 202, (D, 3 * D), 0.35)


def draw_square_output_weight(key, part):
    return second_moment(key, 203, (D, D), 0.07)


def draw_square_gain_two(key, part):
    return second_moment(key, 204, (D,), 0.2)


def draw_square_up_weight(key, part):
    return second_moment(key, 205, (D, FF), 0.1)


def draw_square_down_weight(key, part):
    return second_moment(key, 206, (FF, D), 0.2)


def draw_square_patch_weight(key, part):
    return second_moment(key, 207, (D, D), 0.45)


def draw_square_class_weight(key, part):
    return second_moment(key, 208, (D, D), 0.44)


def draw_square_class_embed(key, part):
    return second_moment(key, 209, (NCLS, D), 0.036)


def levels(rng, shape, shards, least, largest):
    level = 1.0
    for dim, parts in shards:
        heights = jax.random.uniform(jax.random.fold_in(jax.random.fold_in(rng, 6), dim), (parts,), jnp.float32, least / len(shards), largest / len(shards))
        level = level * jnp.repeat(jnp.exp(heights), shape[dim] // parts).reshape((-1,) + (1,) * (len(shape) - 1 - dim))
    return level


def profile(amount, total, reach, slope):
    weights = [(1 << 20) // math.isqrt(grade ** slope) + 1 for grade in range(2, amount + 1)]
    rest, counts = total - reach - (amount - 1), [1] * (amount - 1)
    while rest > 0:
        candidates = [i for i in range(amount - 1) if counts[i] < reach]
        mass, remaining = sum([weights[i] for i in candidates]), rest
        for i in candidates:
            more = min(reach - counts[i], max(1, remaining * weights[i] // mass), rest)
            counts[i] = counts[i] + more
            rest = rest - more
    return np.array([reach] + counts)


def uneven(key, count, total, most, slope):
    if count == 2:
        one = jax.random.randint(key, (), max(1, total - most), min(most, total - 1) + 1)
        return jnp.stack([one, total - one])
    lengths = jnp.asarray(profile(count, total, most, slope), jnp.int32)
    pairs = (count - 1) // 2
    giver, sink = lengths[1:1 + 2 * pairs:2], lengths[2:2 + 2 * pairs:2]
    margin = jnp.minimum(giver - 1, most - sink)
    shifted = jax.random.randint(jax.random.fold_in(key, 1), (pairs,), 0, 1 << 20) % (margin + 1)
    lengths = lengths.at[1:1 + 2 * pairs:2].set(giver - shifted).at[2:2 + 2 * pairs:2].set(sink + shifted)
    return lengths[jax.random.permutation(jax.random.fold_in(key, 2), count)]


def scatter_about(key, shape, scale, reach, cuts=(), dtype=jnp.bfloat16):
    result = scale * jax.random.normal(key, shape, jnp.float32)
    if cuts:
        result = result * levels(key, shape, cuts, -0.22, 0.18)
    return jnp.clip(result, -reach, reach).astype(dtype)


def setup_inputs(seed: int = 0) -> dict:
    key_of = jax.random.split(jax.random.key(seed), 31)
    return {
        "tokens": scatter_about(key_of[0], (TOKENS, D), 1.0, 6.0, ((0, 32),)),
        "segments": jax.vmap(lambda own: jnp.searchsorted(jnp.cumsum(uneven(own, 2 * SEQ // PATCH, SEQ, PATCH, 1)), jnp.arange(SEQ), side="right"))(jax.random.split(key_of[1], NSEQ)).reshape((NSEQ, SEQ)).astype(jnp.int32),
        "mask_grad": scatter_about(key_of[2], (TOKENS, NCLS), 1.0, 6.0, ((0, 32),), jnp.float32),
        "gain_one": jnp.clip(1.0 + 0.1 * jax.random.normal(key_of[3], (D,), jnp.float32), 0.5, 1.5),
        "attend_weight": scatter_about(key_of[4], (D, 3 * D), D ** -0.5, 0.21875, ((0, 8), (1, 4)), jnp.float32),
        "output_weight": scatter_about(key_of[5], (D, D), (D // 16) ** -0.5, 0.875, ((0, 4), (1, 8)), jnp.float32),
        "gain_two": jnp.clip(1.0 + 0.1 * jax.random.normal(key_of[6], (D,), jnp.float32), 0.5, 1.5),
        "up_weight": scatter_about(key_of[7], (D, FF), D ** -0.5, 0.21875, ((0, 8), (1, 4)), jnp.float32),
        "down_weight": scatter_about(key_of[8], (FF, D), FF ** -0.5, 0.109375, ((0, 4), (1, 8)), jnp.float32),
        "patch_weight": scatter_about(key_of[9], (D, D), D ** -0.5, 0.21875, ((0, 8), (1, 4)), jnp.float32),
        "class_weight": scatter_about(key_of[10], (D, D), D ** -0.5, 0.21875, ((0, 8), (1, 4)), jnp.float32),
        "class_embed": scatter_about(key_of[11], (NCLS, D), 1.0, 6.0, ((1, 8),), jnp.float32),
        "mean_gain_one": draw_mean_gain_one(jax.random.fold_in(key_of[30], 71), 0),
        "mean_attend_weight": draw_mean_attend_weight(jax.random.fold_in(key_of[30], 71), 0),
        "mean_output_weight": draw_mean_output_weight(jax.random.fold_in(key_of[30], 71), 0),
        "mean_gain_two": draw_mean_gain_two(jax.random.fold_in(key_of[30], 71), 0),
        "mean_up_weight": draw_mean_up_weight(jax.random.fold_in(key_of[30], 71), 0),
        "mean_down_weight": draw_mean_down_weight(jax.random.fold_in(key_of[30], 71), 0),
        "mean_patch_weight": draw_mean_patch_weight(jax.random.fold_in(key_of[30], 71), 0),
        "mean_class_weight": draw_mean_class_weight(jax.random.fold_in(key_of[30], 71), 0),
        "mean_class_embed": draw_mean_class_embed(jax.random.fold_in(key_of[30], 71), 0),
        "square_gain_one": draw_square_gain_one(jax.random.fold_in(key_of[30], 71), 0),
        "square_attend_weight": draw_square_attend_weight(jax.random.fold_in(key_of[30], 71), 0),
        "square_output_weight": draw_square_output_weight(jax.random.fold_in(key_of[30], 71), 0),
        "square_gain_two": draw_square_gain_two(jax.random.fold_in(key_of[30], 71), 0),
        "square_up_weight": draw_square_up_weight(jax.random.fold_in(key_of[30], 71), 0),
        "square_down_weight": draw_square_down_weight(jax.random.fold_in(key_of[30], 71), 0),
        "square_patch_weight": draw_square_patch_weight(jax.random.fold_in(key_of[30], 71), 0),
        "square_class_weight": draw_square_class_weight(jax.random.fold_in(key_of[30], 71), 0),
        "square_class_embed": draw_square_class_embed(jax.random.fold_in(key_of[30], 71), 0),
    }


@jax.custom_vjp
def low(v):
    return lax.optimization_barrier(v.astype(jnp.bfloat16)).astype(jnp.float32)

@jax.custom_vjp
def low_back(v):
    return v

def low_keep(v):
    return (low(v), None)

def low_pass(kept, grad):
    return (grad,)

def back_keep(v):
    return (v, None)

def back_low(kept, grad):
    return (low(grad),)
low.defvjp(low_keep, low_pass)
low_back.defvjp(back_keep, back_low)
epsilon_norm = 1e-05
epsilon_unit = 1e-06
masked_score = -1000000000.0
first_decay = 0.9
second_decay = 0.999
first_fix = 0.99997343860112
second_fix = 0.09520785288629
adam_epsilon = 1e-08
block_scale = 0.65
weight_decay = 0.05

def product(left, right):
    return jnp.dot(left, right, precision=lax.Precision.HIGHEST, preferred_element_type=jnp.float32)

def layer_norm(values, gain):
    center = values - lax.optimization_barrier(jnp.mean(values, axis=-1, keepdims=True))
    spread = lax.optimization_barrier(jnp.mean(center * center, axis=-1, keepdims=True))
    return center * lax.rsqrt(spread + epsilon_norm) * gain

def unit_rows(values):
    return values * lax.rsqrt(lax.optimization_barrier(jnp.sum(values * values, axis=-1, keepdims=True)) + epsilon_unit)

def gelu_exact(values):
    return jax.nn.gelu(values, approximate=False)

def adamw_update(current, gradient, mean_old, square_old, step_scale, decay_rate):
    mean_new = first_decay * mean_old + (1.0 - first_decay) * gradient
    square_new = second_decay * square_old + (1.0 - second_decay) * gradient * gradient
    moved = mean_new / first_fix / (jnp.sqrt(square_new / second_fix) + adam_epsilon)
    return (step_scale * (moved + decay_rate * current), mean_new)

def attend_one(query_rows, key_rows, value_rows, segment_row):
    scores = jnp.einsum('qhd,khd->hqk', query_rows, key_rows, precision=lax.Precision.HIGHEST) * HD ** (-0.5)
    scores = low_back(scores)
    matches = segment_row[:, None] == segment_row[None, :]
    scores = jnp.where(matches[None], scores, masked_score)
    maxima = lax.optimization_barrier(jnp.max(scores, axis=-1, keepdims=True))
    exponent = jnp.exp(scores - maxima)
    weights = exponent / lax.optimization_barrier(jnp.sum(exponent, axis=-1, keepdims=True))
    return jnp.einsum('hqk,khd->qhd', low(weights), value_rows, precision=lax.Precision.HIGHEST)

def group_rows(token_rows, segment_rows, gain_first, attend_low, output_low, gain_second, up_low, down_low, patch_low, class_unit):
    group_count = segment_rows.shape[0]
    length = segment_rows.shape[1]
    norm_one = low(layer_norm(token_rows, gain_first))
    joint = low(low_back(product(norm_one, attend_low)))
    joint = joint.reshape(group_count, length, HEADS, 3, HD)
    attended = jax.vmap(attend_one)(joint[:, :, :, 0], joint[:, :, :, 1], joint[:, :, :, 2], segment_rows)
    attended = low(low_back(attended.reshape(group_count * length, HEADS * HD)))
    resid_one = token_rows + low_back(product(attended, output_low))
    norm_two = low(layer_norm(resid_one, gain_second))
    hidden = low(gelu_exact(low_back(product(norm_two, up_low))))
    resid_two = resid_one + low_back(product(hidden, down_low))
    patch_feat = low_back(product(low(resid_two), patch_low))
    patch_unit = low(unit_rows(patch_feat))
    products = low_back(product(patch_unit, class_unit.T))
    return layer_norm(products, 1.0)

def reference(tokens, segments, mask_grad, gain_one, attend_weight, output_weight, gain_two, up_weight, down_weight, patch_weight, class_weight, class_embed, mean_gain_one, mean_attend_weight, mean_output_weight, mean_gain_two, mean_up_weight, mean_down_weight, mean_patch_weight, mean_class_weight, mean_class_embed, square_gain_one, square_attend_weight, square_output_weight, square_gain_two, square_up_weight, square_down_weight, square_patch_weight, square_class_weight, square_class_embed):
    group_seq = 4 if NSEQ % 4 == 0 else 2 if NSEQ % 2 == 0 else 1
    segment_groups = segments.reshape(NSEQ // group_seq, group_seq, SEQ)

    def forward(token_wide, params):
        gain_first, attend_full, output_full, gain_second, up_full, down_full, patch_full, class_full, embed_full = params
        class_feat = low_back(product(low(embed_full), low(class_full)))
        class_unit = low(unit_rows(class_feat))
        rounded = (low(gain_first), low(attend_full), low(output_full), low(gain_second), low(up_full), low(down_full), low(patch_full))
        token_groups = token_wide.reshape(NSEQ // group_seq, group_seq * SEQ, D)
        checked = jax.checkpoint(group_rows)

        def advance(carried, pieces):
            return (carried, checked(pieces[0], pieces[1], rounded[0], rounded[1], rounded[2], rounded[3], rounded[4], rounded[5], rounded[6], class_unit))
        carried, results = lax.scan(advance, jnp.zeros((), jnp.float32), (token_groups, segment_groups))
        return results.reshape(TOKENS, NCLS)
    params = (gain_one, attend_weight, output_weight, gain_two, up_weight, down_weight, patch_weight, class_weight, class_embed)
    means = (mean_gain_one, mean_attend_weight, mean_output_weight, mean_gain_two, mean_up_weight, mean_down_weight, mean_patch_weight, mean_class_weight, mean_class_embed)
    squares = (square_gain_one, square_attend_weight, square_output_weight, square_gain_two, square_up_weight, square_down_weight, square_patch_weight, square_class_weight, square_class_embed)
    masks, pull_back = jax.vjp(forward, tokens.astype(jnp.float32), params)
    token_grad, param_grads = pull_back(mask_grad)
    step_scales = (block_scale,) * 6 + (1.0,) * 3
    decay_rates = (0.0, weight_decay, weight_decay, 0.0, weight_decay, weight_decay, weight_decay, weight_decay, weight_decay)
    updated = [adamw_update(params[number], param_grads[number], means[number], squares[number], step_scales[number], decay_rates[number]) for number in range(9)]
    return (masks, token_grad, updated[0][0], updated[1][0], updated[2][0], updated[3][0], updated[4][0], updated[5][0], updated[6][0], updated[7][0], updated[8][0], updated[0][1], updated[1][1], updated[2][1], updated[3][1], updated[4][1], updated[5][1], updated[6][1], updated[7][1], updated[8][1])
```

```python
import functools

import jax
import jax.numpy as jnp
from jax import lax
from jax.experimental import pallas as pl
from jax.experimental.pallas import tpu as pltpu
from jax.sharding import PartitionSpec as P

HD = 64
HALO = 128
BF = jnp.bfloat16
F32 = jnp.float32
MESH = pl.DeviceIdType.MESH

epsilon_norm = 1e-05
epsilon_unit = 1e-06
masked_score = -1000000000.0
first_decay = 0.9
second_decay = 0.999
first_fix = 0.99997343860112
second_fix = 0.09520785288629
adam_epsilon = 1e-08
block_scale = 0.65
weight_decay = 0.05


def dot(left, right, dims=((1,), (0,))):
    return lax.dot_general(left, right, (dims, ((), ())), preferred_element_type=F32)


def layer_norm(values, gain):
    center = values - jnp.mean(values, axis=-1, keepdims=True)
    spread = jnp.mean(center * center, axis=-1, keepdims=True)
    return center * lax.rsqrt(spread + epsilon_norm) * gain


def norm_parts(values):
    center = values - jnp.mean(values, axis=-1, keepdims=True)
    spread = jnp.mean(center * center, axis=-1, keepdims=True)
    inverse = lax.rsqrt(spread + epsilon_norm)
    return center * inverse, inverse


def norm_back(gradient, xhat, inverse):
    return inverse * (
        gradient
        - jnp.mean(gradient, axis=-1, keepdims=True)
        - xhat * jnp.mean(gradient * xhat, axis=-1, keepdims=True)
    )


def unit_parts(values):
    inverse = lax.rsqrt(jnp.sum(values * values, axis=-1, keepdims=True) + epsilon_unit)
    return values * inverse, inverse


def unit_back(gradient, unit, inverse):
    return inverse * (gradient - unit * jnp.sum(unit * gradient, axis=-1, keepdims=True))


def adamw_update(current, gradient, mean_old, square_old, step_scale, decay_rate):
    mean_new = first_decay * mean_old + (1.0 - first_decay) * gradient
    square_new = second_decay * square_old + (1.0 - second_decay) * gradient * gradient
    moved = mean_new / first_fix / (jnp.sqrt(square_new / second_fix) + adam_epsilon)
    return (step_scale * (moved + decay_rate * current), mean_new)


def places():
    dp = lax.axis_index("dp")
    tensor = lax.axis_index("tensor")
    core = dp % 2
    col = (dp // 2) % 2
    row = dp // 4
    over_x = dp + 2 * (1 - 2 * col)
    over_y = dp + 4 * (1 - 2 * row)
    sibling = dp + 1 - 2 * core
    return dp, tensor, over_x, over_y, sibling


def greet():
    dp, tensor, over_x, over_y, sibling = places()
    barrier = pltpu.get_barrier_semaphore()
    targets = [(over_x, tensor), (over_y, tensor), (sibling, tensor)]
    targets += [(dp, (tensor + j) % 4) for j in (1, 2, 3)]
    for target in targets:
        pl.semaphore_signal(barrier, inc=1, device_id=target, device_id_type=MESH)
    pl.semaphore_wait(barrier, 6)


def remote(source, target_ref, sends, receives, device):
    return pltpu.make_async_remote_copy(
        src_ref=source,
        dst_ref=target_ref,
        send_sem=sends,
        recv_sem=receives,
        device_id=device,
        device_id_type=MESH,
    )


def gather_kernel(count, *refs):
    shards, fulls = refs[:count], refs[count : 2 * count]
    sends, receives = refs[2 * count :]
    dp, tensor, over_x, over_y, sibling = places()
    across = over_x + over_y - dp
    greet()

    def copy(w, k):
        full = fulls[w]
        if full.shape[0] == 8:
            half = full.shape[1] // 2
            own = full.at[dp]
            views = {3: own, 4: own, 5: own}
            views[6] = full.at[over_x, 0:half]
            views[7] = full.at[over_y, half : 2 * half]
            views[8], views[9], views[10] = (full.at[d] for d in (over_x, over_y, across))
        else:
            own = full.at[:, dp]
            views = {k: full.at[tensor, dp] for k in (0, 1, 2)}
            views.update({3: own, 4: own, 5: own})
            views[6] = full.at[0:2, over_x]
            views[7] = full.at[2:4, over_y]
            views[8], views[9], views[10] = (full.at[:, d] for d in (over_x, over_y, across))
        target = {
            0: (dp, (tensor + 1) % 4),
            1: (dp, (tensor + 2) % 4),
            2: (dp, (tensor + 3) % 4),
            3: (over_x, tensor),
            4: (over_y, tensor),
            5: (sibling, tensor),
            6: (over_y, tensor),
            7: (over_x, tensor),
            8: (sibling, tensor),
            9: (sibling, tensor),
            10: (sibling, tensor),
        }[k]
        return remote(views[k], views[k], sends.at[w, k], receives.at[w, k], target)

    for w in range(count):
        if fulls[w].shape[0] == 8:
            fulls[w][dp] = shards[w][...]
        else:
            fulls[w][tensor, dp] = shards[w][...]
            for k in (0, 1, 2):
                copy(w, k).start()
    for stage in range(count + 3):
        w = stage
        if w < count:
            if fulls[w].shape[0] != 8:
                for k in (0, 1, 2):
                    copy(w, k).wait_recv()
            for k in (3, 4, 5):
                copy(w, k).start()
        w = stage - 1
        if 0 <= w < count:
            copy(w, 3).wait_recv()
            copy(w, 6).start()
            copy(w, 8).start()
            copy(w, 4).wait_recv()
            copy(w, 7).start()
            copy(w, 9).start()
        w = stage - 2
        if 0 <= w < count:
            copy(w, 6).wait_recv()
            copy(w, 7).wait_recv()
            copy(w, 10).start()
        w = stage - 3
        if 0 <= w < count:
            for k in (5, 8, 9, 10):
                copy(w, k).wait_recv()
    for w in range(count):
        for k in range(3 if fulls[w].shape[0] == 8 else 0, 11):
            copy(w, k).wait_send()


def gather_call(shards, embed):
    operands = list(shards) + [embed]
    count = len(operands)
    outs = [jax.ShapeDtypeStruct((4, 8) + s.shape, BF) for s in shards]
    outs.append(jax.ShapeDtypeStruct((8,) + embed.shape, BF))
    return pl.pallas_call(
        functools.partial(gather_kernel, count),
        out_shape=outs,
        in_specs=[pl.BlockSpec(memory_space=pltpu.VMEM)] * count,
        out_specs=[pl.BlockSpec(memory_space=pltpu.VMEM)] * count,
        scratch_shapes=[pltpu.SemaphoreType.DMA((count, 11))] * 2,
        compiler_params=pltpu.CompilerParams(
            collective_id=0, has_side_effects=True, vmem_limit_bytes=60 << 20
        ),
    )(*operands)


def scatter_kernel(count, *refs):
    grads, outs = refs[:count], refs[count : 2 * count]
    scratch = refs[2 * count :]
    sends, receives = scratch[-2:]
    bufs = [scratch[6 * w : 6 * w + 6] for w in range(count)]
    dp, tensor, over_x, over_y, sibling = places()
    core, col, row = dp % 2, (dp // 2) % 2, dp // 4
    greet()

    def copy(w, k):
        g = grads[w]
        r1, r2a, r2b, r3a, r3b, r4 = bufs[w]
        if k == 0:
            pair = (g.at[:, :, :, 1 - core], r1, (sibling, tensor))
        elif k == 1:
            pair = (r1.at[0:2, :, 1 - col], r2a, (over_x, tensor))
        elif k == 2:
            pair = (r1.at[2:4, 1 - row], r2b, (over_y, tensor))
        elif k == 3:
            pair = (r1.at[0:2, 1 - row, col], r3a, (over_y, tensor))
        elif k == 4:
            pair = (r1.at[2:4, row, 1 - col], r3b, (over_x, tensor))
        else:
            j = k - 4
            peer = (tensor + j) % 4
            pair = (r1.at[peer, row, col], r4.at[j - 1], (dp, peer))
        return remote(pair[0], pair[1], sends.at[w, k], receives.at[w, k], pair[2])

    def add(ref, index, other):
        ref[index] = (ref[index].astype(F32) + other.astype(F32)).astype(BF)

    for w in range(count):
        copy(w, 0).start()
    for stage in range(count + 3):
        w = stage
        if w < count:
            copy(w, 0).wait_recv()
            r1 = bufs[w][0]
            for t in range(4):
                add(r1, t, grads[w][t, :, :, core])
            copy(w, 1).start()
            copy(w, 2).start()
        w = stage - 1
        if 0 <= w < count:
            r1, r2a, r2b, r3a, r3b, r4 = bufs[w]
            copy(w, 1).wait_recv()
            for t in range(2):
                for y in range(2):
                    add(r1, (t, y, col), r2a[t, y])
            copy(w, 3).start()
            copy(w, 2).wait_recv()
            for t in range(2):
                for x in range(2):
                    add(r1, (2 + t, row, x), r2b[t, x])
            copy(w, 4).start()
        w = stage - 2
        if 0 <= w < count:
            r1, r2a, r2b, r3a, r3b, r4 = bufs[w]
            copy(w, 3).wait_recv()
            for t in range(2):
                add(r1, (t, row, col), r3a[t])
            copy(w, 4).wait_recv()
            for t in range(2):
                add(r1, (2 + t, row, col), r3b[t])
            for j in (1, 2, 3):
                copy(w, 4 + j).start()
        w = stage - 3
        if 0 <= w < count:
            r1, r4 = bufs[w][0], bufs[w][5]
            for j in (1, 2, 3):
                copy(w, 4 + j).wait_recv()
            total = r1[tensor, row, col].astype(F32)
            for j in range(3):
                total = total + r4[j].astype(F32)
            outs[w][...] = total
    for w in range(count):
        for k in range(8):
            copy(w, k).wait_send()


def scatter_call(grads):
    count = len(grads)
    grads = [g.reshape(4, 2, 2, 2, 96, g.shape[-1]) for g in grads]
    scratch = []
    for g in grads:
        c = g.shape[-1]
        scratch += [
            pltpu.VMEM((4, 2, 2, 96, c), BF),
            pltpu.VMEM((2, 2, 96, c), BF),
            pltpu.VMEM((2, 2, 96, c), BF),
            pltpu.VMEM((2, 96, c), BF),
            pltpu.VMEM((2, 96, c), BF),
            pltpu.VMEM((3, 96, c), BF),
        ]
    return pl.pallas_call(
        functools.partial(scatter_kernel, count),
        out_shape=[jax.ShapeDtypeStruct((96, g.shape[-1]), F32) for g in grads],
        in_specs=[pl.BlockSpec(memory_space=pltpu.VMEM)] * count,
        out_specs=[pl.BlockSpec(memory_space=pltpu.VMEM)] * count,
        scratch_shapes=scratch + [pltpu.SemaphoreType.DMA((count, 8))] * 2,
        compiler_params=pltpu.CompilerParams(
            collective_id=1, has_side_effects=True, vmem_limit_bytes=60 << 20
        ),
    )(*grads)


def gather_plain(shards, embed):
    def full(s):
        return lax.all_gather(lax.all_gather(s, "dp", axis=0), "tensor", axis=0)

    return [full(s) for s in shards] + [lax.all_gather(embed, "dp", axis=0)]


def scatter_plain(grads):
    def share(g):
        part = lax.psum_scatter(g, "dp", scatter_dimension=1, tiled=True)
        return lax.psum_scatter(part, "tensor", scatter_dimension=0, tiled=True)[0]

    return [share(g).astype(F32) for g in grads]


def with_halo(rows, parts):
    forward = [(i, i + 1) for i in range(parts - 1)]
    backward = [(i + 1, i) for i in range(parts - 1)]
    before = lax.ppermute(rows[-HALO:], "tensor", forward)
    after = lax.ppermute(rows[:HALO], "tensor", backward)
    return jnp.concatenate((before, rows, after), axis=0)


def local(
    custom,
    parts,
    tokens,
    segments,
    mask_grad,
    gain_one,
    attend_weight,
    output_weight,
    gain_two,
    up_weight,
    down_weight,
    patch_weight,
    class_weight,
    class_embed,
    *moments,
):
    means, squares = moments[:9], moments[9:]
    own = tokens.shape[0]
    width = tokens.shape[1]
    classes = class_embed.shape[0]
    dp_index = lax.axis_index("dp")
    tensor_index = lax.axis_index("tensor")
    low = lambda v: v.astype(BF)

    shard_a = jnp.concatenate((low(attend_weight), low(output_weight).T), axis=1)
    shard_u = low(up_weight)
    shard_d = low(down_weight).T
    shard_p = jnp.concatenate((low(patch_weight), low(class_weight)), axis=1)
    rows_e = -(-(classes + 2) // 32) * 32
    shard_e = jnp.zeros((rows_e, class_embed.shape[1]), BF)
    shard_e = shard_e.at[:classes].set(low(class_embed))
    shard_e = shard_e.at[classes].set(low(gain_one)).at[classes + 1].set(low(gain_two))
    gather = gather_call if custom else gather_plain
    full_a, full_u, full_d, full_p, full_e = gather(
        (shard_a, shard_u, shard_d, shard_p), shard_e
    )
    full_a, full_u, full_d, full_p = (
        v.reshape(v.shape[0], width, v.shape[-1]) for v in (full_a, full_u, full_d, full_p)
    )
    embed_rows = full_e.transpose(1, 0, 2).reshape(rows_e, width)
    embed = embed_rows[:classes]
    gain_first = embed_rows[classes].astype(F32)[None]
    gain_second = embed_rows[classes + 1].astype(F32)[None]

    cut = attend_weight.shape[1]
    heads = cut // (3 * HD)
    w_attend, w_output = full_a[:, :, :cut], full_a[:, :, cut:]
    narrow = patch_weight.shape[1]
    w_patch, w_class = full_p[:, :, :narrow], full_p[:, :, narrow:]
    w_patch = w_patch.transpose(1, 0, 2).reshape(width, -1)
    w_class = w_class.transpose(1, 0, 2).reshape(width, -1)

    window = with_halo(tokens, parts)
    token_wide = window.astype(F32)
    xhat_one, inverse_one = norm_parts(token_wide)
    norm_one = low(xhat_one * gain_first)
    joint = jnp.einsum("sd,tdn->stn", norm_one, w_attend, preferred_element_type=F32)
    joint = low(joint).reshape(own + 2 * HALO, parts * heads, 3, HD)
    queries, keys, values = joint[:, :, 0], joint[:, :, 1], joint[:, :, 2]
    padded = jnp.pad(segments[0], HALO, constant_values=-1)
    seg = lax.dynamic_slice_in_dim(padded, tensor_index * own, own + 2 * HALO, 0)
    scores = jnp.einsum("qhd,khd->hqk", queries, keys, preferred_element_type=F32) * HD**-0.5
    scores = jnp.where(seg[None, :, None] == seg[None, None, :], scores, masked_score)
    exponent = jnp.exp(scores - jnp.max(scores, axis=-1, keepdims=True))
    prob = exponent / jnp.sum(exponent, axis=-1, keepdims=True)
    prob_low = low(prob)
    mine = slice(HALO, HALO + own)
    attended = jnp.einsum(
        "hqk,khd->qhd", prob_low[:, mine], values, preferred_element_type=F32
    )
    attended = low(attended).reshape(own, parts, heads * HD)
    resid_one = token_wide[mine] + jnp.einsum(
        "stn,tdn->sd", attended, w_output, preferred_element_type=F32
    )
    xhat_two, inverse_two = norm_parts(resid_one)
    norm_two = low(xhat_two * gain_second)
    hidden_pre = jnp.einsum("sd,tdn->stn", norm_two, full_u, preferred_element_type=F32)
    hidden, gelu_back = jax.vjp(lambda v: jax.nn.gelu(v, approximate=False), hidden_pre)
    hidden = low(hidden)
    resid_two = resid_one + jnp.einsum(
        "stn,tdn->sd", hidden, full_d, preferred_element_type=F32
    )
    resid_low = low(resid_two)
    patch_feat = dot(resid_low, w_patch)
    patch_wide, patch_inverse = unit_parts(patch_feat)
    patch_unit = low(patch_wide)
    class_feat = dot(embed, w_class)
    class_wide, class_inverse = unit_parts(class_feat)
    class_unit = low(class_wide)
    products = dot(patch_unit, class_unit, ((1,), (1,)))
    masks, mask_inverse = norm_parts(products)
    d_products = low(norm_back(mask_grad, masks, mask_inverse))
    d_class_unit = lax.psum(dot(d_products, patch_unit, ((0,), (0,))), ("dp", "tensor"))
    d_patch_unit = dot(d_products, class_unit)
    d_patch_feat = low(unit_back(d_patch_unit, patch_wide, patch_inverse))
    grad_patch = dot(resid_low, d_patch_feat, ((0,), (0,)))
    d_resid_two = dot(d_patch_feat, w_patch, ((1,), (1,)))
    d_branch_two = low(d_resid_two)
    d_hidden = jnp.einsum("sd,tdn->stn", d_branch_two, full_d, preferred_element_type=F32)
    grad_down = jnp.einsum("sd,stn->tdn", d_branch_two, hidden, preferred_element_type=F32)
    d_hidden_pre = low(gelu_back(d_hidden)[0])
    grad_up = jnp.einsum("sd,stn->tdn", norm_two, d_hidden_pre, preferred_element_type=F32)
    d_norm_two = jnp.einsum("stn,tdn->sd", d_hidden_pre, full_u, preferred_element_type=F32)
    d_resid_one = d_resid_two + norm_back(d_norm_two * gain_second, xhat_two, inverse_two)
    grad_gain_two = jnp.sum(d_norm_two * xhat_two, axis=0)
    d_branch_one = with_halo(low(d_resid_one), parts)
    d_attended = low(
        jnp.einsum("sd,tdn->stn", d_branch_one, w_output, preferred_element_type=F32)
    )
    grad_output = jnp.einsum(
        "sd,stn->tdn", d_branch_one[mine], attended, preferred_element_type=F32
    )
    d_attended = d_attended.reshape(own + 2 * HALO, parts * heads, HD)
    d_prob = jnp.einsum("qhd,khd->hqk", d_attended, values, preferred_element_type=F32)
    delta = jnp.sum(prob * d_prob, axis=-1, keepdims=True)
    d_scores = low(prob * (d_prob - delta))
    d_query = jnp.einsum(
        "hqk,khd->qhd", d_scores[:, mine], keys, preferred_element_type=F32
    )
    d_key = jnp.einsum(
        "hqk,qhd->khd", d_scores[:, :, mine], queries, preferred_element_type=F32
    )
    d_value = jnp.einsum(
        "hqk,qhd->khd", prob_low[:, :, mine], d_attended, preferred_element_type=F32
    )
    d_joint = low(
        jnp.stack((d_query * HD**-0.5, d_key * HD**-0.5, d_value), axis=2)
    ).reshape(own, parts, cut)
    grad_attend = jnp.einsum(
        "sd,stn->tdn", norm_one[mine], d_joint, preferred_element_type=F32
    )
    d_norm_one = jnp.einsum("stn,tdn->sd", d_joint, w_attend, preferred_element_type=F32)
    token_grad = d_resid_one + norm_back(
        d_norm_one * gain_first, xhat_one[mine], inverse_one[mine]
    )
    grad_gain_one = jnp.sum(d_norm_one * xhat_one[mine], axis=0)

    grad_patch = grad_patch.reshape(width, parts, narrow).transpose(1, 0, 2)
    scatter = scatter_call if custom else scatter_plain
    share_p, share_d, share_u, share_a = scatter(
        [
            low(grad_patch),
            low(grad_down),
            low(grad_up),
            low(jnp.concatenate((grad_attend, grad_output), axis=2)),
        ]
    )
    gains = lax.psum((grad_gain_one, grad_gain_two), ("dp", "tensor"))
    step = gain_one.shape[0]
    share_one, share_two = (lax.dynamic_slice_in_dim(g, dp_index * step, step, 0) for g in gains)
    d_class_feat = low(unit_back(d_class_unit, class_wide, class_inverse))
    d_class_own = lax.dynamic_slice_in_dim(d_class_feat, tensor_index * narrow, narrow, 1)
    share_class = dot(low(class_embed), d_class_own, ((0,), (0,)))
    class_rows = lax.dynamic_slice_in_dim(w_class, dp_index * step, step, 0)
    share_embed = dot(d_class_feat, class_rows, ((1,), (1,)))
    grads = (
        share_one,
        share_a[:, :cut],
        share_a[:, cut:].T,
        share_two,
        share_u,
        share_d.T,
        share_p,
        share_class,
        share_embed,
    )
    params = (
        gain_one,
        attend_weight,
        output_weight,
        gain_two,
        up_weight,
        down_weight,
        patch_weight,
        class_weight,
        class_embed,
    )
    scales = (block_scale,) * 6 + (1.0,) * 3
    decays = (0.0, weight_decay, weight_decay, 0.0) + (weight_decay,) * 5
    new = [adamw_update(*v) for v in zip(params, grads, means, squares, scales, decays)]
    return (masks, token_grad) + tuple(n[0] for n in new) + tuple(n[1] for n in new)


def solution(mesh):
    parts = mesh.shape["tensor"]
    custom = mesh.shape["dp"] == 8 and parts == 4
    params = (
        P("dp"),
        P("dp", "tensor"),
        P("tensor", "dp"),
        P("dp"),
        P("dp", "tensor"),
        P("tensor", "dp"),
        P("dp", "tensor"),
        P("dp", "tensor"),
        P(None, "dp"),
    )
    rows = P(("dp", "tensor"), None)
    return jax.shard_map(
        functools.partial(local, custom, parts),
        mesh=mesh,
        in_specs=(rows, P("dp", None), rows) + params * 3,
        out_specs=(rows, rows) + params * 2,
        check_vma=False,
    )
```

```python
import functools

import jax
import jax.numpy as jnp
from jax import lax
from jax.experimental import pallas as pl
from jax.experimental.pallas import tpu as pltpu
from jax.sharding import PartitionSpec as P

HD = 64
HALO = 128
BF = jnp.bfloat16
F32 = jnp.float32
MESH = pl.DeviceIdType.MESH
VMEM_LIMIT = 64 * 1024 * 1024 - 512 * 1024

epsilon_norm = 1e-05
epsilon_unit = 1e-06
masked_score = -1000000000.0
first_decay = 0.9
second_decay = 0.999
first_fix = 0.99997343860112
second_fix = 0.09520785288629
adam_epsilon = 1e-08
block_scale = 0.65
weight_decay = 0.05


def dot(left, right, dims=((1,), (0,))):
    return lax.dot_general(left, right, (dims, ((), ())), preferred_element_type=F32)


def layer_norm(values, gain):
    center = values - jnp.mean(values, axis=-1, keepdims=True)
    spread = jnp.mean(center * center, axis=-1, keepdims=True)
    return center * lax.rsqrt(spread + epsilon_norm) * gain


def norm_parts(values):
    center = values - jnp.mean(values, axis=-1, keepdims=True)
    spread = jnp.mean(center * center, axis=-1, keepdims=True)
    inverse = lax.rsqrt(spread + epsilon_norm)
    return center * inverse, inverse


def norm_back(gradient, xhat, inverse):
    return inverse * (
        gradient
        - jnp.mean(gradient, axis=-1, keepdims=True)
        - xhat * jnp.mean(gradient * xhat, axis=-1, keepdims=True)
    )


def unit_parts(values):
    inverse = lax.rsqrt(jnp.sum(values * values, axis=-1, keepdims=True) + epsilon_unit)
    return values * inverse, inverse


def unit_back(gradient, unit, inverse):
    return inverse * (gradient - unit * jnp.sum(unit * gradient, axis=-1, keepdims=True))


def adamw_update(current, gradient, mean_old, square_old, step_scale, decay_rate):
    mean_new = first_decay * mean_old + (1.0 - first_decay) * gradient
    square_new = second_decay * square_old + (1.0 - second_decay) * gradient * gradient
    moved = mean_new / first_fix / (jnp.sqrt(square_new / second_fix) + adam_epsilon)
    return (step_scale * (moved + decay_rate * current), mean_new)


def places():
    dp = lax.axis_index("dp")
    tensor = lax.axis_index("tensor")
    core = dp % 2
    col = (dp // 2) % 2
    row = dp // 4
    over_x = dp + 2 * (1 - 2 * col)
    over_y = dp + 4 * (1 - 2 * row)
    sibling = dp + 1 - 2 * core
    return dp, tensor, over_x, over_y, sibling


def greet():
    dp, tensor, over_x, over_y, sibling = places()
    barrier = pltpu.get_barrier_semaphore()
    targets = [(over_x, tensor), (over_y, tensor), (sibling, tensor)]
    targets += [(dp, (tensor + j) % 4) for j in (1, 2, 3)]
    for target in targets:
        pl.semaphore_signal(barrier, inc=1, device_id=target, device_id_type=MESH)
    pl.semaphore_wait(barrier, 6)


def remote(source, target_ref, sends, receives, device):
    return pltpu.make_async_remote_copy(
        src_ref=source,
        dst_ref=target_ref,
        send_sem=sends,
        recv_sem=receives,
        device_id=device,
        device_id_type=MESH,
    )


def plain_copy(source, target, semaphore):
    return pltpu.make_async_copy(source, target, semaphore)


class Gather:
    def __init__(self, full, sends, receives, w):
        self.full, self.sends, self.receives, self.w = full, sends, receives, w
        self.flat = full.shape[0] == 8

    def copy(self, k):
        dp, tensor, over_x, over_y, sibling = places()
        across = over_x + over_y - dp
        full = self.full
        if k < 3:
            view = full.at[tensor, dp]
            target = (dp, (tensor + 1 + k) % 4)
        elif k < 15:
            j = (k - 3) // 3
            view = full.at[dp] if self.flat else full.at[(tensor + j) % 4, dp]
            target = ((over_x, over_y, sibling)[(k - 3) % 3], tensor)
        elif k < 17:
            other = over_x if k == 15 else over_y
            if self.flat:
                half = full.shape[1] // 2
                view = full.at[other, pl.ds((k - 15) * half, half)]
            else:
                view = full.at[pl.ds((k - 15) * 2, 2), other]
            target = (over_y if k == 15 else over_x, tensor)
        else:
            other = (over_x, over_y, across)[k - 17]
            view = full.at[other] if self.flat else full.at[:, other]
            target = (sibling, tensor)
        return remote(view, view, self.sends.at[self.w, k], self.receives.at[self.w, k], target)

    def pieces(self):
        return range(1 if self.flat else 4)

    def first(self, shard):
        dp, tensor = places()[:2]
        if self.flat:
            self.full[dp] = shard[...]
        else:
            self.full[tensor, dp] = shard[...]
            for k in range(3):
                self.copy(k).start()
        for k in (3, 4, 5):
            self.copy(k).start()

    def spread(self):
        if not self.flat:
            for j in (3, 2, 1):
                self.copy(j - 1).wait_recv()
                for k in range(3):
                    self.copy(3 + 3 * (4 - j) + k).start()

    def forward(self):
        for j in self.pieces():
            self.copy(3 + 3 * j).wait_recv()
        self.copy(15).start()
        self.copy(17).start()
        for j in self.pieces():
            self.copy(4 + 3 * j).wait_recv()
        self.copy(16).start()
        self.copy(18).start()

    def across(self):
        self.copy(15).wait_recv()
        self.copy(16).wait_recv()
        self.copy(19).start()

    def last(self):
        for j in self.pieces():
            self.copy(5 + 3 * j).wait_recv()
        for k in (17, 18, 19):
            self.copy(k).wait_recv()

    def drain(self):
        if not self.flat:
            for k in range(3):
                self.copy(k).wait_send()
        for j in self.pieces():
            for k in range(3):
                self.copy(3 + 3 * j + k).wait_send()
        for k in range(15, 20):
            self.copy(k).wait_send()


def whole(value):
    return value.reshape(value.shape[0] * value.shape[1], value.shape[2])


def gelu_parts(values):
    cumulative = 0.5 * (1.0 + lax.erf(values * 0.7071067811865476))
    density = 0.3989422804014327 * jnp.exp(-0.5 * values * values)
    return values * cumulative, cumulative + values * density


HEAD_SET = 3
SPAN = 3 * HD


def forward_kernel(classes, *refs):
    (tokens, seg_col, seg_row, mask_grad, shard_e, shard_a, shard_u, shard_d, shard_p) = refs[:9]
    (masks_out, d_class_out, class_out, gains_out) = refs[9:13]
    saves_out = refs[13:25]
    scratch = refs[25:]
    (
        full_a,
        full_u,
        full_d,
        full_p,
        joint,
        attended,
        norm_two,
        hidden,
        slope,
        d_resid,
        grad_p,
        resid_one,
        full_e,
        window,
        norm_one,
        embed,
        feat,
        unit_low,
        class_low,
        resid_low,
        sends,
        receives,
        halo_sems,
        save_sems,
    ) = scratch
    kept = (
        full_a,
        full_u,
        full_d,
        full_p,
        joint,
        attended,
        norm_two,
        hidden,
        slope,
        resid_one,
        d_resid,
        grad_p,
    )

    def save(n):
        return plain_copy(kept[n], saves_out[n], save_sems.at[n])

    dp, tensor = places()[:2]
    own = tokens.shape[0]
    span = own + 2 * HALO
    greet()
    ge, ga, gu, gd, gp = (
        Gather(full, sends, receives, w)
        for w, full in enumerate((full_e, full_a, full_u, full_d, full_p))
    )
    ge.first(shard_e)
    window[HALO : HALO + own] = tokens[...]
    halo_before = remote(
        window.at[pl.ds(HALO, HALO)],
        window.at[pl.ds(HALO + own, HALO)],
        halo_sems.at[0],
        halo_sems.at[1],
        (dp, (tensor + 3) % 4),
    )
    halo_after = remote(
        window.at[pl.ds(own, HALO)],
        window.at[pl.ds(0, HALO)],
        halo_sems.at[2],
        halo_sems.at[3],
        (dp, (tensor + 1) % 4),
    )
    halo_before.start()
    halo_after.start()
    ga.first(shard_a)
    gu.first(shard_u)
    gd.first(shard_d)
    gp.first(shard_p)
    ge.forward()
    ge.across()
    ga.spread()
    ge.last()
    halo_before.wait_recv()
    halo_after.wait_recv()
    for d in range(8):
        embed[:, d * 96 : (d + 1) * 96] = full_e[d]
    gains = embed[classes : classes + 2, :].astype(F32)
    gains_out[...] = gains
    gain_first, gain_second = gains[0:1], gains[1:2]

    def first_norm(i, carry):
        rows = pl.ds(pl.multiple_of(i * 128, 128), 128)
        xhat, _ = norm_parts(window[rows].astype(F32))
        norm_one[rows] = (xhat * gain_first).astype(BF)
        return carry

    lax.fori_loop(0, span // 128, first_norm, 0)
    gu.spread()
    ga.forward()
    ga.across()
    gd.spread()
    ga.last()
    save(0).start()

    def project(t, carry):
        weight = whole(full_a[t])[:, : HEAD_SET * SPAN]
        joint[t] = dot(norm_one[...], weight).astype(BF)
        return carry

    lax.fori_loop(0, 4, project, 0)
    save(4).start()
    gu.forward()

    def attend(t, carry):
        for h in range(HEAD_SET):
            for b in range(own // 128):
                near = slice(b * 128, b * 128 + 384)
                query = joint[t, HALO + b * 128 : HALO + (b + 1) * 128, h * SPAN : h * SPAN + HD]
                key = joint[t, near, h * SPAN + HD : h * SPAN + 2 * HD]
                value = joint[t, near, h * SPAN + 2 * HD : h * SPAN + 3 * HD]
                scores = dot(query, key, ((1,), (1,))) * HD**-0.5
                match = seg_col[HALO + b * 128 : HALO + (b + 1) * 128] == seg_row[:, near]
                scores = jnp.where(match, scores, masked_score)
                exponent = jnp.exp(scores - jnp.max(scores, axis=-1, keepdims=True))
                total = jnp.sum(exponent, axis=-1, keepdims=True)
                prob = (exponent / total).astype(BF)
                attended[t, b * 128 : (b + 1) * 128, h * HD : (h + 1) * HD] = dot(
                    prob, value
                ).astype(BF)
        return carry

    lax.fori_loop(0, 2, attend, 0)
    gp.spread()
    gu.across()
    lax.fori_loop(2, 4, attend, 0)
    save(5).start()
    gd.forward()
    resid_one[...] = tokens[...].astype(F32)

    def output(t, carry):
        weight = whole(full_a[t])[:, HEAD_SET * SPAN :]
        resid_one[...] += dot(attended[t], weight, ((1,), (1,)))
        return carry

    lax.fori_loop(0, 4, output, 0)
    xhat, _ = norm_parts(resid_one[...])
    norm_two[...] = (xhat * gain_second).astype(BF)
    save(6).start()
    save(9).start()
    gu.last()
    save(1).start()
    gp.forward()

    def expand(t, carry):
        value, derivative = gelu_parts(dot(norm_two[...], whole(full_u[t])))
        hidden[t] = value.astype(BF)
        slope[t] = derivative.astype(BF)
        return carry

    lax.fori_loop(0, 4, expand, 0)
    save(7).start()
    save(8).start()
    gd.across()
    gp.across()
    gd.last()
    save(2).start()
    feat[...] = resid_one[...]

    def contract(t, carry):
        feat[...] += dot(hidden[t], whole(full_d[t]), ((1,), (1,)))
        return carry

    lax.fori_loop(0, 4, contract, 0)
    resid_low[...] = feat[...].astype(BF)
    gp.last()
    save(3).start()
    narrow = unit_low.shape[2]

    square = jnp.zeros((own, 1), F32)
    class_square = jnp.zeros((embed.shape[0], 1), F32)
    pieces, class_pieces = [], []
    for t in range(4):
        both = whole(full_p[t])
        piece = dot(resid_low[...], both[:, :narrow])
        square += jnp.sum(piece * piece, axis=-1, keepdims=True)
        pieces.append(piece)
        piece = dot(embed[...], both[:, narrow:])
        class_square += jnp.sum(piece * piece, axis=-1, keepdims=True)
        class_pieces.append(piece)
        class_out[t] = piece[:classes]
    inverse = lax.rsqrt(square + epsilon_unit)
    class_inverse = lax.rsqrt(class_square + epsilon_unit)
    products = jnp.zeros((own, embed.shape[0]), F32)
    for t in range(4):
        pieces[t] = pieces[t] * inverse
        unit_low[t] = pieces[t].astype(BF)
        class_low[t] = (class_pieces[t] * class_inverse).astype(BF)
        products += dot(unit_low[t], class_low[t], ((1,), (1,)))
    masks, mask_inverse = norm_parts(products[:, :classes])
    masks_out[...] = masks
    d_products = norm_back(mask_grad[...], masks, mask_inverse).astype(BF)
    along = jnp.zeros((own, 1), F32)
    d_pieces = []
    for t in range(4):
        d_class_out[t] = dot(d_products, unit_low[t], ((0,), (0,)))
        piece = dot(d_products, class_low[t, :classes])
        along += jnp.sum(piece * pieces[t], axis=-1, keepdims=True)
        d_pieces.append(piece)
    total = jnp.zeros(feat.shape, F32)
    flipped = resid_low[...].T
    for t in range(4):
        piece = (inverse * (d_pieces[t] - pieces[t] * along)).astype(BF)
        total += dot(piece, whole(full_p[t])[:, :narrow], ((1,), (1,)))
        block = dot(flipped, piece).astype(BF)
        grad_p[t] = block.reshape((2, 2, 2, block.shape[0] // 8, narrow))
    d_resid[...] = total
    save(10).start()
    save(11).start()
    for n in range(len(kept)):
        save(n).wait()
    halo_before.wait_send()
    halo_after.wait_send()
    for gather in (ge, ga, gu, gd, gp):
        gather.drain()


def any_specs(count):
    return [pl.BlockSpec(memory_space=pl.ANY)] * count


def vmem_specs(count):
    return [pl.BlockSpec(memory_space=pltpu.VMEM)] * count


def kept_shapes(own, width, cut, narrow, high):
    piece = width // 8
    span = own + 2 * HALO
    return [
        ((4, 8, piece, width), BF),
        ((4, 8, piece, high), BF),
        ((4, 8, piece, high), BF),
        ((4, 8, piece, 2 * narrow), BF),
        ((4, span, cut), BF),
        ((4, own, cut // 3), BF),
        ((own, width), BF),
        ((4, own, high), BF),
        ((4, own, high), BF),
        ((own, width), F32),
        ((own, width), F32),
        ((4, 2, 2, 2, piece, narrow), BF),
    ]


def forward_call(classes, kept, tokens, seg_col, seg_row, mask_grad, shard_e, shards):
    own, width = tokens.shape
    rows_e = shard_e.shape[0]
    narrow = shards[3].shape[1] // 2
    span = own + 2 * HALO
    count = len(shards) + 1
    scratch = [pltpu.VMEM(*k) for k in kept[:9]] + [
        pltpu.VMEM(*kept[10]),
        pltpu.VMEM(*kept[11]),
        pltpu.VMEM(*kept[9]),
        pltpu.VMEM((8,) + shard_e.shape, BF),
        pltpu.VMEM((span, width), BF),
        pltpu.VMEM((span, width), BF),
        pltpu.VMEM((rows_e, width), BF),
        pltpu.VMEM((own, width), F32),
        pltpu.VMEM((4, own, narrow), BF),
        pltpu.VMEM((4, rows_e, narrow), BF),
        pltpu.VMEM((own, width), BF),
        pltpu.SemaphoreType.DMA((count, 20)),
        pltpu.SemaphoreType.DMA((count, 20)),
        pltpu.SemaphoreType.DMA((4,)),
        pltpu.SemaphoreType.DMA((len(kept),)),
    ]
    outs = [
        jax.ShapeDtypeStruct((own, classes), F32),
        jax.ShapeDtypeStruct((4, classes, narrow), F32),
        jax.ShapeDtypeStruct((4, classes, narrow), F32),
        jax.ShapeDtypeStruct((2, width), F32),
    ]
    return pl.pallas_call(
        functools.partial(forward_kernel, classes),
        out_shape=outs + [jax.ShapeDtypeStruct(*k) for k in kept],
        in_specs=vmem_specs(9),
        out_specs=vmem_specs(4) + any_specs(len(kept)),
        scratch_shapes=scratch,
        compiler_params=pltpu.CompilerParams(
            collective_id=0, has_side_effects=True, vmem_limit_bytes=VMEM_LIMIT
        ),
    )(tokens, seg_col, seg_row, mask_grad, shard_e, *shards)


class Scatter:
    def __init__(self, grad, buffers, sends, receives, w):
        self.grad, self.sends, self.receives, self.w = grad, sends, receives, w
        self.r1, self.r2a, self.r2b, self.r3a, self.r3b, self.r4 = buffers

    def copy(self, k):
        dp, tensor, over_x, over_y, sibling = places()
        core, col, row = dp % 2, (dp // 2) % 2, dp // 4
        r1 = self.r1
        if k == 0:
            pair = (self.grad.at[:, :, :, 1 - core], r1, (sibling, tensor))
        elif k == 1:
            pair = (r1.at[0:2, :, 1 - col], self.r2a, (over_x, tensor))
        elif k == 2:
            pair = (r1.at[2:4, 1 - row], self.r2b, (over_y, tensor))
        elif k == 3:
            pair = (r1.at[0:2, 1 - row, col], self.r3a, (over_y, tensor))
        elif k == 4:
            pair = (r1.at[2:4, row, 1 - col], self.r3b, (over_x, tensor))
        else:
            j = k - 4
            peer = (tensor + j) % 4
            pair = (r1.at[peer, row, col], self.r4.at[j - 1], (dp, peer))
        return remote(
            pair[0], pair[1], self.sends.at[self.w, k], self.receives.at[self.w, k], pair[2]
        )

    def add(self, index, other):
        ref = self.r1
        ref[index] = (ref[index].astype(F32) + other.astype(F32)).astype(ref.dtype)

    def start(self):
        self.copy(0).start()

    def planes(self):
        dp = lax.axis_index("dp")
        core = dp % 2
        self.copy(0).wait_recv()

        def step(i, carry):
            t, y = i // 2, i % 2
            self.add((t, y), self.grad[t, y, :, core])
            return carry

        lax.fori_loop(0, 8, step, 0)
        self.copy(1).start()
        self.copy(2).start()

    def lines(self):
        dp = lax.axis_index("dp")
        col, row = (dp // 2) % 2, dp // 4
        self.copy(1).wait_recv()
        for t in range(2):
            for y in range(2):
                self.add((t, y, col), self.r2a[t, y])
        self.copy(3).start()
        self.copy(2).wait_recv()
        for t in range(2):
            for x in range(2):
                self.add((2 + t, row, x), self.r2b[t, x])
        self.copy(4).start()

    def points(self):
        dp = lax.axis_index("dp")
        col, row = (dp // 2) % 2, dp // 4
        self.copy(3).wait_recv()
        for t in range(2):
            self.add((t, row, col), self.r3a[t])
        self.copy(4).wait_recv()
        for t in range(2):
            self.add((2 + t, row, col), self.r3b[t])
        for j in (1, 2, 3):
            self.copy(4 + j).start()

    def result(self, out):
        dp, tensor = places()[:2]
        col, row = (dp // 2) % 2, dp // 4
        for j in (1, 2, 3):
            self.copy(4 + j).wait_recv()
        total = self.r1[tensor, row, col].astype(F32)
        for j in range(3):
            total = total + self.r4[j].astype(F32)
        out[...] = total

    def drain(self):
        for k in range(8):
            self.copy(k).wait_send()


def scatter_buffers(rows, cols, dtype):
    return [
        pltpu.VMEM((4, 2, 2, rows, cols), dtype),
        pltpu.VMEM((2, 2, rows, cols), dtype),
        pltpu.VMEM((2, 2, rows, cols), dtype),
        pltpu.VMEM((2, rows, cols), dtype),
        pltpu.VMEM((2, rows, cols), dtype),
        pltpu.VMEM((3, rows, cols), dtype),
    ]


def backward_kernel(*refs):
    (tokens, seg_col, seg_row, gains) = refs[:4]
    loads_in = refs[4:15]
    token_grad, share_p, share_d, share_u, share_a, share_n = refs[15:21]
    scratch = refs[21:]
    loaded = scratch[:11]
    (
        d_resid,
        grad_p,
        hidden,
        full_d,
        slope,
        norm_two,
        full_u,
        resid_one,
        attended,
        full_a,
        joint,
    ) = loaded
    (grad_d, grad_u, grad_a, grad_n, window, d_attended, norm_one, total, stack_p, stack_s) = scratch[
        11:21
    ]
    buffers = scratch[21:51]
    sends, receives, halo_sems, load_sems = scratch[51:]

    def load(n):
        return plain_copy(loads_in[n], loaded[n], load_sems.at[n])

    for n in range(11):
        load(n).start()
    dp, tensor = places()[:2]
    own, width = tokens.shape
    cut = joint.shape[2]
    piece = width // 8
    sp, sd, su, sa, sn = (
        Scatter(g, buffers[6 * w : 6 * w + 6], sends, receives, w)
        for w, g in enumerate((grad_p, grad_d, grad_u, grad_a, grad_n))
    )
    greet()
    load(1).wait()
    sp.start()
    load(0).wait()
    load(2).wait()
    branch = d_resid[...].astype(BF)
    flipped = branch.T

    def down(t, carry):
        grad_d[t] = dot(flipped, hidden[t]).astype(BF).reshape(grad_d.shape[1:])
        return carry

    lax.fori_loop(0, 4, down, 0)
    sd.start()
    load(3).wait()
    load(4).wait()
    load(5).wait()
    flipped = norm_two[...].T

    def up(t, carry):
        back = dot(branch, whole(full_d[t])) * slope[t].astype(F32)
        back = back.astype(BF)
        slope[t] = back
        grad_u[t] = dot(flipped, back).astype(BF).reshape(grad_u.shape[1:])
        return carry

    lax.fori_loop(0, 4, up, 0)
    su.start()
    sp.planes()
    sd.planes()
    load(6).wait()
    load(7).wait()
    total[...] = jnp.zeros_like(total)

    def narrow_back(t, carry):
        total[...] += dot(slope[t], whole(full_u[t]), ((1,), (1,)))
        return carry

    lax.fori_loop(0, 4, narrow_back, 0)
    gain_first, gain_second = gains[0:1], gains[1:2]
    xhat, inverse = norm_parts(resid_one[...])
    gain_two = jnp.sum(total[...] * xhat, axis=0, keepdims=True)
    d_resid[...] += norm_back(total[...] * gain_second, xhat, inverse)
    window[HALO : HALO + own] = d_resid[...].astype(BF)
    halo_before = remote(
        window.at[pl.ds(HALO, HALO)],
        window.at[pl.ds(HALO + own, HALO)],
        halo_sems.at[0],
        halo_sems.at[1],
        (dp, (tensor + 3) % 4),
    )
    halo_after = remote(
        window.at[pl.ds(own, HALO)],
        window.at[pl.ds(0, HALO)],
        halo_sems.at[2],
        halo_sems.at[3],
        (dp, (tensor + 1) % 4),
    )
    halo_before.start()
    halo_after.start()
    su.planes()
    sp.lines()
    load(8).wait()
    flipped = window[HALO : HALO + own].T

    def outer(t, carry):
        block = dot(flipped, attended[t]).astype(BF)
        grad_a[t, :, :, :, :, cut:] = block.reshape((2, 2, 2, piece, cut // 3))
        return carry

    lax.fori_loop(0, 4, outer, 0)
    xhat, inverse = norm_parts(tokens[...].astype(F32))
    norm_one[...] = (xhat * gain_first).astype(BF)
    load(9).wait()
    load(10).wait()
    halo_before.wait_recv()
    halo_after.wait_recv()

    def attended_back(t, carry):
        weight = whole(full_a[t])[:, cut:]
        d_attended[t] = dot(window[...], weight).astype(BF)
        return carry

    lax.fori_loop(0, 4, attended_back, 0)
    sd.lines()
    sp.points()
    mine = slice(HALO, HALO + own)
    stack_p[...] = jnp.zeros_like(stack_p)
    stack_s[...] = jnp.zeros_like(stack_s)

    def attend(t, carry):
        for h in range(HEAD_SET):
            q_cols = slice(h * SPAN, h * SPAN + HD)
            k_cols = slice(h * SPAN + HD, h * SPAN + 2 * HD)
            v_cols = slice(h * SPAN + 2 * HD, h * SPAN + 3 * HD)
            d_cols = slice(h * HD, (h + 1) * HD)
            for b in range(4):
                rows = slice(b * 128, (b + 1) * 128)
                low_key, high_key = max(b - 1, 0) * 128, min(b + 2, 4) * 128
                near = slice(low_key, high_key)
                key = joint[t, near, k_cols]
                scores = dot(joint[t, rows, q_cols], key, ((1,), (1,))) * HD**-0.5
                match = seg_col[rows] == seg_row[:, near]
                scores = jnp.where(match, scores, masked_score)
                exponent = jnp.exp(scores - jnp.max(scores, axis=-1, keepdims=True))
                prob = exponent / jnp.sum(exponent, axis=-1, keepdims=True)
                d_prob = dot(d_attended[t, rows, d_cols], joint[t, near, v_cols], ((1,), (1,)))
                delta = jnp.sum(prob * d_prob, axis=-1, keepdims=True)
                d_scores = (prob * (d_prob - delta)).astype(BF)
                prob = prob.astype(BF)
                first, last = max(low_key, HALO), min(high_key, HALO + own)
                stack_p[rows, first - HALO : last - HALO] = prob[:, first - low_key : last - low_key]
                stack_s[rows, first - HALO : last - HALO] = d_scores[
                    :, first - low_key : last - low_key
                ]
                if b in (1, 2):
                    hidden[t, (b - 1) * 128 : b * 128, q_cols] = (
                        dot(d_scores, key) * HD**-0.5
                    ).astype(BF)
            hidden[t, :, k_cols] = (
                dot(stack_s[...], joint[t, :, q_cols], ((0,), (0,))) * HD**-0.5
            ).astype(BF)
            hidden[t, :, v_cols] = dot(
                stack_p[...], d_attended[t, :, d_cols], ((0,), (0,))
            ).astype(BF)
        return carry

    lax.fori_loop(0, 2, attend, 0)
    su.lines()
    lax.fori_loop(2, 4, attend, 0)
    flipped = norm_one[...].T

    def attend_grad(t, carry):
        block = dot(flipped, hidden[t, :, :cut]).astype(BF)
        grad_a[t, :, :, :, :, :cut] = block.reshape((2, 2, 2, piece, cut))
        return carry

    lax.fori_loop(0, 4, attend_grad, 0)
    sa.start()
    sd.points()
    sa.planes()
    total[...] = jnp.zeros_like(total)

    def joint_back(t, carry):
        weight = whole(full_a[t])[:, :cut]
        total[...] += dot(hidden[t, :, :cut], weight, ((1,), (1,)))
        return carry

    lax.fori_loop(0, 4, joint_back, 0)
    su.points()
    xhat, inverse = norm_parts(tokens[...].astype(F32))
    gain_one = jnp.sum(total[...] * xhat, axis=0, keepdims=True)
    token_grad[...] = d_resid[...] + norm_back(total[...] * gain_first, xhat, inverse)
    grad_n[...] = jnp.zeros_like(grad_n)
    for d in range(8):
        cols = slice(d * piece, (d + 1) * piece)
        y, x, c = d // 4, (d // 2) % 2, d % 2
        for t in range(4):
            grad_n[t, y, x, c, 0:1, 0:piece] = gain_one[:, cols]
            grad_n[t, y, x, c, 1:2, 0:piece] = gain_two[:, cols]
    sn.start()
    sn.planes()
    sp.result(share_p)
    sa.lines()
    sn.lines()
    sd.result(share_d)
    sa.points()
    sn.points()
    su.result(share_u)
    sa.result(share_a)
    sn.result(share_n)
    halo_before.wait_send()
    halo_after.wait_send()
    for scatter in (sp, sd, su, sa, sn):
        scatter.drain()


LOADED = (10, 11, 7, 2, 8, 6, 1, 9, 5, 0, 4)


def backward_call(kept, tokens, seg_col, seg_row, gains, saved):
    own, width = tokens.shape
    cut, narrow, high = kept[4][0][2], kept[11][0][5], kept[7][0][2]
    piece = width // 8
    span = own + 2 * HALO
    scratch = [pltpu.VMEM(*kept[n]) for n in LOADED] + [
        pltpu.VMEM((4, 2, 2, 2, piece, high), BF),
        pltpu.VMEM((4, 2, 2, 2, piece, high), BF),
        pltpu.VMEM((4, 2, 2, 2, piece, width), BF),
        pltpu.VMEM((4, 2, 2, 2, 8, 128), F32),
        pltpu.VMEM((span, width), BF),
        pltpu.VMEM((4, span, cut // 3), BF),
        pltpu.VMEM((own, width), BF),
        pltpu.VMEM((own, width), F32),
        pltpu.VMEM((span, own), BF),
        pltpu.VMEM((span, own), BF),
    ]
    for cols in (narrow, high, high, width):
        scratch += scatter_buffers(piece, cols, BF)
    scratch += scatter_buffers(8, 128, F32)
    scratch += [
        pltpu.SemaphoreType.DMA((5, 8)),
        pltpu.SemaphoreType.DMA((5, 8)),
        pltpu.SemaphoreType.DMA((4,)),
        pltpu.SemaphoreType.DMA((len(LOADED),)),
    ]
    return pl.pallas_call(
        backward_kernel,
        out_shape=[
            jax.ShapeDtypeStruct((own, width), F32),
            jax.ShapeDtypeStruct((piece, narrow), F32),
            jax.ShapeDtypeStruct((piece, high), F32),
            jax.ShapeDtypeStruct((piece, high), F32),
            jax.ShapeDtypeStruct((piece, width), F32),
            jax.ShapeDtypeStruct((8, 128), F32),
        ],
        in_specs=vmem_specs(4) + any_specs(len(LOADED)),
        out_specs=vmem_specs(6),
        scratch_shapes=scratch,
        compiler_params=pltpu.CompilerParams(
            collective_id=1, has_side_effects=True, vmem_limit_bytes=VMEM_LIMIT
        ),
    )(tokens, seg_col, seg_row, gains, *(saved[n] for n in LOADED))


def finish(masks, token_grad, grads, params, means, squares):
    scales = (block_scale,) * 6 + (1.0,) * 3
    decays = (0.0, weight_decay, weight_decay, 0.0) + (weight_decay,) * 5
    new = [adamw_update(*v) for v in zip(params, grads, means, squares, scales, decays)]
    return (masks, token_grad) + tuple(n[0] for n in new) + tuple(n[1] for n in new)


def gather_plain(shards, embed):
    def full(s):
        return lax.all_gather(lax.all_gather(s, "dp", axis=0), "tensor", axis=0)

    return [full(s) for s in shards] + [lax.all_gather(embed, "dp", axis=0)]


def scatter_plain(grads):
    def share(g):
        part = lax.psum_scatter(g, "dp", scatter_dimension=1, tiled=True)
        return lax.psum_scatter(part, "tensor", scatter_dimension=0, tiled=True)[0]

    return [share(g).astype(F32) for g in grads]


def with_halo(rows, parts):
    forward = [(i, i + 1) for i in range(parts - 1)]
    backward = [(i + 1, i) for i in range(parts - 1)]
    before = lax.ppermute(rows[-HALO:], "tensor", forward)
    after = lax.ppermute(rows[:HALO], "tensor", backward)
    return jnp.concatenate((before, rows, after), axis=0)


def local_plain(
    parts,
    tokens,
    segments,
    mask_grad,
    gain_one,
    attend_weight,
    output_weight,
    gain_two,
    up_weight,
    down_weight,
    patch_weight,
    class_weight,
    class_embed,
    *moments,
):
    means, squares = moments[:9], moments[9:]
    own = tokens.shape[0]
    width = tokens.shape[1]
    classes = class_embed.shape[0]
    dp_index = lax.axis_index("dp")
    tensor_index = lax.axis_index("tensor")
    low = lambda v: v.astype(BF)

    shard_a = jnp.concatenate((low(attend_weight), low(output_weight).T), axis=1)
    shard_u = low(up_weight)
    shard_d = low(down_weight).T
    shard_p = jnp.concatenate((low(patch_weight), low(class_weight)), axis=1)
    rows_e = -(-(classes + 2) // 32) * 32
    shard_e = jnp.zeros((rows_e, class_embed.shape[1]), BF)
    shard_e = shard_e.at[:classes].set(low(class_embed))
    shard_e = shard_e.at[classes].set(low(gain_one)).at[classes + 1].set(low(gain_two))
    full_a, full_u, full_d, full_p, full_e = gather_plain(
        (shard_a, shard_u, shard_d, shard_p), shard_e
    )
    full_a, full_u, full_d, full_p = (
        v.reshape(v.shape[0], width, v.shape[-1]) for v in (full_a, full_u, full_d, full_p)
    )
    embed_rows = full_e.transpose(1, 0, 2).reshape(rows_e, width)
    embed = embed_rows[:classes]
    gain_first = embed_rows[classes].astype(F32)[None]
    gain_second = embed_rows[classes + 1].astype(F32)[None]

    cut = attend_weight.shape[1]
    heads = cut // (3 * HD)
    w_attend, w_output = full_a[:, :, :cut], full_a[:, :, cut:]
    narrow = patch_weight.shape[1]
    w_patch, w_class = full_p[:, :, :narrow], full_p[:, :, narrow:]
    w_patch = w_patch.transpose(1, 0, 2).reshape(width, -1)
    w_class = w_class.transpose(1, 0, 2).reshape(width, -1)

    window = with_halo(tokens, parts)
    token_wide = window.astype(F32)
    xhat_one, inverse_one = norm_parts(token_wide)
    norm_one = low(xhat_one * gain_first)
    joint = jnp.einsum("sd,tdn->stn", norm_one, w_attend, preferred_element_type=F32)
    joint = low(joint).reshape(own + 2 * HALO, parts * heads, 3, HD)
    queries, keys, values = joint[:, :, 0], joint[:, :, 1], joint[:, :, 2]
    padded = jnp.pad(segments[0], HALO, constant_values=-1)
    seg = lax.dynamic_slice_in_dim(padded, tensor_index * own, own + 2 * HALO, 0)
    scores = jnp.einsum("qhd,khd->hqk", queries, keys, preferred_element_type=F32) * HD**-0.5
    scores = jnp.where(seg[None, :, None] == seg[None, None, :], scores, masked_score)
    exponent = jnp.exp(scores - jnp.max(scores, axis=-1, keepdims=True))
    prob = exponent / jnp.sum(exponent, axis=-1, keepdims=True)
    prob_low = low(prob)
    mine = slice(HALO, HALO + own)
    attended = jnp.einsum(
        "hqk,khd->qhd", prob_low[:, mine], values, preferred_element_type=F32
    )
    attended = low(attended).reshape(own, parts, heads * HD)
    resid_one = token_wide[mine] + jnp.einsum(
        "stn,tdn->sd", attended, w_output, preferred_element_type=F32
    )
    xhat_two, inverse_two = norm_parts(resid_one)
    norm_two = low(xhat_two * gain_second)
    hidden_pre = jnp.einsum("sd,tdn->stn", norm_two, full_u, preferred_element_type=F32)
    hidden, gelu_back = jax.vjp(lambda v: jax.nn.gelu(v, approximate=False), hidden_pre)
    hidden = low(hidden)
    resid_two = resid_one + jnp.einsum(
        "stn,tdn->sd", hidden, full_d, preferred_element_type=F32
    )
    resid_low = low(resid_two)
    patch_feat = dot(resid_low, w_patch)
    patch_wide, patch_inverse = unit_parts(patch_feat)
    patch_unit = low(patch_wide)
    class_feat = dot(embed, w_class)
    class_wide, class_inverse = unit_parts(class_feat)
    class_unit = low(class_wide)
    products = dot(patch_unit, class_unit, ((1,), (1,)))
    masks, mask_inverse = norm_parts(products)
    d_products = low(norm_back(mask_grad, masks, mask_inverse))
    d_class_unit = lax.psum(dot(d_products, patch_unit, ((0,), (0,))), ("dp", "tensor"))
    d_patch_unit = dot(d_products, class_unit)
    d_patch_feat = low(unit_back(d_patch_unit, patch_wide, patch_inverse))
    grad_patch = dot(resid_low, d_patch_feat, ((0,), (0,)))
    d_resid_two = dot(d_patch_feat, w_patch, ((1,), (1,)))
    d_branch_two = low(d_resid_two)
    d_hidden = jnp.einsum("sd,tdn->stn", d_branch_two, full_d, preferred_element_type=F32)
    grad_down = jnp.einsum("sd,stn->tdn", d_branch_two, hidden, preferred_element_type=F32)
    d_hidden_pre = low(gelu_back(d_hidden)[0])
    grad_up = jnp.einsum("sd,stn->tdn", norm_two, d_hidden_pre, preferred_element_type=F32)
    d_norm_two = jnp.einsum("stn,tdn->sd", d_hidden_pre, full_u, preferred_element_type=F32)
    d_resid_one = d_resid_two + norm_back(d_norm_two * gain_second, xhat_two, inverse_two)
    grad_gain_two = jnp.sum(d_norm_two * xhat_two, axis=0)
    d_branch_one = with_halo(low(d_resid_one), parts)
    d_attended = low(
        jnp.einsum("sd,tdn->stn", d_branch_one, w_output, preferred_element_type=F32)
    )
    grad_output = jnp.einsum(
        "sd,stn->tdn", d_branch_one[mine], attended, preferred_element_type=F32
    )
    d_attended = d_attended.reshape(own + 2 * HALO, parts * heads, HD)
    d_prob = jnp.einsum("qhd,khd->hqk", d_attended, values, preferred_element_type=F32)
    delta = jnp.sum(prob * d_prob, axis=-1, keepdims=True)
    d_scores = low(prob * (d_prob - delta))
    d_query = jnp.einsum(
        "hqk,khd->qhd", d_scores[:, mine], keys, preferred_element_type=F32
    )
    d_key = jnp.einsum(
        "hqk,qhd->khd", d_scores[:, :, mine], queries, preferred_element_type=F32
    )
    d_value = jnp.einsum(
        "hqk,qhd->khd", prob_low[:, :, mine], d_attended, preferred_element_type=F32
    )
    d_joint = low(
        jnp.stack((d_query * HD**-0.5, d_key * HD**-0.5, d_value), axis=2)
    ).reshape(own, parts, cut)
    grad_attend = jnp.einsum(
        "sd,stn->tdn", norm_one[mine], d_joint, preferred_element_type=F32
    )
    d_norm_one = jnp.einsum("stn,tdn->sd", d_joint, w_attend, preferred_element_type=F32)
    token_grad = d_resid_one + norm_back(
        d_norm_one * gain_first, xhat_one[mine], inverse_one[mine]
    )
    grad_gain_one = jnp.sum(d_norm_one * xhat_one[mine], axis=0)

    grad_patch = grad_patch.reshape(width, parts, narrow).transpose(1, 0, 2)
    share_p, share_d, share_u, share_a = scatter_plain(
        [
            grad_patch,
            grad_down,
            grad_up,
            jnp.concatenate((grad_attend, grad_output), axis=2),
        ]
    )
    gains = lax.psum((grad_gain_one, grad_gain_two), ("dp", "tensor"))
    step = gain_one.shape[0]
    share_one, share_two = (lax.dynamic_slice_in_dim(g, dp_index * step, step, 0) for g in gains)
    d_class_feat = low(unit_back(d_class_unit, class_wide, class_inverse))
    d_class_own = lax.dynamic_slice_in_dim(d_class_feat, tensor_index * narrow, narrow, 1)
    share_class = dot(low(class_embed), d_class_own, ((0,), (0,)))
    class_rows = lax.dynamic_slice_in_dim(w_class, dp_index * step, step, 0)
    share_embed = dot(d_class_feat, class_rows, ((1,), (1,)))
    return finish(
        masks,
        token_grad,
        (
            share_one,
            share_a[:, :cut],
            share_a[:, cut:].T,
            share_two,
            share_u,
            share_d.T,
            share_p,
            share_class,
            share_embed,
        ),
        (
            gain_one,
            attend_weight,
            output_weight,
            gain_two,
            up_weight,
            down_weight,
            patch_weight,
            class_weight,
            class_embed,
        ),
        means,
        squares,
    )


def local_kernels(
    tokens,
    segments,
    mask_grad,
    gain_one,
    attend_weight,
    output_weight,
    gain_two,
    up_weight,
    down_weight,
    patch_weight,
    class_weight,
    class_embed,
    *moments,
):
    means, squares = moments[:9], moments[9:]
    own, width = tokens.shape
    classes = class_embed.shape[0]
    dp_index = lax.axis_index("dp")
    tensor_index = lax.axis_index("tensor")
    low = lambda v: v.astype(BF)

    shard_a = jnp.concatenate((low(attend_weight), low(output_weight).T), axis=1)
    shard_u = low(up_weight)
    shard_d = low(down_weight).T
    shard_p = jnp.concatenate((low(patch_weight), low(class_weight)), axis=1)
    rows_e = -(-(classes + 2) // 32) * 32
    shard_e = jnp.concatenate(
        (
            low(class_embed),
            low(gain_one)[None],
            low(gain_two)[None],
            jnp.zeros((rows_e - classes - 2, class_embed.shape[1]), BF),
        )
    )
    padded = jnp.pad(segments[0], HALO, constant_values=-1)
    seg = lax.dynamic_slice_in_dim(padded, tensor_index * own, own + 2 * HALO, 0)
    seg_col, seg_row = seg[:, None], seg[None, :]
    cut, narrow = attend_weight.shape[1], patch_weight.shape[1]
    kept = kept_shapes(own, width, cut, narrow, up_weight.shape[1])
    masks, d_class_part, class_feat, gains, *saved = forward_call(
        classes,
        kept,
        tokens,
        seg_col,
        seg_row,
        mask_grad,
        shard_e,
        (shard_a, shard_u, shard_d, shard_p),
    )
    d_class_unit = lax.psum(d_class_part, ("dp", "tensor"))
    token_grad, share_p, share_d, share_u, share_a, share_n = backward_call(
        kept, tokens, seg_col, seg_row, gains, saved
    )
    inverse = lax.rsqrt(jnp.sum(class_feat * class_feat, axis=(0, 2), keepdims=True) + epsilon_unit)
    class_wide = class_feat * inverse
    along = jnp.sum(class_wide * d_class_unit, axis=(0, 2), keepdims=True)
    d_class_feat = low(inverse * (d_class_unit - class_wide * along))
    d_class_own = lax.dynamic_index_in_dim(d_class_feat, tensor_index, 0, False)
    share_class = dot(low(class_embed), d_class_own, ((0,), (0,)))
    class_rows = lax.dynamic_index_in_dim(saved[3], dp_index, 1, False)[:, :, narrow:]
    share_embed = jnp.einsum(
        "tcn,trn->cr", d_class_feat, class_rows, preferred_element_type=F32
    )
    step = gain_one.shape[0]
    return finish(
        masks,
        token_grad,
        (
            share_n[0, :step],
            share_a[:, :cut],
            share_a[:, cut:].T,
            share_n[1, :step],
            share_u,
            share_d.T,
            share_p,
            share_class,
            share_embed,
        ),
        (
            gain_one,
            attend_weight,
            output_weight,
            gain_two,
            up_weight,
            down_weight,
            patch_weight,
            class_weight,
            class_embed,
        ),
        means,
        squares,
    )


def solution(mesh):
    parts = mesh.shape["tensor"]
    custom = mesh.shape["dp"] == 8 and parts == 4
    params = (
        P("dp"),
        P("dp", "tensor"),
        P("tensor", "dp"),
        P("dp"),
        P("dp", "tensor"),
        P("tensor", "dp"),
        P("dp", "tensor"),
        P("dp", "tensor"),
        P(None, "dp"),
    )
    rows = P(("dp", "tensor"), None)
    return jax.shard_map(
        local_kernels if custom else functools.partial(local_plain, parts),
        mesh=mesh,
        in_specs=(rows, P("dp", None), rows) + params * 3,
        out_specs=(rows, rows) + params * 2,
        check_vma=False,
    )
```

```python
import functools

import jax
import jax.numpy as jnp
from jax import lax
from jax.experimental import pallas as pl
from jax.experimental.pallas import tpu as pltpu
from jax.sharding import PartitionSpec as P

HD = 64
HALO = 128
BF = jnp.bfloat16
F32 = jnp.float32
MESH = pl.DeviceIdType.MESH
VMEM_LIMIT = 64 * 1024 * 1024 - 512 * 1024

epsilon_norm = 1e-05
epsilon_unit = 1e-06
masked_score = -1000000000.0
first_decay = 0.9
second_decay = 0.999
first_fix = 0.99997343860112
second_fix = 0.09520785288629
adam_epsilon = 1e-08
block_scale = 0.65
weight_decay = 0.05


def dot(left, right, dims=((1,), (0,))):
    return lax.dot_general(left, right, (dims, ((), ())), preferred_element_type=F32)


def layer_norm(values, gain):
    center = values - jnp.mean(values, axis=-1, keepdims=True)
    spread = jnp.mean(center * center, axis=-1, keepdims=True)
    return center * lax.rsqrt(spread + epsilon_norm) * gain


def norm_parts(values):
    center = values - jnp.mean(values, axis=-1, keepdims=True)
    spread = jnp.mean(center * center, axis=-1, keepdims=True)
    inverse = lax.rsqrt(spread + epsilon_norm)
    return center * inverse, inverse


def norm_back(gradient, xhat, inverse):
    return inverse * (
        gradient
        - jnp.mean(gradient, axis=-1, keepdims=True)
        - xhat * jnp.mean(gradient * xhat, axis=-1, keepdims=True)
    )


def unit_parts(values):
    inverse = lax.rsqrt(jnp.sum(values * values, axis=-1, keepdims=True) + epsilon_unit)
    return values * inverse, inverse


def unit_back(gradient, unit, inverse):
    return inverse * (gradient - unit * jnp.sum(unit * gradient, axis=-1, keepdims=True))


def adamw_update(current, gradient, mean_old, square_old, step_scale, decay_rate):
    mean_new = first_decay * mean_old + (1.0 - first_decay) * gradient
    square_new = second_decay * square_old + (1.0 - second_decay) * gradient * gradient
    moved = mean_new / first_fix / (jnp.sqrt(square_new / second_fix) + adam_epsilon)
    return (step_scale * (moved + decay_rate * current), mean_new)


class Place:
    def __init__(self):
        dp, z = lax.axis_index("dp"), lax.axis_index("tensor")
        self.dp, self.z = dp, z
        self.core, self.col, self.row = dp % 2, (dp // 2) % 2, dp // 4
        self.x = (dp + 2 * (1 - 2 * self.col), z)
        self.y = (dp + 4 * (1 - 2 * self.row), z)
        self.sibling = (dp + 1 - 2 * self.core, z)

    def along(self, j):
        return (self.dp, (self.z + j) % 4)


def greet(place):
    barrier = pltpu.get_barrier_semaphore()
    targets = [place.x, place.y, place.sibling] + [place.along(j) for j in (1, 2, 3)]
    for target in targets:
        pl.semaphore_signal(barrier, inc=1, device_id=target, device_id_type=MESH)
    pl.semaphore_wait(barrier, 6)


def remote(source, target_ref, sends, receives, device):
    return pltpu.make_async_remote_copy(
        src_ref=source,
        dst_ref=target_ref,
        send_sem=sends,
        recv_sem=receives,
        device_id=device,
        device_id_type=MESH,
    )


class Line:
    def __init__(self, place, full, sends, receives):
        self.copies = [
            remote(
                full.at[place.z], full.at[place.z], sends.at[k], receives.at[k], place.along(k + 1)
            )
            for k in range(3)
        ]

    def start(self):
        for copy in self.copies:
            copy.start()

    def wait(self):
        for copy in self.copies:
            copy.wait_recv()

    def drain(self):
        for copy in self.copies:
            copy.wait_send()


class Gather:
    def __init__(self, place, full, sends, receives, w):
        self.place, self.full, self.w = place, full, w
        self.sends, self.receives = sends, receives
        self.flat = len(full.shape) == 5

    def copy(self, k):
        place, full = self.place, self.full
        row, col, core, z = place.row, place.col, place.core, place.z
        if k < 3:
            view, target = full.at[z, row, col, core], place.along(k + 1)
        elif k < 15:
            j = (k - 3) // 3
            if self.flat:
                view = full.at[row, col, core]
            else:
                view = full.at[(z + j) % 4, row, col, core]
            target = (place.x, place.y, place.sibling)[(k - 3) % 3]
        elif k < 17:
            spot = (row, 1 - col, core) if k == 15 else (1 - row, col, core)
            if self.flat:
                half = full.shape[3] // 2
                view = full.at[spot + (pl.ds((k - 15) * half, half),)]
            else:
                view = full.at[(pl.ds((k - 15) * 2, 2),) + spot]
            target = place.y if k == 15 else place.x
        else:
            spot = ((row, 1 - col, core), (1 - row, col, core), (1 - row, 1 - col, core))[k - 17]
            view = full.at[spot] if self.flat else full.at[(slice(None),) + spot]
            target = place.sibling
        return remote(view, view, self.sends.at[self.w, k], self.receives.at[self.w, k], target)

    def pieces(self):
        return range(1 if self.flat else 4)

    def start(self):
        if not self.flat:
            for k in range(3):
                self.copy(k).start()
        for k in (3, 4, 5):
            self.copy(k).start()

    def spread(self):
        if not self.flat:
            for j in (1, 2, 3):
                self.copy(j - 1).wait_recv()
                for k in range(3):
                    self.copy(3 + 3 * (4 - j) + k).start()

    def forward(self):
        for j in self.pieces():
            self.copy(3 + 3 * j).wait_recv()
        self.copy(15).start()
        self.copy(17).start()
        for j in self.pieces():
            self.copy(4 + 3 * j).wait_recv()
        self.copy(16).start()
        self.copy(18).start()

    def across(self):
        self.copy(15).wait_recv()
        self.copy(16).wait_recv()
        self.copy(19).start()

    def last(self):
        for j in self.pieces():
            self.copy(5 + 3 * j).wait_recv()
        for k in (17, 18, 19):
            self.copy(k).wait_recv()

    def drain(self):
        if not self.flat:
            for k in range(3):
                self.copy(k).wait_send()
        for j in self.pieces():
            for k in range(3):
                self.copy(3 + 3 * j + k).wait_send()
        for k in range(15, 20):
            self.copy(k).wait_send()


class Scatter:
    def __init__(self, place, grad, buffers, sends, receives, w):
        self.place, self.grad, self.w = place, grad, w
        self.sends, self.receives = sends, receives
        self.r1, self.r2a, self.r2b, self.r3a, self.r3b, self.r4 = buffers

    def copy(self, k):
        place, r1 = self.place, self.r1
        row, col, core = place.row, place.col, place.core
        if k == 0:
            pair = (self.grad.at[:, :, :, 1 - core], r1, place.sibling)
        elif k == 1:
            pair = (r1.at[0:2, :, 1 - col], self.r2a, place.x)
        elif k == 2:
            pair = (r1.at[2:4, 1 - row], self.r2b, place.y)
        elif k == 3:
            pair = (r1.at[0:2, 1 - row, col], self.r3a, place.y)
        elif k == 4:
            pair = (r1.at[2:4, row, 1 - col], self.r3b, place.x)
        else:
            peer = place.along(k - 4)
            pair = (r1.at[peer[1], row, col], self.r4.at[k - 5], peer)
        return remote(
            pair[0], pair[1], self.sends.at[self.w, k], self.receives.at[self.w, k], pair[2]
        )

    def add(self, index, other):
        ref = self.r1
        ref[index] = (ref[index].astype(F32) + other.astype(F32)).astype(ref.dtype)

    def start(self):
        self.copy(0).start()

    def planes(self):
        core = self.place.core
        self.copy(0).wait_recv()

        def step(i, carry):
            t, y = i // 2, i % 2
            self.add((t, y), self.grad[t, y, :, core])
            return carry

        lax.fori_loop(0, 8, step, 0)
        self.copy(1).start()
        self.copy(2).start()

    def lines(self):
        col, row = self.place.col, self.place.row
        self.copy(1).wait_recv()
        for t in range(2):
            for y in range(2):
                self.add((t, y, col), self.r2a[t, y])
        self.copy(3).start()
        self.copy(2).wait_recv()
        for t in range(2):
            for x in range(2):
                self.add((2 + t, row, x), self.r2b[t, x])
        self.copy(4).start()

    def points(self):
        col, row = self.place.col, self.place.row
        self.copy(3).wait_recv()
        for t in range(2):
            self.add((t, row, col), self.r3a[t])
        self.copy(4).wait_recv()
        for t in range(2):
            self.add((2 + t, row, col), self.r3b[t])
        for k in (5, 6, 7):
            self.copy(k).start()

    def result(self):
        place = self.place
        for k in (5, 6, 7):
            self.copy(k).wait_recv()
        total = self.r1[place.z, place.row, place.col].astype(F32)
        for j in range(3):
            total = total + self.r4[j].astype(F32)
        return total

    def drain(self):
        for k in range(8):
            self.copy(k).wait_send()


def scatter_buffers(rows, cols, dtype):
    return [
        pltpu.VMEM((4, 2, 2, rows, cols), dtype),
        pltpu.VMEM((2, 2, rows, cols), dtype),
        pltpu.VMEM((2, 2, rows, cols), dtype),
        pltpu.VMEM((2, rows, cols), dtype),
        pltpu.VMEM((2, rows, cols), dtype),
        pltpu.VMEM((3, rows, cols), dtype),
    ]


HEAD_SET = 3
SPAN = 3 * HD
CUT = HEAD_SET * SPAN
TILE_ROWS, TILE_COLS = 16, 256


def whole(value):
    return value.reshape(-1, value.shape[-1])


def gelu_parts(values):
    cumulative = 0.5 * (1.0 + lax.erf(values * 0.7071067811865476))
    density = 0.3989422804014327 * jnp.exp(-0.5 * values * values)
    return values * cumulative, cumulative + values * density


def halo_copies(place, window, own, semaphores):
    before = remote(
        window.at[pl.ds(HALO, HALO)],
        window.at[pl.ds(HALO + own, HALO)],
        semaphores.at[0],
        semaphores.at[1],
        place.along(3),
    )
    after = remote(
        window.at[pl.ds(own, HALO)],
        window.at[pl.ds(0, HALO)],
        semaphores.at[2],
        semaphores.at[3],
        place.along(1),
    )
    return before, after


def loader(inputs, places, semaphores):
    return [
        pltpu.make_async_copy(source, target, semaphores.at[n])
        for n, (source, target) in enumerate(zip(inputs, places))
    ]


def step_kernel(*refs):
    inputs, outputs, held = refs[:12], refs[12:22], refs[22:34]
    (
        tokens,
        segments,
        mask_grad,
        gain_one,
        attend_weight,
        output_weight,
        gain_two,
        up_weight,
        down_weight,
        patch_weight,
        class_weight,
        class_embed,
    ) = held
    results = refs[34:44]
    (
        masks,
        d_resid,
        share_p,
        share_d,
        share_u,
        share_a,
        share_n,
        class_all,
        class_row,
        class_sum,
    ) = results
    (
        full_a,
        full_u,
        full_d,
        full_p,
        full_c,
        full_e,
        grad_d,
        grad_u,
        grad_p,
        grad_n,
        grad_c,
        joint,
        attended,
        resid_one,
        norm_two,
        hidden,
        slope,
        total,
        window,
        back_window,
        norm_one,
        embed,
        embed_wide,
        resid_low,
        unit_low,
        class_low,
        stack_p,
        stack_s,
        seg_wide,
        seg_col,
        seg_row,
        class_wide,
        r4_a,
    ) = refs[44:77]
    buffers = refs[77:107]
    (
        gather_sends,
        gather_receives,
        scatter_sends,
        scatter_receives,
        line_sems,
        halo_sems,
        in_sems,
        out_sems,
    ) = refs[107:]
    loads = loader(inputs, held, in_sems)
    stores = loader(results, outputs, out_sems)
    for n in (11, 3, 6, 0, 4, 5, 10, 7, 8, 9, 1, 2):
        loads[n].start()

    place = Place()
    z, row, col, core = place.z, place.row, place.col, place.core
    own, width = tokens.shape
    span = own + 2 * HALO
    piece = width // 8
    narrow = patch_weight.shape[1]
    classes = class_embed.shape[0]
    mine = slice(HALO, HALO + own)
    ge, ga, gc, gu, gd, gp, gs = (
        Gather(place, full, gather_sends, gather_receives, w)
        for w, full in enumerate((full_e, full_a, full_c, full_u, full_d, full_p, class_sum))
    )
    sp, sd, su, sn, sc = (
        Scatter(place, g, buffers[6 * w : 6 * w + 6], scatter_sends, scatter_receives, w)
        for w, g in enumerate((grad_p, grad_d, grad_u, grad_n, grad_c))
    )
    a_buffers = (
        full_d.at[:, :, :, 0],
        full_d.at[0:2, :, 0, 1],
        full_d.at[2:4, :, 0, 1],
        full_d.at[0:2, 0, 1, 1],
        full_d.at[2:4, 0, 1, 1],
        r4_a,
    )
    grad_a = full_u
    sa = Scatter(place, grad_a, a_buffers, scatter_sends, scatter_receives, 5)
    line_row = Line(place, class_row, line_sems.at[0], line_sems.at[1])
    line_all = Line(place, class_all, line_sems.at[2], line_sems.at[3])

    embed_wide[...] = jnp.zeros_like(embed_wide)
    for n in (11, 3, 6):
        loads[n].wait()
    embed_wide[0:classes] = class_embed[...]
    embed_wide[classes : classes + 1] = gain_one[...]
    embed_wide[classes + 1 : classes + 2] = gain_two[...]
    full_e[row, col, core] = embed_wide[...].astype(BF)
    greet(place)
    ge.start()
    loads[0].wait()
    window[mine] = tokens[...]
    before, after = halo_copies(place, window, own, halo_sems.at[0])
    before.start()
    after.start()
    loads[4].wait()
    loads[5].wait()
    full_a[z, row, col, core, :, 0:CUT] = attend_weight[...].astype(BF)
    full_a[z, row, col, core, :, CUT:] = output_weight[...].T.astype(BF)
    ga.start()
    loads[10].wait()
    full_c[row, col, core] = class_weight[...].astype(BF)
    gc.start()
    class_row[z] = class_weight[...].astype(BF)
    line_row.start()
    loads[7].wait()
    full_u[z, row, col, core] = up_weight[...].astype(BF)
    gu.start()
    loads[8].wait()
    loads[9].wait()
    full_d[z, row, col, core] = down_weight[...].astype(BF)
    full_p[z, row, col, core] = patch_weight[...].astype(BF)

    loads[1].wait()
    loads[2].wait()
    seg_wide[...] = jnp.full_like(seg_wide, -1.0)
    seg_wide[:, HALO : HALO + segments.shape[1]] = segments[...].astype(F32)
    seg_row[...] = seg_wide[:, pl.ds(pl.multiple_of(z * own, 128), span)]
    seg_col[...] = jnp.broadcast_to(seg_row[...], (8, span)).T[:, 0:1]

    ge.forward()
    ge.across()
    ga.spread()
    ge.last()
    gd.start()
    gc.forward()
    before.wait_recv()
    after.wait_recv()
    for d in range(8):
        embed[:, d * piece : (d + 1) * piece] = full_e[d // 4, (d // 2) % 2, d % 2]
    gains = embed[classes : classes + 2, :].astype(F32)
    gain_first, gain_second = gains[0:1], gains[1:2]

    def first_norm(i, carry):
        rows = pl.ds(pl.multiple_of(i * 128, 128), 128)
        xhat, _ = norm_parts(window[rows].astype(F32))
        norm_one[rows] = (xhat * gain_first).astype(BF)
        return carry

    lax.fori_loop(0, span // 128, first_norm, 0)
    gu.spread()
    ga.forward()
    gc.across()
    ga.across()
    gc.last()
    gd.spread()
    gp.start()
    class_all[z] = dot(embed[...], whole(full_c[...]))
    line_all.start()
    line_row.wait()
    stores[8].start()
    ga.last()

    def project(t, carry):
        joint[t] = dot(norm_one[...], whole(full_a[t])[:, :CUT]).astype(BF)
        return carry

    lax.fori_loop(0, 4, project, 0)
    gu.forward()

    def attend(t, carry):
        for h in range(HEAD_SET):
            q_cols = slice(h * SPAN, h * SPAN + HD)
            k_cols = slice(h * SPAN + HD, h * SPAN + 2 * HD)
            v_cols = slice(h * SPAN + 2 * HD, h * SPAN + 3 * HD)
            for b in range(own // 128):
                near = slice(b * 128, b * 128 + 384)
                rows = slice(HALO + b * 128, HALO + (b + 1) * 128)
                scores = dot(joint[t, rows, q_cols], joint[t, near, k_cols], ((1,), (1,)))
                match = seg_col[rows] == seg_row[:, near]
                scores = jnp.where(match, scores * HD**-0.5, masked_score)
                exponent = jnp.exp(scores - jnp.max(scores, axis=-1, keepdims=True))
                row_total = jnp.sum(exponent, axis=-1, keepdims=True)
                prob = (exponent / row_total).astype(BF)
                attended[t, b * 128 : (b + 1) * 128, h * HD : (h + 1) * HD] = dot(
                    prob, joint[t, near, v_cols]
                ).astype(BF)
        return carry

    lax.fori_loop(0, 2, attend, 0)
    gp.spread()
    gu.across()
    lax.fori_loop(2, 4, attend, 0)
    gd.forward()
    resid_one[...] = tokens[...].astype(F32)

    def output(t, carry):
        resid_one[...] += dot(attended[t], whole(full_a[t])[:, CUT:], ((1,), (1,)))
        return carry

    lax.fori_loop(0, 4, output, 0)
    xhat, _ = norm_parts(resid_one[...])
    norm_two[...] = (xhat * gain_second).astype(BF)
    line_all.wait()
    stores[7].start()
    class_square = jnp.zeros((class_all.shape[1], 1), F32)
    for t in range(4):
        class_square += jnp.sum(class_all[t] * class_all[t], axis=-1, keepdims=True)
    class_inverse = lax.rsqrt(class_square + epsilon_unit)
    for t in range(4):
        class_low[t] = (class_all[t] * class_inverse).astype(BF)
    gu.last()
    gp.forward()

    def expand(t, carry):
        value, derivative = gelu_parts(dot(norm_two[...], whole(full_u[t])))
        hidden[t] = value.astype(BF)
        slope[t] = derivative.astype(BF)
        return carry

    lax.fori_loop(0, 4, expand, 0)
    gd.across()
    gp.across()
    gd.last()
    total[...] = resid_one[...]

    def contract(t, carry):
        total[...] += dot(hidden[t], whole(full_d[t]), ((1,), (1,)))
        return carry

    lax.fori_loop(0, 4, contract, 0)
    resid_low[...] = total[...].astype(BF)
    gp.last()

    square = jnp.zeros((own, 1), F32)
    pieces = []
    for t in range(4):
        value = dot(resid_low[...], whole(full_p[t]))
        square += jnp.sum(value * value, axis=-1, keepdims=True)
        pieces.append(value)
    inverse = lax.rsqrt(square + epsilon_unit)
    products = jnp.zeros((class_low.shape[1], own), F32)
    for t in range(4):
        pieces[t] = pieces[t] * inverse
        unit_low[t] = pieces[t].astype(BF)
        products += dot(class_low[t], unit_low[t], ((1,), (1,)))
    products = products[:classes]
    centred = products - jnp.mean(products, axis=0, keepdims=True)
    spread = jnp.mean(centred * centred, axis=0, keepdims=True)
    mask_inverse = lax.rsqrt(spread + epsilon_norm)
    centred = centred * mask_inverse
    masks[...] = centred
    stores[0].start()
    d_masks = mask_grad[...]
    d_products = mask_inverse * (
        d_masks
        - jnp.mean(d_masks, axis=0, keepdims=True)
        - centred * jnp.mean(d_masks * centred, axis=0, keepdims=True)
    )
    d_products = d_products.astype(BF)
    along = jnp.zeros((own, 1), F32)
    d_pieces = []
    for t in range(4):
        value = dot(d_products, class_low[t, :classes], ((0,), (0,)))
        along += jnp.sum(value * pieces[t], axis=-1, keepdims=True)
        d_pieces.append(value)
    flipped = resid_low[...].T
    d_total = jnp.zeros((own, width), F32)
    for t in range(4):
        value = (inverse * (d_pieces[t] - pieces[t] * along)).astype(BF)
        grad_p[t] = dot(flipped, value).astype(BF).reshape(grad_p.shape[1:])
        d_total += dot(value, whole(full_p[t]), ((1,), (1,)))
    sp.start()
    d_resid[...] = d_total
    branch = d_total.astype(BF)
    flipped = branch.T

    def down(t, carry):
        grad_d[t] = dot(flipped, hidden[t]).astype(BF).reshape(grad_d.shape[1:])
        return carry

    lax.fori_loop(0, 4, down, 0)
    sd.start()
    sp.planes()
    flipped = norm_two[...].T

    def up(t, carry):
        back = dot(branch, whole(full_d[t])) * slope[t].astype(F32)
        back = back.astype(BF)
        slope[t] = back
        grad_u[t] = dot(flipped, back).astype(BF).reshape(grad_u.shape[1:])
        return carry

    lax.fori_loop(0, 4, up, 0)
    sd.planes()
    for transfer in (ge, ga, gc, gu, gd, gp):
        transfer.drain()
    su.start()
    class_wide[...] = jnp.zeros_like(class_wide)
    for t in range(4):
        class_wide[0:classes, t * narrow : (t + 1) * narrow] = dot(
            d_products, unit_low[t]
        )
    grad_c[...] = jnp.zeros_like(grad_c)
    tiles = width // TILE_COLS
    for i in range(class_wide.shape[0] // TILE_ROWS * tiles):
        r, q = i // tiles, i % tiles
        grad_c[i // 8, (i // 4) % 2, (i // 2) % 2, i % 2] = class_wide[
            r * TILE_ROWS : (r + 1) * TILE_ROWS, q * TILE_COLS : (q + 1) * TILE_COLS
        ].astype(BF)
    sc.start()
    total[...] = jnp.zeros_like(total)

    def narrow_back(t, carry):
        total[...] += dot(slope[t], whole(full_u[t]), ((1,), (1,)))
        return carry

    lax.fori_loop(0, 4, narrow_back, 0)
    su.planes()
    sc.planes()
    xhat, inverse = norm_parts(resid_one[...])
    gain_two_sum = jnp.sum(total[...] * xhat, axis=0, keepdims=True)
    d_resid[...] += norm_back(total[...] * gain_second, xhat, inverse)
    back_window[mine] = d_resid[...].astype(BF)
    back_before, back_after = halo_copies(place, back_window, own, halo_sems.at[1])
    back_before.start()
    back_after.start()
    sp.lines()
    flipped = back_window[mine].T

    def outer(t, carry):
        block = dot(flipped, attended[t]).astype(BF)
        grad_a[t, :, :, :, :, CUT:] = block.reshape((2, 2, 2, piece, width - CUT))
        return carry

    lax.fori_loop(0, 4, outer, 0)
    sc.lines()
    back_before.wait_recv()
    back_after.wait_recv()

    def attended_back(t, carry):
        value = dot(back_window[...], whole(full_a[t])[:, CUT:]).astype(BF)
        slope[t, :, 0:narrow] = value[0:own]
        slope[t, :, 256 : 256 + narrow] = value[own:span]
        return carry

    lax.fori_loop(0, 4, attended_back, 0)
    sd.lines()
    sp.points()
    sc.points()
    stack_p[...] = jnp.zeros_like(stack_p)
    stack_s[...] = jnp.zeros_like(stack_s)

    def attend_back(t, carry):
        for h in range(HEAD_SET):
            q_cols = slice(h * SPAN, h * SPAN + HD)
            k_cols = slice(h * SPAN + HD, h * SPAN + 2 * HD)
            v_cols = slice(h * SPAN + 2 * HD, h * SPAN + 3 * HD)
            for b in range(4):
                rows = slice(b * 128, (b + 1) * 128)
                low_key, high_key = max(b - 1, 0) * 128, min(b + 2, 4) * 128
                near = slice(low_key, high_key)
                key = joint[t, near, k_cols]
                scores = dot(joint[t, rows, q_cols], key, ((1,), (1,)))
                match = seg_col[rows] == seg_row[:, near]
                scores = jnp.where(match, scores * HD**-0.5, masked_score)
                exponent = jnp.exp(scores - jnp.max(scores, axis=-1, keepdims=True))
                prob = exponent / jnp.sum(exponent, axis=-1, keepdims=True)
                d_cols = slice(b // 2 * 256 + h * HD, b // 2 * 256 + (h + 1) * HD)
                d_rows = slice(b % 2 * 128, (b % 2 + 1) * 128)
                d_prob = dot(slope[t, d_rows, d_cols], joint[t, near, v_cols], ((1,), (1,)))
                delta = jnp.sum(prob * d_prob, axis=-1, keepdims=True)
                d_scores = (prob * (d_prob - delta)).astype(BF)
                prob = prob.astype(BF)
                first, last = max(low_key, HALO), min(high_key, HALO + own)
                place_in = slice(first - HALO, last - HALO)
                part = slice(first - low_key, last - low_key)
                stack_p[rows, place_in] = prob[:, part]
                stack_s[rows, place_in] = d_scores[:, part]
                if b in (1, 2):
                    hidden[t, (b - 1) * 128 : b * 128, q_cols] = (
                        dot(d_scores, key) * HD**-0.5
                    ).astype(BF)
            hidden[t, :, k_cols] = (
                dot(stack_s[...], joint[t, :, q_cols], ((0,), (0,))) * HD**-0.5
            ).astype(BF)
            d_value = dot(stack_p[0:own], slope[t, :, h * HD : (h + 1) * HD], ((0,), (0,)))
            d_value += dot(
                stack_p[own:span], slope[t, :, 256 + h * HD : 256 + (h + 1) * HD], ((0,), (0,))
            )
            hidden[t, :, v_cols] = d_value.astype(BF)
        return carry

    lax.fori_loop(0, 2, attend_back, 0)
    su.lines()
    class_sum[z, row, col, core] = sc.result().astype(BF)
    gs.start()
    lax.fori_loop(2, 4, attend_back, 0)
    gs.spread()
    flipped = norm_one[mine].T

    def attend_grad(t, carry):
        block = dot(flipped, hidden[t, :, :CUT]).astype(BF)
        grad_a[t, :, :, :, :, :CUT] = block.reshape((2, 2, 2, piece, CUT))
        return carry

    lax.fori_loop(0, 4, attend_grad, 0)
    sa.start()
    sd.points()
    sa.planes()
    total[...] = jnp.zeros_like(total)

    def joint_back(t, carry):
        total[...] += dot(hidden[t, :, :CUT], whole(full_a[t])[:, :CUT], ((1,), (1,)))
        return carry

    lax.fori_loop(0, 4, joint_back, 0)
    su.points()
    gs.forward()
    xhat, inverse = norm_parts(tokens[...].astype(F32))
    gain_one_sum = jnp.sum(total[...] * xhat, axis=0, keepdims=True)
    d_resid[...] += norm_back(total[...] * gain_first, xhat, inverse)
    stores[1].start()
    grad_n[...] = jnp.zeros_like(grad_n)
    for d in range(8):
        cols = slice(d * piece, (d + 1) * piece)
        for t in range(4):
            spot = (t, d // 4, (d // 2) % 2, d % 2)
            grad_n[spot + (slice(0, 1), slice(0, piece))] = gain_one_sum[:, cols]
            grad_n[spot + (slice(1, 2), slice(0, piece))] = gain_two_sum[:, cols]
    sn.start()
    sn.planes()
    share_p[...] = sp.result()
    stores[2].start()
    sa.lines()
    sn.lines()
    gs.across()
    share_d[...] = sd.result()
    stores[3].start()
    gs.last()
    stores[9].start()
    sa.points()
    sn.points()
    share_u[...] = su.result()
    stores[4].start()
    share_n[...] = sn.result()
    stores[6].start()
    share_a[...] = sa.result()
    stores[5].start()
    for copy in (before, after, back_before, back_after):
        copy.wait_send()
    for transfer in (gs, sp, sd, su, sn, sc, sa, line_row, line_all):
        transfer.drain()
    for store in stores:
        store.wait()


def vmem_specs(count):
    return [pl.BlockSpec(memory_space=pltpu.VMEM)] * count


def any_specs(count):
    return [pl.BlockSpec(memory_space=pl.ANY)] * count


def step_call(tokens, segments, mask_grad, params):
    own, width = tokens.shape
    gain_one, attend, output, gain_two, up, down, patch, classed, embed = params
    classes = embed.shape[0]
    rows_e = -(-(classes + 2) // 32) * 32
    piece, high, narrow = up.shape[0], up.shape[1], patch.shape[1]
    span = own + 2 * HALO
    low = lambda *shape: pltpu.VMEM(shape, BF)
    wide = lambda *shape: pltpu.VMEM(shape, F32)
    shape = jax.ShapeDtypeStruct
    operands = (tokens, segments, mask_grad, gain_one[None], attend, output, gain_two[None])
    operands += tuple(params[4:])
    outs = [
        shape((classes, own), F32),
        shape((own, width), F32),
        shape((piece, narrow), F32),
        shape((piece, high), F32),
        shape((piece, high), F32),
        shape((piece, width), F32),
        shape((8, 128), F32),
        shape((4, rows_e, narrow), F32),
        shape((4, piece, narrow), BF),
        shape((4, 2, 2, 2, TILE_ROWS, TILE_COLS), BF),
    ]
    scratch = [pltpu.VMEM(v.shape, v.dtype) for v in operands]
    scratch += [pltpu.VMEM(v.shape, v.dtype) for v in outs]
    scratch += [
        low(4, 2, 2, 2, piece, width),
        low(4, 2, 2, 2, piece, high),
        low(4, 2, 2, 2, piece, high),
        low(4, 2, 2, 2, piece, narrow),
        low(2, 2, 2, piece, narrow),
        low(2, 2, 2, rows_e, piece),
        low(4, 2, 2, 2, piece, high),
        low(4, 2, 2, 2, piece, high),
        low(4, 2, 2, 2, piece, narrow),
        wide(4, 2, 2, 2, 8, 128),
        low(4, 2, 2, 2, TILE_ROWS, TILE_COLS),
        low(4, span, CUT),
        low(4, own, narrow),
        wide(own, width),
        low(own, width),
        low(4, own, high),
        low(4, own, high),
        wide(own, width),
        low(span, width),
        low(span, width),
        low(span, width),
        low(rows_e, width),
        wide(rows_e, piece),
        low(own, width),
        low(4, own, narrow),
        low(4, rows_e, narrow),
        low(span, own),
        low(span, own),
        wide(1, segments.shape[1] + 2 * HALO),
        wide(span, 1),
        wide(1, span),
        wide(rows_e, width),
        low(3, piece, width),
    ]
    for rows, cols, dtype in (
        (piece, narrow, BF),
        (piece, high, BF),
        (piece, high, BF),
        (8, 128, F32),
        (TILE_ROWS, TILE_COLS, BF),
    ):
        scratch += scatter_buffers(rows, cols, dtype)
    scratch += [
        pltpu.SemaphoreType.DMA((7, 20)),
        pltpu.SemaphoreType.DMA((7, 20)),
        pltpu.SemaphoreType.DMA((6, 8)),
        pltpu.SemaphoreType.DMA((6, 8)),
        pltpu.SemaphoreType.DMA((4, 3)),
        pltpu.SemaphoreType.DMA((2, 4)),
        pltpu.SemaphoreType.DMA((len(operands),)),
        pltpu.SemaphoreType.DMA((len(outs),)),
    ]
    return pl.pallas_call(
        step_kernel,
        out_shape=outs,
        in_specs=any_specs(len(operands)),
        out_specs=any_specs(len(outs)),
        scratch_shapes=scratch,
        compiler_params=pltpu.CompilerParams(
            collective_id=0, has_side_effects=True, vmem_limit_bytes=VMEM_LIMIT
        ),
    )(*operands)


def update_kernel(*refs):
    inputs, outputs, held = refs[:37], refs[37:57], refs[57:94]
    class_back, sum_wide, in_sems, out_sems = refs[94:]
    masks, token_grad, share_p, share_d, share_u, share_a, share_n = held[:7]
    class_all, class_row, class_sum = held[7:10]
    params, means, squares = held[10:19], held[19:28], held[28:37]
    loads = loader(inputs, held, in_sems)
    stores = loader(held[:2] + squares + means, outputs, out_sems)
    order = (0, 3, 6, 4, 5, 2, 1, 8, 7)
    for n in (6, 0, 1, 2, 4, 3, 5, 7, 8, 9):
        loads[n].start()
    for n in order:
        for k in (10, 19, 28):
            loads[k + n].start()
    for n in range(10):
        loads[n].wait()
        if n < 2:
            stores[n].start()

    def update(n, gradient):
        scale = block_scale if n < 6 else 1.0
        decay = 0.0 if n in (0, 3) else weight_decay
        for k in (10, 19, 28):
            if k + n != 18:
                loads[k + n].wait()
        squares[n][...], means[n][...] = adamw_update(
            params[n][...], gradient, means[n][...], squares[n][...], scale, decay
        )
        stores[2 + n].start()
        stores[11 + n].start()

    piece = share_p.shape[0]
    update(0, share_n[0:1, 0:piece])
    update(3, share_n[1:2, 0:piece])
    update(6, share_p[...])
    update(4, share_u[...])
    update(5, share_d[...])
    update(2, share_a[:, CUT:].T)
    update(1, share_a[:, :CUT])

    classes = params[8].shape[0]
    narrow = class_all.shape[2]
    tiles = sum_wide.shape[1] // TILE_COLS
    for i in range(sum_wide.shape[0] // TILE_ROWS * tiles):
        r, q = i // tiles, i % tiles
        sum_wide[
            r * TILE_ROWS : (r + 1) * TILE_ROWS, q * TILE_COLS : (q + 1) * TILE_COLS
        ] = class_sum[i // 8, (i // 4) % 2, (i // 2) % 2, i % 2].astype(F32)
    square = jnp.zeros((classes, 1), F32)
    for t in range(4):
        value = class_all[t, :classes]
        square += jnp.sum(value * value, axis=-1, keepdims=True)
    inverse = lax.rsqrt(square + epsilon_unit)
    along = jnp.zeros((classes, 1), F32)
    for t in range(4):
        unit = class_all[t, :classes] * inverse
        d_unit = sum_wide[:classes, t * narrow : (t + 1) * narrow]
        along += jnp.sum(unit * d_unit, axis=-1, keepdims=True)
    share_embed = jnp.zeros((classes, piece), F32)
    loads[18].wait()
    embed_low = params[8][...].astype(BF)
    for t in range(4):
        unit = class_all[t, :classes] * inverse
        d_unit = sum_wide[:classes, t * narrow : (t + 1) * narrow]
        value = (inverse * (d_unit - unit * along)).astype(BF)
        class_back[t] = value
        share_embed += dot(value, class_row[t], ((1,), (1,)))
    update(8, share_embed)
    update(7, dot(embed_low, class_back[lax.axis_index("tensor")], ((0,), (0,))))
    for store in stores:
        store.wait()


def update_call(results, params, means, squares):
    flat = lambda arrays: [a[None] if a.ndim == 1 else a for a in arrays]
    params, means, squares = flat(params), flat(means), flat(squares)
    classes, narrow = params[8].shape[0], params[7].shape[1]
    rows_e, width = results[7].shape[1], results[1].shape[1]
    operands = (*results, *params, *means, *squares)
    shape = jax.ShapeDtypeStruct
    outs = [shape(r.shape, F32) for r in results[:2]]
    outs += [shape(p.shape, F32) for p in params] * 2
    return pl.pallas_call(
        update_kernel,
        out_shape=outs,
        in_specs=any_specs(len(operands)),
        out_specs=any_specs(len(outs)),
        scratch_shapes=[pltpu.VMEM(v.shape, v.dtype) for v in operands]
        + [
            pltpu.VMEM((4, classes, narrow), BF),
            pltpu.VMEM((rows_e, width), F32),
            pltpu.SemaphoreType.DMA((len(operands),)),
            pltpu.SemaphoreType.DMA((len(outs),)),
        ],
        compiler_params=pltpu.CompilerParams(vmem_limit_bytes=VMEM_LIMIT),
    )(*operands)


def finish(masks, token_grad, grads, params, means, squares):
    scales = (block_scale,) * 6 + (1.0,) * 3
    decays = (0.0, weight_decay, weight_decay, 0.0) + (weight_decay,) * 5
    new = [adamw_update(*v) for v in zip(params, grads, means, squares, scales, decays)]
    return (masks, token_grad) + tuple(n[0] for n in new) + tuple(n[1] for n in new)


def gather_plain(shards, embed):
    def full(s):
        return lax.all_gather(lax.all_gather(s, "dp", axis=0), "tensor", axis=0)

    return [full(s) for s in shards] + [lax.all_gather(embed, "dp", axis=0)]


def scatter_plain(grads):
    def share(g):
        part = lax.psum_scatter(g, "dp", scatter_dimension=1, tiled=True)
        return lax.psum_scatter(part, "tensor", scatter_dimension=0, tiled=True)[0]

    return [share(g).astype(F32) for g in grads]


def with_halo(rows, parts):
    forward = [(i, i + 1) for i in range(parts - 1)]
    backward = [(i + 1, i) for i in range(parts - 1)]
    before = lax.ppermute(rows[-HALO:], "tensor", forward)
    after = lax.ppermute(rows[:HALO], "tensor", backward)
    return jnp.concatenate((before, rows, after), axis=0)


def local_plain(
    parts,
    tokens,
    segments,
    mask_grad,
    gain_one,
    attend_weight,
    output_weight,
    gain_two,
    up_weight,
    down_weight,
    patch_weight,
    class_weight,
    class_embed,
    *moments,
):
    means, squares = moments[:9], moments[9:]
    own = tokens.shape[0]
    width = tokens.shape[1]
    classes = class_embed.shape[0]
    dp_index = lax.axis_index("dp")
    tensor_index = lax.axis_index("tensor")
    low = lambda v: v.astype(BF)

    shard_a = jnp.concatenate((low(attend_weight), low(output_weight).T), axis=1)
    shard_u = low(up_weight)
    shard_d = low(down_weight).T
    shard_p = jnp.concatenate((low(patch_weight), low(class_weight)), axis=1)
    rows_e = -(-(classes + 2) // 32) * 32
    shard_e = jnp.zeros((rows_e, class_embed.shape[1]), BF)
    shard_e = shard_e.at[:classes].set(low(class_embed))
    shard_e = shard_e.at[classes].set(low(gain_one)).at[classes + 1].set(low(gain_two))
    full_a, full_u, full_d, full_p, full_e = gather_plain(
        (shard_a, shard_u, shard_d, shard_p), shard_e
    )
    full_a, full_u, full_d, full_p = (
        v.reshape(v.shape[0], width, v.shape[-1]) for v in (full_a, full_u, full_d, full_p)
    )
    embed_rows = full_e.transpose(1, 0, 2).reshape(rows_e, width)
    embed = embed_rows[:classes]
    gain_first = embed_rows[classes].astype(F32)[None]
    gain_second = embed_rows[classes + 1].astype(F32)[None]

    cut = attend_weight.shape[1]
    heads = cut // (3 * HD)
    w_attend, w_output = full_a[:, :, :cut], full_a[:, :, cut:]
    narrow = patch_weight.shape[1]
    w_patch, w_class = full_p[:, :, :narrow], full_p[:, :, narrow:]
    w_patch = w_patch.transpose(1, 0, 2).reshape(width, -1)
    w_class = w_class.transpose(1, 0, 2).reshape(width, -1)

    window = with_halo(tokens, parts)
    token_wide = window.astype(F32)
    xhat_one, inverse_one = norm_parts(token_wide)
    norm_one = low(xhat_one * gain_first)
    joint = jnp.einsum("sd,tdn->stn", norm_one, w_attend, preferred_element_type=F32)
    joint = low(joint).reshape(own + 2 * HALO, parts * heads, 3, HD)
    queries, keys, values = joint[:, :, 0], joint[:, :, 1], joint[:, :, 2]
    padded = jnp.pad(segments[0], HALO, constant_values=-1)
    seg = lax.dynamic_slice_in_dim(padded, tensor_index * own, own + 2 * HALO, 0)
    scores = jnp.einsum("qhd,khd->hqk", queries, keys, preferred_element_type=F32) * HD**-0.5
    scores = jnp.where(seg[None, :, None] == seg[None, None, :], scores, masked_score)
    exponent = jnp.exp(scores - jnp.max(scores, axis=-1, keepdims=True))
    prob = exponent / jnp.sum(exponent, axis=-1, keepdims=True)
    prob_low = low(prob)
    mine = slice(HALO, HALO + own)
    attended = jnp.einsum(
        "hqk,khd->qhd", prob_low[:, mine], values, preferred_element_type=F32
    )
    attended = low(attended).reshape(own, parts, heads * HD)
    resid_one = token_wide[mine] + jnp.einsum(
        "stn,tdn->sd", attended, w_output, preferred_element_type=F32
    )
    xhat_two, inverse_two = norm_parts(resid_one)
    norm_two = low(xhat_two * gain_second)
    hidden_pre = jnp.einsum("sd,tdn->stn", norm_two, full_u, preferred_element_type=F32)
    hidden, gelu_back = jax.vjp(lambda v: jax.nn.gelu(v, approximate=False), hidden_pre)
    hidden = low(hidden)
    resid_two = resid_one + jnp.einsum(
        "stn,tdn->sd", hidden, full_d, preferred_element_type=F32
    )
    resid_low = low(resid_two)
    patch_feat = dot(resid_low, w_patch)
    patch_wide, patch_inverse = unit_parts(patch_feat)
    patch_unit = low(patch_wide)
    class_feat = dot(embed, w_class)
    class_wide, class_inverse = unit_parts(class_feat)
    class_unit = low(class_wide)
    products = dot(patch_unit, class_unit, ((1,), (1,)))
    masks, mask_inverse = norm_parts(products)
    d_products = low(norm_back(mask_grad, masks, mask_inverse))
    d_class_unit = lax.psum(dot(d_products, patch_unit, ((0,), (0,))), ("dp", "tensor"))
    d_patch_unit = dot(d_products, class_unit)
    d_patch_feat = low(unit_back(d_patch_unit, patch_wide, patch_inverse))
    grad_patch = dot(resid_low, d_patch_feat, ((0,), (0,)))
    d_resid_two = dot(d_patch_feat, w_patch, ((1,), (1,)))
    d_branch_two = low(d_resid_two)
    d_hidden = jnp.einsum("sd,tdn->stn", d_branch_two, full_d, preferred_element_type=F32)
    grad_down = jnp.einsum("sd,stn->tdn", d_branch_two, hidden, preferred_element_type=F32)
    d_hidden_pre = low(gelu_back(d_hidden)[0])
    grad_up = jnp.einsum("sd,stn->tdn", norm_two, d_hidden_pre, preferred_element_type=F32)
    d_norm_two = jnp.einsum("stn,tdn->sd", d_hidden_pre, full_u, preferred_element_type=F32)
    d_resid_one = d_resid_two + norm_back(d_norm_two * gain_second, xhat_two, inverse_two)
    grad_gain_two = jnp.sum(d_norm_two * xhat_two, axis=0)
    d_branch_one = with_halo(low(d_resid_one), parts)
    d_attended = low(
        jnp.einsum("sd,tdn->stn", d_branch_one, w_output, preferred_element_type=F32)
    )
    grad_output = jnp.einsum(
        "sd,stn->tdn", d_branch_one[mine], attended, preferred_element_type=F32
    )
    d_attended = d_attended.reshape(own + 2 * HALO, parts * heads, HD)
    d_prob = jnp.einsum("qhd,khd->hqk", d_attended, values, preferred_element_type=F32)
    delta = jnp.sum(prob * d_prob, axis=-1, keepdims=True)
    d_scores = low(prob * (d_prob - delta))
    d_query = jnp.einsum(
        "hqk,khd->qhd", d_scores[:, mine], keys, preferred_element_type=F32
    )
    d_key = jnp.einsum(
        "hqk,qhd->khd", d_scores[:, :, mine], queries, preferred_element_type=F32
    )
    d_value = jnp.einsum(
        "hqk,qhd->khd", prob_low[:, :, mine], d_attended, preferred_element_type=F32
    )
    d_joint = low(
        jnp.stack((d_query * HD**-0.5, d_key * HD**-0.5, d_value), axis=2)
    ).reshape(own, parts, cut)
    grad_attend = jnp.einsum(
        "sd,stn->tdn", norm_one[mine], d_joint, preferred_element_type=F32
    )
    d_norm_one = jnp.einsum("stn,tdn->sd", d_joint, w_attend, preferred_element_type=F32)
    token_grad = d_resid_one + norm_back(
        d_norm_one * gain_first, xhat_one[mine], inverse_one[mine]
    )
    grad_gain_one = jnp.sum(d_norm_one * xhat_one[mine], axis=0)

    grad_patch = grad_patch.reshape(width, parts, narrow).transpose(1, 0, 2)
    share_p, share_d, share_u, share_a = scatter_plain(
        [
            grad_patch,
            grad_down,
            grad_up,
            jnp.concatenate((grad_attend, grad_output), axis=2),
        ]
    )
    gains = lax.psum((grad_gain_one, grad_gain_two), ("dp", "tensor"))
    step = gain_one.shape[0]
    share_one, share_two = (lax.dynamic_slice_in_dim(g, dp_index * step, step, 0) for g in gains)
    d_class_feat = low(unit_back(d_class_unit, class_wide, class_inverse))
    d_class_own = lax.dynamic_slice_in_dim(d_class_feat, tensor_index * narrow, narrow, 1)
    share_class = dot(low(class_embed), d_class_own, ((0,), (0,)))
    class_rows = lax.dynamic_slice_in_dim(w_class, dp_index * step, step, 0)
    share_embed = dot(d_class_feat, class_rows, ((1,), (1,)))
    return finish(
        masks,
        token_grad,
        (
            share_one,
            share_a[:, :cut],
            share_a[:, cut:].T,
            share_two,
            share_u,
            share_d.T,
            share_p,
            share_class,
            share_embed,
        ),
        (
            gain_one,
            attend_weight,
            output_weight,
            gain_two,
            up_weight,
            down_weight,
            patch_weight,
            class_weight,
            class_embed,
        ),
        means,
        squares,
    )


def local_kernels(tokens, segments, mask_grad, *arrays):
    def turned(group):
        return (*group[:5], group[5].T, *group[6:])

    params, means, squares = (turned(arrays[n : n + 9]) for n in (0, 9, 18))
    results = step_call(tokens, segments, mask_grad.T, params)
    masks, token_grad, *new = update_call(results, params, means, squares)
    new = [n.reshape(p.shape) for n, p in zip(new, params * 2)]
    return (masks.T, token_grad, *turned(new[:9]), *turned(new[9:]))


def solution(mesh):
    parts = mesh.shape["tensor"]
    custom = mesh.shape["dp"] == 8 and parts == 4
    params = (
        P("dp"),
        P("dp", "tensor"),
        P("tensor", "dp"),
        P("dp"),
        P("dp", "tensor"),
        P("tensor", "dp"),
        P("dp", "tensor"),
        P("dp", "tensor"),
        P(None, "dp"),
    )
    rows = P(("dp", "tensor"), None)
    return jax.shard_map(
        local_kernels if custom else functools.partial(local_plain, parts),
        mesh=mesh,
        in_specs=(rows, P("dp", None), rows) + params * 3,
        out_specs=(rows, rows) + params * 2,
        check_vma=False,
    )
```

```python
import functools

import jax
import jax.numpy as jnp
from jax import lax
from jax.experimental import pallas as pl
from jax.experimental.pallas import tpu as pltpu
from jax.sharding import PartitionSpec as P

HD = 64
HALO = 128
BF = jnp.bfloat16
F32 = jnp.float32
MESH = pl.DeviceIdType.MESH
VMEM_LIMIT = 64 * 1024 * 1024 - 512 * 1024

epsilon_norm = 1e-05
epsilon_unit = 1e-06
masked_score = -1000000000.0
first_decay = 0.9
second_decay = 0.999
first_fix = 0.99997343860112
second_fix = 0.09520785288629
adam_epsilon = 1e-08
block_scale = 0.65
weight_decay = 0.05


def dot(left, right, dims=((1,), (0,))):
    return lax.dot_general(left, right, (dims, ((), ())), preferred_element_type=F32)


def layer_norm(values, gain):
    center = values - jnp.mean(values, axis=-1, keepdims=True)
    spread = jnp.mean(center * center, axis=-1, keepdims=True)
    return center * lax.rsqrt(spread + epsilon_norm) * gain


def norm_parts(values):
    center = values - jnp.mean(values, axis=-1, keepdims=True)
    spread = jnp.mean(center * center, axis=-1, keepdims=True)
    inverse = lax.rsqrt(spread + epsilon_norm)
    return center * inverse, inverse


def norm_back(gradient, xhat, inverse):
    return inverse * (
        gradient
        - jnp.mean(gradient, axis=-1, keepdims=True)
        - xhat * jnp.mean(gradient * xhat, axis=-1, keepdims=True)
    )


def unit_parts(values):
    inverse = lax.rsqrt(jnp.sum(values * values, axis=-1, keepdims=True) + epsilon_unit)
    return values * inverse, inverse


def unit_back(gradient, unit, inverse):
    return inverse * (gradient - unit * jnp.sum(unit * gradient, axis=-1, keepdims=True))


def adamw_update(current, gradient, mean_old, square_old, step_scale, decay_rate):
    mean_new = first_decay * mean_old + (1.0 - first_decay) * gradient
    square_new = second_decay * square_old + (1.0 - second_decay) * gradient * gradient
    moved = mean_new / first_fix / (jnp.sqrt(square_new / second_fix) + adam_epsilon)
    return (step_scale * (moved + decay_rate * current), mean_new)


class Place:
    def __init__(self):
        dp, z = lax.axis_index("dp"), lax.axis_index("tensor")
        self.dp, self.z = dp, z
        self.core, self.col, self.row = dp % 2, (dp // 2) % 2, dp // 4
        self.x = (dp + 2 * (1 - 2 * self.col), z)
        self.y = (dp + 4 * (1 - 2 * self.row), z)
        self.sibling = (dp + 1 - 2 * self.core, z)

    def along(self, j):
        return (self.dp, (self.z + j) % 4)


def greet(place):
    barrier = pltpu.get_barrier_semaphore()
    targets = [place.x, place.y, place.sibling] + [place.along(j) for j in (1, 2, 3)]
    for target in targets:
        pl.semaphore_signal(barrier, inc=1, device_id=target, device_id_type=MESH)
    pl.semaphore_wait(barrier, 6)


def remote(source, target_ref, sends, receives, device):
    return pltpu.make_async_remote_copy(
        src_ref=source,
        dst_ref=target_ref,
        send_sem=sends,
        recv_sem=receives,
        device_id=device,
        device_id_type=MESH,
    )


class Line:
    def __init__(self, place, full, sends, receives):
        self.copies = [
            remote(
                full.at[place.z], full.at[place.z], sends.at[k], receives.at[k], place.along(k + 1)
            )
            for k in range(3)
        ]

    def start(self):
        for copy in self.copies:
            copy.start()

    def wait(self):
        for copy in self.copies:
            copy.wait_recv()

    def drain(self):
        for copy in self.copies:
            copy.wait_send()


class Gather:
    def __init__(self, place, full, sends, receives, w):
        self.place, self.full, self.w = place, full, w
        self.sends, self.receives = sends, receives
        self.flat = len(full.shape) == 5

    def copy(self, k):
        place, full = self.place, self.full
        row, col, core, z = place.row, place.col, place.core, place.z
        if k < 3:
            view, target = full.at[z, row, col, core], place.along(k + 1)
        elif k < 15:
            j = (k - 3) // 3
            if self.flat:
                view = full.at[row, col, core]
            else:
                view = full.at[(z + j) % 4, row, col, core]
            target = (place.x, place.y, place.sibling)[(k - 3) % 3]
        elif k < 17:
            spot = (row, 1 - col, core) if k == 15 else (1 - row, col, core)
            if self.flat:
                half = full.shape[3] // 2
                view = full.at[spot + (pl.ds((k - 15) * half, half),)]
            else:
                view = full.at[(pl.ds((k - 15) * 2, 2),) + spot]
            target = place.y if k == 15 else place.x
        else:
            spot = ((row, 1 - col, core), (1 - row, col, core), (1 - row, 1 - col, core))[k - 17]
            view = full.at[spot] if self.flat else full.at[(slice(None),) + spot]
            target = place.sibling
        return remote(view, view, self.sends.at[self.w, k], self.receives.at[self.w, k], target)

    def pieces(self):
        return range(1 if self.flat else 4)

    def start(self):
        if not self.flat:
            for k in range(3):
                self.copy(k).start()
        for k in (3, 4, 5):
            self.copy(k).start()

    def spread(self):
        if not self.flat:
            for j in (1, 2, 3):
                self.copy(j - 1).wait_recv()
                for k in range(3):
                    self.copy(3 + 3 * (4 - j) + k).start()

    def forward(self):
        for j in self.pieces():
            self.copy(3 + 3 * j).wait_recv()
        self.copy(15).start()
        self.copy(17).start()
        for j in self.pieces():
            self.copy(4 + 3 * j).wait_recv()
        self.copy(16).start()
        self.copy(18).start()

    def across(self):
        self.copy(15).wait_recv()
        self.copy(16).wait_recv()
        self.copy(19).start()

    def last(self):
        for j in self.pieces():
            self.copy(5 + 3 * j).wait_recv()
        for k in (17, 18, 19):
            self.copy(k).wait_recv()

    def drain(self):
        if not self.flat:
            for k in range(3):
                self.copy(k).wait_send()
        for j in self.pieces():
            for k in range(3):
                self.copy(3 + 3 * j + k).wait_send()
        for k in range(15, 20):
            self.copy(k).wait_send()


class Scatter:
    def __init__(self, place, grad, buffers, sends, receives, w):
        self.place, self.grad, self.w = place, grad, w
        self.sends, self.receives = sends, receives
        self.r1, self.r2a, self.r2b, self.r3a, self.r3b, self.r4 = buffers

    def copy(self, k):
        place, r1 = self.place, self.r1
        row, col, core = place.row, place.col, place.core
        if k == 0:
            pair = (self.grad.at[:, :, :, 1 - core], r1, place.sibling)
        elif k == 1:
            pair = (r1.at[0:2, :, 1 - col], self.r2a, place.x)
        elif k == 2:
            pair = (r1.at[2:4, 1 - row], self.r2b, place.y)
        elif k == 3:
            pair = (r1.at[0:2, 1 - row, col], self.r3a, place.y)
        elif k == 4:
            pair = (r1.at[2:4, row, 1 - col], self.r3b, place.x)
        else:
            peer = place.along(k - 4)
            pair = (r1.at[peer[1], row, col], self.r4.at[k - 5], peer)
        return remote(
            pair[0], pair[1], self.sends.at[self.w, k], self.receives.at[self.w, k], pair[2]
        )

    def add(self, index, other):
        ref = self.r1
        ref[index] = (ref[index].astype(F32) + other.astype(F32)).astype(ref.dtype)

    def start(self):
        self.copy(0).start()

    def planes(self):
        core = self.place.core
        self.copy(0).wait_recv()

        def step(i, carry):
            t, y = i // 2, i % 2
            self.add((t, y), self.grad[t, y, :, core])
            return carry

        lax.fori_loop(0, 8, step, 0)
        self.copy(1).start()
        self.copy(2).start()

    def lines(self):
        col, row = self.place.col, self.place.row
        self.copy(1).wait_recv()
        for t in range(2):
            for y in range(2):
                self.add((t, y, col), self.r2a[t, y])
        self.copy(3).start()
        self.copy(2).wait_recv()
        for t in range(2):
            for x in range(2):
                self.add((2 + t, row, x), self.r2b[t, x])
        self.copy(4).start()

    def points(self):
        col, row = self.place.col, self.place.row
        self.copy(3).wait_recv()
        for t in range(2):
            self.add((t, row, col), self.r3a[t])
        self.copy(4).wait_recv()
        for t in range(2):
            self.add((2 + t, row, col), self.r3b[t])
        for k in (5, 6, 7):
            self.copy(k).start()

    def result(self):
        place = self.place
        for k in (5, 6, 7):
            self.copy(k).wait_recv()
        total = self.r1[place.z, place.row, place.col].astype(F32)
        for j in range(3):
            total = total + self.r4[j].astype(F32)
        return total

    def drain(self):
        for k in range(8):
            self.copy(k).wait_send()


def scatter_buffers(rows, cols, dtype):
    return [
        pltpu.VMEM((4, 2, 2, rows, cols), dtype),
        pltpu.VMEM((2, 2, rows, cols), dtype),
        pltpu.VMEM((2, 2, rows, cols), dtype),
        pltpu.VMEM((2, rows, cols), dtype),
        pltpu.VMEM((2, rows, cols), dtype),
        pltpu.VMEM((3, rows, cols), dtype),
    ]


HEAD_SET = 3
SPAN = 3 * HD
CUT = HEAD_SET * SPAN
TILE_ROWS, TILE_COLS = 16, 256


def whole(value):
    return value.reshape(-1, value.shape[-1])


def gelu_parts(values):
    cumulative = 0.5 * (1.0 + lax.erf(values * 0.7071067811865476))
    density = 0.3989422804014327 * jnp.exp(-0.5 * values * values)
    return values * cumulative, cumulative + values * density


class Halo:
    def __init__(self, place, window, own, semaphores):
        edge = HALO + own
        self.place, self.window, self.edge = place, window, edge
        self.down = remote(
            window.at[pl.ds(HALO, HALO)],
            window.at[pl.ds(edge, HALO)],
            semaphores.at[0],
            semaphores.at[1],
            place.along(3),
        )
        self.up = remote(
            window.at[pl.ds(own, HALO)],
            window.at[pl.ds(0, HALO)],
            semaphores.at[2],
            semaphores.at[3],
            place.along(1),
        )

    def start(self):
        z, window = self.place.z, self.window
        blank = jnp.zeros((HALO, window.shape[1]), window.dtype)

        @pl.when(z > 0)
        def _():
            self.down.start()

        @pl.when(z < 3)
        def _():
            self.up.start()

        @pl.when(z == 0)
        def _():
            window[0:HALO] = blank

        @pl.when(z == 3)
        def _():
            window[self.edge : self.edge + HALO] = blank

    def wait(self):
        z = self.place.z

        @pl.when(z < 3)
        def _():
            self.down.wait_recv()

        @pl.when(z > 0)
        def _():
            self.up.wait_recv()

    def drain(self):
        z = self.place.z

        @pl.when(z > 0)
        def _():
            self.down.wait_send()

        @pl.when(z < 3)
        def _():
            self.up.wait_send()


def loader(inputs, places, semaphores):
    return [
        pltpu.make_async_copy(source, target, semaphores.at[n])
        for n, (source, target) in enumerate(zip(inputs, places))
    ]


def step_kernel(*refs):
    inputs, outputs, held = refs[:12], refs[12:22], refs[22:34]
    (
        tokens,
        segments,
        mask_grad,
        gain_one,
        attend_weight,
        output_weight,
        gain_two,
        up_weight,
        down_weight,
        patch_weight,
        class_weight,
        class_embed,
    ) = held
    results = refs[34:44]
    (
        masks,
        d_resid,
        share_p,
        share_d,
        share_u,
        share_a,
        share_n,
        class_all,
        class_row,
        class_sum,
    ) = results
    (
        full_a,
        full_u,
        full_d,
        full_p,
        full_c,
        full_e,
        grad_d,
        grad_u,
        grad_p,
        grad_n,
        grad_c,
        joint,
        attended,
        resid_one,
        norm_two,
        hidden,
        slope,
        total,
        window,
        norm_one,
        embed,
        embed_wide,
        resid_low,
        unit_low,
        class_low,
        probs,
        stack,
        seg_wide,
        seg_col,
        seg_row,
        class_wide,
        r4_a,
    ) = refs[44:76]
    buffers = refs[76:106]
    (
        gather_sends,
        gather_receives,
        scatter_sends,
        scatter_receives,
        line_sems,
        halo_sems,
        in_sems,
        out_sems,
    ) = refs[106:]
    loads = loader(inputs, held, in_sems)
    stores = loader(results, outputs, out_sems)
    for n in (11, 3, 6, 0, 4, 5, 10, 7, 8, 9, 1, 2):
        loads[n].start()

    place = Place()
    z, row, col, core = place.z, place.row, place.col, place.core
    own, width = tokens.shape
    span = own + 2 * HALO
    piece = width // 8
    narrow = patch_weight.shape[1]
    classes = class_embed.shape[0]
    mine = slice(HALO, HALO + own)
    ge, ga, gc, gu, gd, gp, gs = (
        Gather(place, full, gather_sends, gather_receives, w)
        for w, full in enumerate((full_e, full_a, full_c, full_u, full_d, full_p, class_sum))
    )
    sp, sd, su, sn, sc = (
        Scatter(place, g, buffers[6 * w : 6 * w + 6], scatter_sends, scatter_receives, w)
        for w, g in enumerate((grad_p, grad_d, grad_u, grad_n, grad_c))
    )
    grad_a = full_u
    parts = (slice(0, piece // 2), slice(piece // 2, piece))
    sa = [
        Scatter(
            place,
            grad_a.at[:, :, :, :, part],
            (
                full_d.at[:, :, :, 0, part],
                full_d.at[0:2, :, 0, 1, part],
                full_d.at[2:4, :, 0, 1, part],
                full_d.at[0:2, 0, 1, 1, part],
                full_d.at[2:4, 0, 1, 1, part],
                r4_a.at[:, part],
            ),
            scatter_sends,
            scatter_receives,
            5 + n,
        )
        for n, part in enumerate(parts)
    ]
    line_row = Line(place, class_row, line_sems.at[0], line_sems.at[1])
    line_all = Line(place, class_all, line_sems.at[2], line_sems.at[3])

    embed_wide[...] = jnp.zeros_like(embed_wide)
    for n in (11, 3, 6):
        loads[n].wait()
    embed_wide[0:classes] = class_embed[...]
    embed_wide[classes : classes + 1] = gain_one[...]
    embed_wide[classes + 1 : classes + 2] = gain_two[...]
    full_e[row, col, core] = embed_wide[...].astype(BF)
    greet(place)
    ge.start()
    loads[0].wait()
    window[mine] = tokens[...]
    halo = Halo(place, window, own, halo_sems.at[0])
    halo.start()
    loads[4].wait()
    loads[5].wait()
    full_a[z, row, col, core, :, 0:CUT] = attend_weight[...].astype(BF)
    full_a[z, row, col, core, :, CUT:] = output_weight[...].T.astype(BF)
    ga.start()
    loads[10].wait()
    full_c[row, col, core] = class_weight[...].astype(BF)
    gc.start()
    loads[7].wait()
    full_u[z, row, col, core] = up_weight[...].astype(BF)
    gu.start()
    loads[8].wait()
    loads[9].wait()
    full_d[z, row, col, core] = down_weight[...].astype(BF)
    full_p[z, row, col, core] = patch_weight[...].astype(BF)

    loads[1].wait()
    loads[2].wait()
    seg_wide[...] = jnp.full_like(seg_wide, -1.0)
    seg_wide[:, HALO : HALO + segments.shape[1]] = segments[...].astype(F32)
    seg_row[...] = seg_wide[:, pl.ds(pl.multiple_of(z * own, 128), span)]
    seg_col[...] = jnp.broadcast_to(seg_row[...], (8, span)).T[:, 0:1]

    ge.forward()
    ge.across()
    ga.spread()
    ge.last()
    gd.start()
    gc.forward()
    halo.wait()
    for d in range(8):
        embed[:, d * piece : (d + 1) * piece] = full_e[d // 4, (d // 2) % 2, d % 2]
    gains = embed[classes : classes + 2, :].astype(F32)
    gain_first, gain_second = gains[0:1], gains[1:2]

    def first_norm(i, carry):
        rows = pl.ds(pl.multiple_of(i * 128, 128), 128)
        xhat, _ = norm_parts(window[rows].astype(F32))
        norm_one[rows] = (xhat * gain_first).astype(BF)
        return carry

    lax.fori_loop(0, span // 128, first_norm, 0)
    gu.spread()
    ga.forward()
    gc.across()
    ga.across()
    gc.last()
    gd.spread()
    gp.start()
    class_all[z] = dot(embed[...], whole(full_c[...])).astype(BF)
    line_all.start()
    ga.last()

    def project(t, carry):
        joint[t] = dot(norm_one[...], whole(full_a[t])[:, :CUT]).astype(BF)
        return carry

    lax.fori_loop(0, 4, project, 0)
    gu.forward()

    probs[...] = jnp.zeros_like(probs)

    def attend(t, carry):
        for h in range(HEAD_SET):
            q_cols = slice(h * SPAN, h * SPAN + HD)
            k_cols = slice(h * SPAN + HD, h * SPAN + 2 * HD)
            v_cols = slice(h * SPAN + 2 * HD, h * SPAN + 3 * HD)
            for b in range(4):
                rows = slice(b * 128, (b + 1) * 128)
                near = slice(max(b - 1, 0) * 128, min(b + 2, 4) * 128)
                scores = dot(joint[t, rows, q_cols], joint[t, near, k_cols], ((1,), (1,)))
                match = seg_col[rows] == seg_row[:, near]
                scores = jnp.where(match, scores * HD**-0.5, masked_score)
                exponent = jnp.exp(scores - jnp.max(scores, axis=-1, keepdims=True))
                row_total = jnp.sum(exponent, axis=-1, keepdims=True)
                prob = (exponent / row_total).astype(BF)
                probs[t, h, rows, near] = prob
                if b in (1, 2):
                    attended[t, (b - 1) * 128 : b * 128, h * HD : (h + 1) * HD] = dot(
                        prob, joint[t, near, v_cols]
                    ).astype(BF)

        @pl.when(t == 1)
        def _():
            gp.spread()
            gu.across()

        return carry

    lax.fori_loop(0, 4, attend, 0)
    gd.forward()
    resid_one[...] = tokens[...].astype(F32)

    def output(t, carry):
        resid_one[...] += dot(attended[t], whole(full_a[t])[:, CUT:], ((1,), (1,)))
        return carry

    lax.fori_loop(0, 4, output, 0)
    xhat, _ = norm_parts(resid_one[...])
    norm_two[...] = (xhat * gain_second).astype(BF)
    line_all.wait()
    stores[7].start()
    class_square = jnp.zeros((class_all.shape[1], 1), F32)
    for t in range(4):
        value = class_all[t].astype(F32)
        class_square += jnp.sum(value * value, axis=-1, keepdims=True)
    class_inverse = lax.rsqrt(class_square + epsilon_unit)
    for t in range(4):
        class_low[t] = (class_all[t].astype(F32) * class_inverse).astype(BF)
    gu.last()
    gp.forward()

    def expand(t, carry):
        value, derivative = gelu_parts(dot(norm_two[...], whole(full_u[t])))
        hidden[t] = value.astype(BF)
        slope[t] = derivative.astype(BF)
        return carry

    lax.fori_loop(0, 4, expand, 0)
    gd.across()
    gp.across()
    gd.last()
    total[...] = resid_one[...]

    def contract(t, carry):
        total[...] += dot(hidden[t], whole(full_d[t]), ((1,), (1,)))
        return carry

    lax.fori_loop(0, 4, contract, 0)
    resid_low[...] = total[...].astype(BF)
    gp.last()

    square = jnp.zeros((own, 1), F32)
    pieces = []
    for t in range(4):
        value = dot(resid_low[...], whole(full_p[t]))
        square += jnp.sum(value * value, axis=-1, keepdims=True)
        pieces.append(value)
    inverse = lax.rsqrt(square + epsilon_unit)
    products = jnp.zeros((class_low.shape[1], own), F32)
    for t in range(4):
        pieces[t] = pieces[t] * inverse
        unit_low[t] = pieces[t].astype(BF)
        products += dot(class_low[t], unit_low[t], ((1,), (1,)))
    products = products[:classes]
    centred = products - jnp.mean(products, axis=0, keepdims=True)
    spread = jnp.mean(centred * centred, axis=0, keepdims=True)
    mask_inverse = lax.rsqrt(spread + epsilon_norm)
    centred = centred * mask_inverse
    masks[...] = centred
    stores[0].start()
    d_masks = mask_grad[...]
    d_products = mask_inverse * (
        d_masks
        - jnp.mean(d_masks, axis=0, keepdims=True)
        - centred * jnp.mean(d_masks * centred, axis=0, keepdims=True)
    )
    d_products = d_products.astype(BF)
    along = jnp.zeros((own, 1), F32)
    d_pieces = []
    for t in range(4):
        value = dot(d_products, class_low[t, :classes], ((0,), (0,)))
        along += jnp.sum(value * pieces[t], axis=-1, keepdims=True)
        d_pieces.append(value)
    flipped = resid_low[...].T
    for t in range(4):
        d_pieces[t] = (inverse * (d_pieces[t] - pieces[t] * along)).astype(BF)
        grad_p[t] = dot(flipped, d_pieces[t]).astype(BF).reshape(grad_p.shape[1:])
    sp.start()
    d_total = jnp.zeros((own, width), F32)
    for t in range(4):
        d_total += dot(d_pieces[t], whole(full_p[t]), ((1,), (1,)))
    d_resid[...] = d_total
    branch = d_total.astype(BF)
    flipped = branch.T
    sp.planes()

    def down(t, carry):
        grad_d[t] = dot(flipped, hidden[t]).astype(BF).reshape(grad_d.shape[1:])
        return carry

    lax.fori_loop(0, 4, down, 0)
    sd.start()
    class_row[z] = class_weight[...].astype(BF)
    line_row.start()
    flipped = norm_two[...].T

    def up(t, carry):
        back = dot(branch, whole(full_d[t])) * slope[t].astype(F32)
        back = back.astype(BF)
        slope[t] = back
        grad_u[t] = dot(flipped, back).astype(BF).reshape(grad_u.shape[1:])

        @pl.when(t == 1)
        def _():
            sd.planes()

        return carry

    lax.fori_loop(0, 4, up, 0)
    for transfer in (ge, ga, gc, gu, gd, gp):
        transfer.drain()
    su.start()
    total[...] = jnp.zeros_like(total)

    def narrow_back(t, carry):
        total[...] += dot(slope[t], whole(full_u[t]), ((1,), (1,)))
        return carry

    lax.fori_loop(0, 4, narrow_back, 0)
    su.planes()
    xhat, inverse = norm_parts(resid_one[...])
    gain_two_sum = jnp.sum(total[...] * xhat, axis=0, keepdims=True)
    d_resid[...] += norm_back(total[...] * gain_second, xhat, inverse)
    halo.drain()
    window[mine] = d_resid[...].astype(BF)
    back_halo = Halo(place, window, own, halo_sems.at[1])
    back_halo.start()
    sp.lines()
    class_wide[...] = jnp.zeros_like(class_wide)
    for t in range(4):
        class_wide[0:classes, t * narrow : (t + 1) * narrow] = dot(d_products, unit_low[t])
    grad_c[...] = jnp.zeros_like(grad_c)
    tiles = width // TILE_COLS
    for i in range(class_wide.shape[0] // TILE_ROWS * tiles):
        r, q = i // tiles, i % tiles
        grad_c[i // 8, (i // 4) % 2, (i // 2) % 2, i % 2] = class_wide[
            r * TILE_ROWS : (r + 1) * TILE_ROWS, q * TILE_COLS : (q + 1) * TILE_COLS
        ].astype(BF)
    sc.start()
    flipped = window[mine].T

    def outer(t, carry):
        block = dot(flipped, attended[t]).astype(BF)
        grad_a[t, :, :, :, :, CUT:] = block.reshape((2, 2, 2, piece, width - CUT))
        return carry

    lax.fori_loop(0, 4, outer, 0)
    sc.planes()
    back_halo.wait()

    def attended_back(t, carry):
        value = dot(window[...], whole(full_a[t])[:, CUT:]).astype(BF)
        slope[t, :, 0:narrow] = value[0:own]
        slope[t, :, 256 : 256 + narrow] = value[own:span]
        return carry

    lax.fori_loop(0, 4, attended_back, 0)
    sd.lines()
    line_row.wait()
    stores[8].start()
    stack[...] = jnp.zeros_like(stack)

    def attend_back(t, carry):
        for h in range(HEAD_SET):
            q_cols = slice(h * SPAN, h * SPAN + HD)
            k_cols = slice(h * SPAN + HD, h * SPAN + 2 * HD)
            v_cols = slice(h * SPAN + 2 * HD, h * SPAN + 3 * HD)
            for b in range(4):
                rows = slice(b * 128, (b + 1) * 128)
                low_key, high_key = max(b - 1, 0) * 128, min(b + 2, 4) * 128
                near = slice(low_key, high_key)
                prob = probs[t, h, rows, near].astype(F32)
                d_cols = slice(b // 2 * 256 + h * HD, b // 2 * 256 + (h + 1) * HD)
                d_rows = slice(b % 2 * 128, (b % 2 + 1) * 128)
                d_prob = dot(slope[t, d_rows, d_cols], joint[t, near, v_cols], ((1,), (1,)))
                delta = jnp.sum(prob * d_prob, axis=-1, keepdims=True)
                d_scores = (prob * (d_prob - delta)).astype(BF)
                first, last = max(low_key, HALO), min(high_key, HALO + own)
                stack[rows, first - HALO : last - HALO] = d_scores[
                    :, first - low_key : last - low_key
                ]
                if b in (1, 2):
                    hidden[t, (b - 1) * 128 : b * 128, q_cols] = (
                        dot(d_scores, joint[t, near, k_cols]) * HD**-0.5
                    ).astype(BF)
            hidden[t, :, k_cols] = (
                dot(stack[...], joint[t, :, q_cols], ((0,), (0,))) * HD**-0.5
            ).astype(BF)
            d_value = jnp.zeros((own, HD), F32)
            for half in range(2):
                d_value += dot(
                    probs[t, h, half * own : (half + 1) * own, mine],
                    slope[t, :, half * 256 + h * HD : half * 256 + (h + 1) * HD],
                    ((0,), (0,)),
                )
            hidden[t, :, v_cols] = d_value.astype(BF)

        @pl.when(t == 0)
        def _():
            sp.points()
            sc.lines()

        @pl.when(t == 2)
        def _():
            su.lines()
            sc.points()

        return carry

    lax.fori_loop(0, 4, attend_back, 0)
    flipped = norm_one[mine].T

    def attend_grad(t, carry):
        block = dot(flipped, hidden[t, :, :CUT]).astype(BF)
        grad_a[t, :, :, :, :, :CUT] = block.reshape((2, 2, 2, piece, CUT))
        return carry

    lax.fori_loop(0, 4, attend_grad, 0)
    for chunk in sa:
        chunk.start()
    sd.points()
    class_sum[z, row, col, core] = sc.result().astype(BF)
    gs.start()
    for chunk in sa:
        chunk.planes()
    gs.spread()
    total[...] = jnp.zeros_like(total)

    def joint_back(t, carry):
        total[...] += dot(hidden[t, :, :CUT], whole(full_a[t])[:, :CUT], ((1,), (1,)))
        return carry

    lax.fori_loop(0, 4, joint_back, 0)
    su.points()
    gs.forward()
    xhat, inverse = norm_parts(tokens[...].astype(F32))
    gain_one_sum = jnp.sum(total[...] * xhat, axis=0, keepdims=True)
    d_resid[...] += norm_back(total[...] * gain_first, xhat, inverse)
    stores[1].start()
    grad_n[...] = jnp.zeros_like(grad_n)
    for d in range(8):
        cols = slice(d * piece, (d + 1) * piece)
        for t in range(4):
            spot = (t, d // 4, (d // 2) % 2, d % 2)
            grad_n[spot + (slice(0, 1), slice(0, piece))] = gain_one_sum[:, cols]
            grad_n[spot + (slice(1, 2), slice(0, piece))] = gain_two_sum[:, cols]
    sn.start()
    sn.planes()
    sa[0].lines()
    share_p[...] = sp.result()
    stores[2].start()
    gs.across()
    sn.lines()
    sa[1].lines()
    share_d[...] = sd.result()
    stores[3].start()
    gs.last()
    stores[9].start()
    sa[0].points()
    sn.points()
    share_u[...] = su.result()
    stores[4].start()
    sa[1].points()
    share_n[...] = sn.result()
    stores[6].start()
    for chunk, part in zip(sa, parts):
        share_a[part] = chunk.result()
    stores[5].start()
    for transfer in (gs, sp, sd, su, sn, sc, *sa, line_row, line_all, back_halo):
        transfer.drain()
    for store in stores:
        store.wait()


def vmem_specs(count):
    return [pl.BlockSpec(memory_space=pltpu.VMEM)] * count


def any_specs(count):
    return [pl.BlockSpec(memory_space=pl.ANY)] * count


def step_call(tokens, segments, mask_grad, params):
    own, width = tokens.shape
    gain_one, attend, output, gain_two, up, down, patch, classed, embed = params
    classes = embed.shape[0]
    rows_e = -(-(classes + 2) // 32) * 32
    piece, high, narrow = up.shape[0], up.shape[1], patch.shape[1]
    span = own + 2 * HALO
    low = lambda *shape: pltpu.VMEM(shape, BF)
    wide = lambda *shape: pltpu.VMEM(shape, F32)
    shape = jax.ShapeDtypeStruct
    operands = (tokens, segments, mask_grad, gain_one[None], attend, output, gain_two[None])
    operands += tuple(params[4:])
    outs = [
        shape((classes, own), F32),
        shape((own, width), F32),
        shape((piece, narrow), F32),
        shape((piece, high), F32),
        shape((piece, high), F32),
        shape((piece, width), F32),
        shape((8, 128), F32),
        shape((4, rows_e, narrow), BF),
        shape((4, piece, narrow), BF),
        shape((4, 2, 2, 2, TILE_ROWS, TILE_COLS), BF),
    ]
    scratch = [pltpu.VMEM(v.shape, v.dtype) for v in operands]
    scratch += [pltpu.VMEM(v.shape, v.dtype) for v in outs]
    scratch += [
        low(4, 2, 2, 2, piece, width),
        low(4, 2, 2, 2, piece, high),
        low(4, 2, 2, 2, piece, high),
        low(4, 2, 2, 2, piece, narrow),
        low(2, 2, 2, piece, narrow),
        low(2, 2, 2, rows_e, piece),
        low(4, 2, 2, 2, piece, high),
        low(4, 2, 2, 2, piece, high),
        low(4, 2, 2, 2, piece, narrow),
        wide(4, 2, 2, 2, 8, 128),
        low(4, 2, 2, 2, TILE_ROWS, TILE_COLS),
        low(4, span, CUT),
        low(4, own, narrow),
        wide(own, width),
        low(own, width),
        low(4, own, high),
        low(4, own, high),
        wide(own, width),
        low(span, width),
        low(span, width),
        low(rows_e, width),
        wide(rows_e, piece),
        low(own, width),
        low(4, own, narrow),
        low(4, rows_e, narrow),
        low(4, HEAD_SET, span, span),
        low(span, own),
        wide(1, segments.shape[1] + 2 * HALO),
        wide(span, 1),
        wide(1, span),
        wide(rows_e, width),
        low(3, piece, width),
    ]
    for rows, cols, dtype in (
        (piece, narrow, BF),
        (piece, high, BF),
        (piece, high, BF),
        (8, 128, F32),
        (TILE_ROWS, TILE_COLS, BF),
    ):
        scratch += scatter_buffers(rows, cols, dtype)
    scratch += [
        pltpu.SemaphoreType.DMA((7, 20)),
        pltpu.SemaphoreType.DMA((7, 20)),
        pltpu.SemaphoreType.DMA((7, 8)),
        pltpu.SemaphoreType.DMA((7, 8)),
        pltpu.SemaphoreType.DMA((4, 3)),
        pltpu.SemaphoreType.DMA((2, 4)),
        pltpu.SemaphoreType.DMA((len(operands),)),
        pltpu.SemaphoreType.DMA((len(outs),)),
    ]
    return pl.pallas_call(
        step_kernel,
        out_shape=outs,
        in_specs=any_specs(len(operands)),
        out_specs=any_specs(len(outs)),
        scratch_shapes=scratch,
        compiler_params=pltpu.CompilerParams(
            collective_id=0, has_side_effects=True, vmem_limit_bytes=VMEM_LIMIT
        ),
    )(*operands)


def update_kernel(*refs):
    inputs, outputs, held = refs[:37], refs[37:57], refs[57:94]
    class_back, sum_wide, in_sems, out_sems = refs[94:]
    masks, token_grad, share_p, share_d, share_u, share_a, share_n = held[:7]
    class_all, class_row, class_sum = held[7:10]
    params, means, squares = held[10:19], held[19:28], held[28:37]
    loads = loader(inputs, held, in_sems)
    stores = loader(held[:2] + squares + means, outputs, out_sems)
    order = (0, 3, 6, 4, 5, 2, 1, 8, 7)
    for n in (6, 0, 1, 2, 4, 3, 5, 7, 8, 9):
        loads[n].start()
    for n in order:
        for k in (10, 19, 28):
            loads[k + n].start()
    for n in range(10):
        loads[n].wait()
        if n < 2:
            stores[n].start()

    def update(n, gradient):
        scale = block_scale if n < 6 else 1.0
        decay = 0.0 if n in (0, 3) else weight_decay
        for k in (10, 19, 28):
            if k + n != 18:
                loads[k + n].wait()
        squares[n][...], means[n][...] = adamw_update(
            params[n][...], gradient, means[n][...], squares[n][...], scale, decay
        )
        stores[2 + n].start()
        stores[11 + n].start()

    piece = share_p.shape[0]
    update(0, share_n[0:1, 0:piece])
    update(3, share_n[1:2, 0:piece])
    update(6, share_p[...])
    update(4, share_u[...])
    update(5, share_d[...])
    update(2, share_a[:, CUT:].T)
    update(1, share_a[:, :CUT])

    classes = params[8].shape[0]
    narrow = class_all.shape[2]
    tiles = sum_wide.shape[1] // TILE_COLS
    for i in range(sum_wide.shape[0] // TILE_ROWS * tiles):
        r, q = i // tiles, i % tiles
        sum_wide[
            r * TILE_ROWS : (r + 1) * TILE_ROWS, q * TILE_COLS : (q + 1) * TILE_COLS
        ] = class_sum[i // 8, (i // 4) % 2, (i // 2) % 2, i % 2].astype(F32)
    square = jnp.zeros((classes, 1), F32)
    for t in range(4):
        value = class_all[t, :classes].astype(F32)
        square += jnp.sum(value * value, axis=-1, keepdims=True)
    inverse = lax.rsqrt(square + epsilon_unit)
    along = jnp.zeros((classes, 1), F32)
    for t in range(4):
        unit = class_all[t, :classes].astype(F32) * inverse
        d_unit = sum_wide[:classes, t * narrow : (t + 1) * narrow]
        along += jnp.sum(unit * d_unit, axis=-1, keepdims=True)
    share_embed = jnp.zeros((classes, piece), F32)
    loads[18].wait()
    embed_low = params[8][...].astype(BF)
    for t in range(4):
        unit = class_all[t, :classes].astype(F32) * inverse
        d_unit = sum_wide[:classes, t * narrow : (t + 1) * narrow]
        value = (inverse * (d_unit - unit * along)).astype(BF)
        class_back[t] = value
        share_embed += dot(value, class_row[t], ((1,), (1,)))
    update(8, share_embed)
    update(7, dot(embed_low, class_back[lax.axis_index("tensor")], ((0,), (0,))))
    for store in stores:
        store.wait()


def update_call(results, params, means, squares):
    flat = lambda arrays: [a[None] if a.ndim == 1 else a for a in arrays]
    params, means, squares = flat(params), flat(means), flat(squares)
    classes, narrow = params[8].shape[0], params[7].shape[1]
    rows_e, width = results[7].shape[1], results[1].shape[1]
    operands = (*results, *params, *means, *squares)
    shape = jax.ShapeDtypeStruct
    outs = [shape(r.shape, F32) for r in results[:2]]
    outs += [shape(p.shape, F32) for p in params] * 2
    return pl.pallas_call(
        update_kernel,
        out_shape=outs,
        in_specs=any_specs(len(operands)),
        out_specs=any_specs(len(outs)),
        scratch_shapes=[pltpu.VMEM(v.shape, v.dtype) for v in operands]
        + [
            pltpu.VMEM((4, classes, narrow), BF),
            pltpu.VMEM((rows_e, width), F32),
            pltpu.SemaphoreType.DMA((len(operands),)),
            pltpu.SemaphoreType.DMA((len(outs),)),
        ],
        compiler_params=pltpu.CompilerParams(vmem_limit_bytes=VMEM_LIMIT),
    )(*operands)


def finish(masks, token_grad, grads, params, means, squares):
    scales = (block_scale,) * 6 + (1.0,) * 3
    decays = (0.0, weight_decay, weight_decay, 0.0) + (weight_decay,) * 5
    new = [adamw_update(*v) for v in zip(params, grads, means, squares, scales, decays)]
    return (masks, token_grad) + tuple(n[0] for n in new) + tuple(n[1] for n in new)


def gather_plain(shards, embed):
    def full(s):
        return lax.all_gather(lax.all_gather(s, "dp", axis=0), "tensor", axis=0)

    return [full(s) for s in shards] + [lax.all_gather(embed, "dp", axis=0)]


def scatter_plain(grads):
    def share(g):
        part = lax.psum_scatter(g, "dp", scatter_dimension=1, tiled=True)
        return lax.psum_scatter(part, "tensor", scatter_dimension=0, tiled=True)[0]

    return [share(g).astype(F32) for g in grads]


def with_halo(rows, parts):
    forward = [(i, i + 1) for i in range(parts - 1)]
    backward = [(i + 1, i) for i in range(parts - 1)]
    before = lax.ppermute(rows[-HALO:], "tensor", forward)
    after = lax.ppermute(rows[:HALO], "tensor", backward)
    return jnp.concatenate((before, rows, after), axis=0)


def local_plain(
    parts,
    tokens,
    segments,
    mask_grad,
    gain_one,
    attend_weight,
    output_weight,
    gain_two,
    up_weight,
    down_weight,
    patch_weight,
    class_weight,
    class_embed,
    *moments,
):
    means, squares = moments[:9], moments[9:]
    own = tokens.shape[0]
    width = tokens.shape[1]
    classes = class_embed.shape[0]
    dp_index = lax.axis_index("dp")
    tensor_index = lax.axis_index("tensor")
    low = lambda v: v.astype(BF)

    shard_a = jnp.concatenate((low(attend_weight), low(output_weight).T), axis=1)
    shard_u = low(up_weight)
    shard_d = low(down_weight).T
    shard_p = jnp.concatenate((low(patch_weight), low(class_weight)), axis=1)
    rows_e = -(-(classes + 2) // 32) * 32
    shard_e = jnp.zeros((rows_e, class_embed.shape[1]), BF)
    shard_e = shard_e.at[:classes].set(low(class_embed))
    shard_e = shard_e.at[classes].set(low(gain_one)).at[classes + 1].set(low(gain_two))
    full_a, full_u, full_d, full_p, full_e = gather_plain(
        (shard_a, shard_u, shard_d, shard_p), shard_e
    )
    full_a, full_u, full_d, full_p = (
        v.reshape(v.shape[0], width, v.shape[-1]) for v in (full_a, full_u, full_d, full_p)
    )
    embed_rows = full_e.transpose(1, 0, 2).reshape(rows_e, width)
    embed = embed_rows[:classes]
    gain_first = embed_rows[classes].astype(F32)[None]
    gain_second = embed_rows[classes + 1].astype(F32)[None]

    cut = attend_weight.shape[1]
    heads = cut // (3 * HD)
    w_attend, w_output = full_a[:, :, :cut], full_a[:, :, cut:]
    narrow = patch_weight.shape[1]
    w_patch, w_class = full_p[:, :, :narrow], full_p[:, :, narrow:]
    w_patch = w_patch.transpose(1, 0, 2).reshape(width, -1)
    w_class = w_class.transpose(1, 0, 2).reshape(width, -1)

    window = with_halo(tokens, parts)
    token_wide = window.astype(F32)
    xhat_one, inverse_one = norm_parts(token_wide)
    norm_one = low(xhat_one * gain_first)
    joint = jnp.einsum("sd,tdn->stn", norm_one, w_attend, preferred_element_type=F32)
    joint = low(joint).reshape(own + 2 * HALO, parts * heads, 3, HD)
    queries, keys, values = joint[:, :, 0], joint[:, :, 1], joint[:, :, 2]
    padded = jnp.pad(segments[0], HALO, constant_values=-1)
    seg = lax.dynamic_slice_in_dim(padded, tensor_index * own, own + 2 * HALO, 0)
    scores = jnp.einsum("qhd,khd->hqk", queries, keys, preferred_element_type=F32) * HD**-0.5
    scores = jnp.where(seg[None, :, None] == seg[None, None, :], scores, masked_score)
    exponent = jnp.exp(scores - jnp.max(scores, axis=-1, keepdims=True))
    prob = exponent / jnp.sum(exponent, axis=-1, keepdims=True)
    prob_low = low(prob)
    mine = slice(HALO, HALO + own)
    attended = jnp.einsum(
        "hqk,khd->qhd", prob_low[:, mine], values, preferred_element_type=F32
    )
    attended = low(attended).reshape(own, parts, heads * HD)
    resid_one = token_wide[mine] + jnp.einsum(
        "stn,tdn->sd", attended, w_output, preferred_element_type=F32
    )
    xhat_two, inverse_two = norm_parts(resid_one)
    norm_two = low(xhat_two * gain_second)
    hidden_pre = jnp.einsum("sd,tdn->stn", norm_two, full_u, preferred_element_type=F32)
    hidden, gelu_back = jax.vjp(lambda v: jax.nn.gelu(v, approximate=False), hidden_pre)
    hidden = low(hidden)
    resid_two = resid_one + jnp.einsum(
        "stn,tdn->sd", hidden, full_d, preferred_element_type=F32
    )
    resid_low = low(resid_two)
    patch_feat = dot(resid_low, w_patch)
    patch_wide, patch_inverse = unit_parts(patch_feat)
    patch_unit = low(patch_wide)
    class_feat = dot(embed, w_class)
    class_wide, class_inverse = unit_parts(class_feat)
    class_unit = low(class_wide)
    products = dot(patch_unit, class_unit, ((1,), (1,)))
    masks, mask_inverse = norm_parts(products)
    d_products = low(norm_back(mask_grad, masks, mask_inverse))
    d_class_unit = lax.psum(dot(d_products, patch_unit, ((0,), (0,))), ("dp", "tensor"))
    d_patch_unit = dot(d_products, class_unit)
    d_patch_feat = low(unit_back(d_patch_unit, patch_wide, patch_inverse))
    grad_patch = dot(resid_low, d_patch_feat, ((0,), (0,)))
    d_resid_two = dot(d_patch_feat, w_patch, ((1,), (1,)))
    d_branch_two = low(d_resid_two)
    d_hidden = jnp.einsum("sd,tdn->stn", d_branch_two, full_d, preferred_element_type=F32)
    grad_down = jnp.einsum("sd,stn->tdn", d_branch_two, hidden, preferred_element_type=F32)
    d_hidden_pre = low(gelu_back(d_hidden)[0])
    grad_up = jnp.einsum("sd,stn->tdn", norm_two, d_hidden_pre, preferred_element_type=F32)
    d_norm_two = jnp.einsum("stn,tdn->sd", d_hidden_pre, full_u, preferred_element_type=F32)
    d_resid_one = d_resid_two + norm_back(d_norm_two * gain_second, xhat_two, inverse_two)
    grad_gain_two = jnp.sum(d_norm_two * xhat_two, axis=0)
    d_branch_one = with_halo(low(d_resid_one), parts)
    d_attended = low(
        jnp.einsum("sd,tdn->stn", d_branch_one, w_output, preferred_element_type=F32)
    )
    grad_output = jnp.einsum(
        "sd,stn->tdn", d_branch_one[mine], attended, preferred_element_type=F32
    )
    d_attended = d_attended.reshape(own + 2 * HALO, parts * heads, HD)
    d_prob = jnp.einsum("qhd,khd->hqk", d_attended, values, preferred_element_type=F32)
    delta = jnp.sum(prob * d_prob, axis=-1, keepdims=True)
    d_scores = low(prob * (d_prob - delta))
    d_query = jnp.einsum(
        "hqk,khd->qhd", d_scores[:, mine], keys, preferred_element_type=F32
    )
    d_key = jnp.einsum(
        "hqk,qhd->khd", d_scores[:, :, mine], queries, preferred_element_type=F32
    )
    d_value = jnp.einsum(
        "hqk,qhd->khd", prob_low[:, :, mine], d_attended, preferred_element_type=F32
    )
    d_joint = low(
        jnp.stack((d_query * HD**-0.5, d_key * HD**-0.5, d_value), axis=2)
    ).reshape(own, parts, cut)
    grad_attend = jnp.einsum(
        "sd,stn->tdn", norm_one[mine], d_joint, preferred_element_type=F32
    )
    d_norm_one = jnp.einsum("stn,tdn->sd", d_joint, w_attend, preferred_element_type=F32)
    token_grad = d_resid_one + norm_back(
        d_norm_one * gain_first, xhat_one[mine], inverse_one[mine]
    )
    grad_gain_one = jnp.sum(d_norm_one * xhat_one[mine], axis=0)

    grad_patch = grad_patch.reshape(width, parts, narrow).transpose(1, 0, 2)
    share_p, share_d, share_u, share_a = scatter_plain(
        [
            grad_patch,
            grad_down,
            grad_up,
            jnp.concatenate((grad_attend, grad_output), axis=2),
        ]
    )
    gains = lax.psum((grad_gain_one, grad_gain_two), ("dp", "tensor"))
    step = gain_one.shape[0]
    share_one, share_two = (lax.dynamic_slice_in_dim(g, dp_index * step, step, 0) for g in gains)
    d_class_feat = low(unit_back(d_class_unit, class_wide, class_inverse))
    d_class_own = lax.dynamic_slice_in_dim(d_class_feat, tensor_index * narrow, narrow, 1)
    share_class = dot(low(class_embed), d_class_own, ((0,), (0,)))
    class_rows = lax.dynamic_slice_in_dim(w_class, dp_index * step, step, 0)
    share_embed = dot(d_class_feat, class_rows, ((1,), (1,)))
    return finish(
        masks,
        token_grad,
        (
            share_one,
            share_a[:, :cut],
            share_a[:, cut:].T,
            share_two,
            share_u,
            share_d.T,
            share_p,
            share_class,
            share_embed,
        ),
        (
            gain_one,
            attend_weight,
            output_weight,
            gain_two,
            up_weight,
            down_weight,
            patch_weight,
            class_weight,
            class_embed,
        ),
        means,
        squares,
    )


def local_kernels(tokens, segments, mask_grad, *arrays):
    def turned(group):
        return (*group[:5], group[5].T, *group[6:])

    params, means, squares = (turned(arrays[n : n + 9]) for n in (0, 9, 18))
    results = step_call(tokens, segments, mask_grad.T, params)
    masks, token_grad, *new = update_call(results, params, means, squares)
    new = [n.reshape(p.shape) for n, p in zip(new, params * 2)]
    return (masks.T, token_grad, *turned(new[:9]), *turned(new[9:]))


def solution(mesh):
    parts = mesh.shape["tensor"]
    custom = mesh.shape["dp"] == 8 and parts == 4
    params = (
        P("dp"),
        P("dp", "tensor"),
        P("tensor", "dp"),
        P("dp"),
        P("dp", "tensor"),
        P("tensor", "dp"),
        P("dp", "tensor"),
        P("dp", "tensor"),
        P(None, "dp"),
    )
    rows = P(("dp", "tensor"), None)
    return jax.shard_map(
        local_kernels if custom else functools.partial(local_plain, parts),
        mesh=mesh,
        in_specs=(rows, P("dp", None), rows) + params * 3,
        out_specs=(rows, rows) + params * 2,
        check_vma=False,
    )
```

```python
import functools

import jax
import jax.numpy as jnp
from jax import lax
from jax.experimental import pallas as pl
from jax.experimental.pallas import tpu as pltpu
from jax.sharding import PartitionSpec as P

HD = 64
HALO = 128
BF = jnp.bfloat16
F32 = jnp.float32
MESH = pl.DeviceIdType.MESH
VMEM_LIMIT = 64 * 1024 * 1024 - 512 * 1024

epsilon_norm = 1e-05
epsilon_unit = 1e-06
masked_score = -1000000000.0
first_decay = 0.9
second_decay = 0.999
first_fix = 0.99997343860112
second_fix = 0.09520785288629
adam_epsilon = 1e-08
block_scale = 0.65
weight_decay = 0.05


def dot(left, right, dims=((1,), (0,))):
    return lax.dot_general(left, right, (dims, ((), ())), preferred_element_type=F32)


def layer_norm(values, gain):
    center = values - jnp.mean(values, axis=-1, keepdims=True)
    spread = jnp.mean(center * center, axis=-1, keepdims=True)
    return center * lax.rsqrt(spread + epsilon_norm) * gain


def norm_parts(values):
    center = values - jnp.mean(values, axis=-1, keepdims=True)
    spread = jnp.mean(center * center, axis=-1, keepdims=True)
    inverse = lax.rsqrt(spread + epsilon_norm)
    return center * inverse, inverse


def norm_back(gradient, xhat, inverse):
    return inverse * (
        gradient
        - jnp.mean(gradient, axis=-1, keepdims=True)
        - xhat * jnp.mean(gradient * xhat, axis=-1, keepdims=True)
    )


def unit_parts(values):
    inverse = lax.rsqrt(jnp.sum(values * values, axis=-1, keepdims=True) + epsilon_unit)
    return values * inverse, inverse


def unit_back(gradient, unit, inverse):
    return inverse * (gradient - unit * jnp.sum(unit * gradient, axis=-1, keepdims=True))


def adamw_update(current, gradient, mean_old, square_old, step_scale, decay_rate):
    mean_new = first_decay * mean_old + (1.0 - first_decay) * gradient
    square_new = second_decay * square_old + (1.0 - second_decay) * gradient * gradient
    moved = mean_new / first_fix / (jnp.sqrt(square_new / second_fix) + adam_epsilon)
    return (step_scale * (moved + decay_rate * current), mean_new)


class Place:
    def __init__(self):
        dp, z = lax.axis_index("dp"), lax.axis_index("tensor")
        self.dp, self.z = dp, z
        self.core, self.col, self.row = dp % 2, (dp // 2) % 2, dp // 4
        self.x = (dp + 2 * (1 - 2 * self.col), z)
        self.y = (dp + 4 * (1 - 2 * self.row), z)
        self.sibling = (dp + 1 - 2 * self.core, z)

    def along(self, j):
        return (self.dp, (self.z + j) % 4)


def greet(place):
    barrier = pltpu.get_barrier_semaphore()
    targets = [place.x, place.y, place.sibling] + [place.along(j) for j in (1, 2, 3)]
    for target in targets:
        pl.semaphore_signal(barrier, inc=1, device_id=target, device_id_type=MESH)
    pl.semaphore_wait(barrier, 6)


def remote(source, target_ref, sends, receives, device):
    return pltpu.make_async_remote_copy(
        src_ref=source,
        dst_ref=target_ref,
        send_sem=sends,
        recv_sem=receives,
        device_id=device,
        device_id_type=MESH,
    )


class Line:
    def __init__(self, place, full, sends, receives):
        self.copies = [
            remote(
                full.at[place.z], full.at[place.z], sends.at[k], receives.at[k], place.along(k + 1)
            )
            for k in range(3)
        ]

    def start(self):
        for copy in self.copies:
            copy.start()

    def wait(self):
        for copy in self.copies:
            copy.wait_recv()

    def drain(self):
        for copy in self.copies:
            copy.wait_send()


class Gather:
    def __init__(self, place, full, sends, receives, w):
        self.place, self.full, self.w = place, full, w
        self.sends, self.receives = sends, receives
        self.flat = len(full.shape) == 5

    def copy(self, k):
        place, full = self.place, self.full
        row, col, core, z = place.row, place.col, place.core, place.z
        if k < 3:
            view, target = full.at[z - k, row, col, core], place.along(1)
        elif k >= 20:
            view, target = full.at[z + k - 20, row, col, core], place.along(3)
        elif k < 15:
            j = (k - 3) // 3
            if self.flat:
                view = full.at[row, col, core]
            else:
                view = full.at[(z + j) % 4, row, col, core]
            target = (place.x, place.y, place.sibling)[(k - 3) % 3]
        elif k < 17:
            spot = (row, 1 - col, core) if k == 15 else (1 - row, col, core)
            if self.flat:
                half = full.shape[3] // 2
                view = full.at[spot + (pl.ds((k - 15) * half, half),)]
            else:
                view = full.at[(pl.ds((k - 15) * 2, 2),) + spot]
            target = place.y if k == 15 else place.x
        else:
            spot = ((row, 1 - col, core), (1 - row, col, core), (1 - row, 1 - col, core))[k - 17]
            view = full.at[spot] if self.flat else full.at[(slice(None),) + spot]
            target = place.sibling
        return remote(view, view, self.sends.at[self.w, k], self.receives.at[self.w, k], target)

    def pieces(self):
        return range(1 if self.flat else 4)

    def start(self):
        for k in (3, 4, 5):
            self.copy(k).start()

    def line(self):
        z = self.place.z

        @pl.when(z < 3)
        def _():
            self.copy(0).start()

        @pl.when(z > 0)
        def _():
            self.copy(20).start()

    def hop(self, h):
        z = self.place.z

        @pl.when(z >= h)
        def _():
            self.copy(h - 1).wait_recv()
            if h < 3:

                @pl.when(z < 3)
                def _():
                    self.copy(h).start()

            for k in range(3):
                self.copy(3 + 3 * (4 - h) + k).start()

        @pl.when(z + h <= 3)
        def _():
            self.copy(19 + h).wait_recv()
            if h < 3:

                @pl.when(z > 0)
                def _():
                    self.copy(20 + h).start()

            for k in range(3):
                self.copy(3 + 3 * h + k).start()

    def forward(self):
        for j in self.pieces():
            self.copy(3 + 3 * j).wait_recv()
        self.copy(15).start()
        self.copy(17).start()
        for j in self.pieces():
            self.copy(4 + 3 * j).wait_recv()
        self.copy(16).start()
        self.copy(18).start()

    def across(self):
        self.copy(15).wait_recv()
        self.copy(16).wait_recv()
        self.copy(19).start()

    def last(self):
        for j in self.pieces():
            self.copy(5 + 3 * j).wait_recv()
        for k in (17, 18, 19):
            self.copy(k).wait_recv()

    def drain(self):
        z = self.place.z
        if not self.flat:
            for k in range(3):

                @pl.when((z < 3) & (z >= k))
                def _(k=k):
                    self.copy(k).wait_send()

                @pl.when((z > 0) & (z + k <= 3))
                def _(k=k):
                    self.copy(20 + k).wait_send()

        for j in self.pieces():
            for k in range(3):
                self.copy(3 + 3 * j + k).wait_send()
        for k in range(15, 20):
            self.copy(k).wait_send()


class Scatter:
    def __init__(self, place, grad, buffers, sends, receives, w):
        self.place, self.grad, self.w = place, grad, w
        self.sends, self.receives = sends, receives
        self.r1, self.r2a, self.r2b, self.r3a, self.r3b, self.r4 = buffers

    def copy(self, k):
        place, r1 = self.place, self.r1
        row, col, core = place.row, place.col, place.core
        if k == 0:
            pair = (self.grad.at[:, :, :, 1 - core], r1, place.sibling)
        elif k == 1:
            pair = (r1.at[0:2, :, 1 - col], self.r2a, place.x)
        elif k == 2:
            pair = (r1.at[2:4, 1 - row], self.r2b, place.y)
        elif k == 3:
            pair = (r1.at[0:2, 1 - row, col], self.r3a, place.y)
        elif k == 4:
            pair = (r1.at[2:4, row, 1 - col], self.r3b, place.x)
        else:
            peer = place.along(k - 4)
            pair = (r1.at[peer[1], row, col], self.r4.at[k - 5], peer)
        return remote(
            pair[0], pair[1], self.sends.at[self.w, k], self.receives.at[self.w, k], pair[2]
        )

    def add(self, index, other):
        ref = self.r1
        ref[index] = (ref[index].astype(F32) + other.astype(F32)).astype(ref.dtype)

    def start(self):
        self.copy(0).start()

    def planes(self):
        core = self.place.core
        self.copy(0).wait_recv()

        def step(i, carry):
            t, y = i // 2, i % 2
            self.add((t, y), self.grad[t, y, :, core])
            return carry

        lax.fori_loop(0, 8, step, 0)

    def spread(self):
        self.copy(1).start()
        self.copy(2).start()

    def lines(self):
        col, row = self.place.col, self.place.row
        self.copy(1).wait_recv()
        for t in range(2):
            for y in range(2):
                self.add((t, y, col), self.r2a[t, y])
        self.copy(3).start()
        self.copy(2).wait_recv()
        for t in range(2):
            for x in range(2):
                self.add((2 + t, row, x), self.r2b[t, x])
        self.copy(4).start()

    def points(self):
        col, row = self.place.col, self.place.row
        self.copy(3).wait_recv()
        for t in range(2):
            self.add((t, row, col), self.r3a[t])
        self.copy(4).wait_recv()
        for t in range(2):
            self.add((2 + t, row, col), self.r3b[t])
        for k in (5, 6, 7):
            self.copy(k).start()

    def result(self):
        place = self.place
        for k in (5, 6, 7):
            self.copy(k).wait_recv()
        total = self.r1[place.z, place.row, place.col].astype(F32)
        for j in range(3):
            total = total + self.r4[j].astype(F32)
        return total

    def drain(self):
        for k in range(8):
            self.copy(k).wait_send()


def scatter_buffers(rows, cols, dtype):
    return [
        pltpu.VMEM((4, 2, 2, rows, cols), dtype),
        pltpu.VMEM((2, 2, rows, cols), dtype),
        pltpu.VMEM((2, 2, rows, cols), dtype),
        pltpu.VMEM((2, rows, cols), dtype),
        pltpu.VMEM((2, rows, cols), dtype),
        pltpu.VMEM((3, rows, cols), dtype),
    ]


HEAD_SET = 3
SPAN = 3 * HD
CUT = HEAD_SET * SPAN
TILE_ROWS, TILE_COLS = 16, 256


def whole(value):
    return value.reshape(-1, value.shape[-1])


def gelu_parts(values):
    cumulative = 0.5 * (1.0 + lax.erf(values * 0.7071067811865476))
    density = 0.3989422804014327 * jnp.exp(-0.5 * values * values)
    return values * cumulative, cumulative + values * density


class Halo:
    def __init__(self, place, window, own, semaphores):
        edge = HALO + own
        self.place, self.window, self.edge = place, window, edge
        self.down = remote(
            window.at[pl.ds(HALO, HALO)],
            window.at[pl.ds(edge, HALO)],
            semaphores.at[0],
            semaphores.at[1],
            place.along(3),
        )
        self.up = remote(
            window.at[pl.ds(own, HALO)],
            window.at[pl.ds(0, HALO)],
            semaphores.at[2],
            semaphores.at[3],
            place.along(1),
        )

    def start(self):
        z, window = self.place.z, self.window
        blank = jnp.zeros((HALO, window.shape[1]), window.dtype)

        @pl.when(z > 0)
        def _():
            self.down.start()

        @pl.when(z < 3)
        def _():
            self.up.start()

        @pl.when(z == 0)
        def _():
            window[0:HALO] = blank

        @pl.when(z == 3)
        def _():
            window[self.edge : self.edge + HALO] = blank

    def wait(self):
        z = self.place.z

        @pl.when(z < 3)
        def _():
            self.down.wait_recv()

        @pl.when(z > 0)
        def _():
            self.up.wait_recv()

    def drain(self):
        z = self.place.z

        @pl.when(z > 0)
        def _():
            self.down.wait_send()

        @pl.when(z < 3)
        def _():
            self.up.wait_send()


def loader(inputs, places, semaphores):
    return [
        pltpu.make_async_copy(source, target, semaphores.at[n])
        for n, (source, target) in enumerate(zip(inputs, places))
    ]


def step_kernel(*refs):
    inputs, outputs, held = refs[:12], refs[12:22], refs[22:34]
    (
        tokens,
        segments,
        mask_grad,
        gain_one,
        attend_weight,
        output_weight,
        gain_two,
        up_weight,
        down_weight,
        patch_weight,
        class_weight,
        class_embed,
    ) = held
    results = refs[34:44]
    (
        masks,
        d_resid,
        share_p,
        share_d,
        share_u,
        share_a,
        share_n,
        class_all,
        class_row,
        class_sum,
    ) = results
    (
        full_a,
        full_u,
        full_d,
        full_p,
        full_c,
        full_e,
        grad_d,
        grad_u,
        grad_p,
        grad_n,
        grad_c,
        joint,
        attended,
        resid_one,
        norm_two,
        hidden,
        slope,
        total,
        window,
        norm_one,
        embed,
        embed_wide,
        resid_low,
        unit_low,
        class_low,
        probs,
        stack,
        seg_wide,
        seg_col,
        seg_row,
        class_wide,
        r4_a,
    ) = refs[44:76]
    buffers = refs[76:106]
    (
        gather_sends,
        gather_receives,
        scatter_sends,
        scatter_receives,
        line_sems,
        halo_sems,
        in_sems,
        out_sems,
    ) = refs[106:]
    loads = loader(inputs, held, in_sems)
    stores = loader(results, outputs, out_sems)
    for n in (11, 3, 6, 0, 4, 5, 10, 7, 8, 9, 1, 2):
        loads[n].start()

    place = Place()
    z, row, col, core = place.z, place.row, place.col, place.core
    own, width = tokens.shape
    span = own + 2 * HALO
    piece = width // 8
    narrow = patch_weight.shape[1]
    classes = class_embed.shape[0]
    mine = slice(HALO, HALO + own)
    ge, ga, gc, gu, gd, gp, gs = (
        Gather(place, full, gather_sends, gather_receives, w)
        for w, full in enumerate((full_e, full_a, full_c, full_u, full_d, full_p, class_sum))
    )
    sp, sd, su, sn, sc = (
        Scatter(place, g, buffers[6 * w : 6 * w + 6], scatter_sends, scatter_receives, w)
        for w, g in enumerate((grad_p, grad_d, grad_u, grad_n, grad_c))
    )
    grad_a = full_u
    third = piece // 3
    parts = [slice(n * third, (n + 1) * third) for n in range(3)]
    sa = [
        Scatter(
            place,
            grad_a.at[:, :, :, :, part],
            (
                full_d.at[:, :, :, 0, part],
                full_d.at[0:2, :, 0, 1, part],
                full_d.at[2:4, :, 0, 1, part],
                full_d.at[0:2, 0, 1, 1, part],
                full_d.at[2:4, 0, 1, 1, part],
                r4_a.at[:, part],
            ),
            scatter_sends,
            scatter_receives,
            5 + n,
        )
        for n, part in enumerate(parts)
    ]
    line_row = Line(place, class_row, line_sems.at[0], line_sems.at[1])
    line_all = Line(place, class_all, line_sems.at[2], line_sems.at[3])

    embed_wide[...] = jnp.zeros_like(embed_wide)
    for n in (11, 3, 6):
        loads[n].wait()
    embed_wide[0:classes] = class_embed[...]
    embed_wide[classes : classes + 1] = gain_one[...]
    embed_wide[classes + 1 : classes + 2] = gain_two[...]
    full_e[row, col, core] = embed_wide[...].astype(BF)
    greet(place)
    ge.start()
    loads[0].wait()
    window[mine] = tokens[...]
    halo = Halo(place, window, own, halo_sems.at[0])
    halo.start()
    loads[4].wait()
    loads[5].wait()
    full_a[z, row, col, core, :, 0:CUT] = attend_weight[...].astype(BF)
    full_a[z, row, col, core, :, CUT:] = output_weight[...].T.astype(BF)
    ga.start()
    ga.line()
    loads[10].wait()
    full_c[row, col, core] = class_weight[...].astype(BF)
    gc.start()
    loads[7].wait()
    full_u[z, row, col, core] = up_weight[...].astype(BF)
    gu.start()
    gu.line()
    loads[8].wait()
    full_d[z, row, col, core] = down_weight[...].astype(BF)
    gd.start()
    loads[9].wait()
    full_p[z, row, col, core] = patch_weight[...].astype(BF)
    gp.start()
    ga.hop(1)

    loads[1].wait()
    loads[2].wait()
    seg_wide[...] = jnp.full_like(seg_wide, -1.0)
    seg_wide[:, HALO : HALO + segments.shape[1]] = segments[...].astype(F32)
    seg_row[...] = seg_wide[:, pl.ds(pl.multiple_of(z * own, 128), span)]
    seg_col[...] = jnp.broadcast_to(seg_row[...], (8, span)).T[:, 0:1]

    ge.forward()
    ga.hop(2)
    ge.across()
    ga.hop(3)
    gd.line()
    gu.hop(1)
    ge.last()
    gc.forward()
    halo.wait()
    for d in range(8):
        embed[:, d * piece : (d + 1) * piece] = full_e[d // 4, (d // 2) % 2, d % 2]
    gains = embed[classes : classes + 2, :].astype(F32)
    gain_first, gain_second = gains[0:1], gains[1:2]

    def first_norm(i, carry):
        rows = pl.ds(pl.multiple_of(i * 128, 128), 128)
        xhat, _ = norm_parts(window[rows].astype(F32))
        norm_one[rows] = (xhat * gain_first).astype(BF)
        return carry

    lax.fori_loop(0, span // 128, first_norm, 0)
    gu.hop(2)
    ga.forward()
    gc.across()
    gu.hop(3)
    gp.line()
    gd.hop(1)
    ga.across()
    gc.last()
    class_all[z] = dot(embed[...], whole(full_c[...])).astype(BF)
    line_all.start()
    gd.hop(2)
    ga.last()

    def project(t, carry):
        joint[t] = dot(norm_one[...], whole(full_a[t])[:, :CUT]).astype(BF)
        return carry

    lax.fori_loop(0, 4, project, 0)
    gd.hop(3)
    gp.hop(1)
    gu.forward()

    probs[...] = jnp.zeros_like(probs)

    def attend(t, carry):
        for h in range(HEAD_SET):
            q_cols = slice(h * SPAN, h * SPAN + HD)
            k_cols = slice(h * SPAN + HD, h * SPAN + 2 * HD)
            v_cols = slice(h * SPAN + 2 * HD, h * SPAN + 3 * HD)
            for b in range(4):
                rows = slice(b * 128, (b + 1) * 128)
                near = slice(max(b - 1, 0) * 128, min(b + 2, 4) * 128)
                scores = dot(joint[t, rows, q_cols], joint[t, near, k_cols], ((1,), (1,)))
                match = seg_col[rows] == seg_row[:, near]
                scores = jnp.where(match, scores * HD**-0.5, masked_score)
                exponent = jnp.exp(scores - jnp.max(scores, axis=-1, keepdims=True))
                row_total = jnp.sum(exponent, axis=-1, keepdims=True)
                prob = (exponent / row_total).astype(BF)
                probs[t, h, rows, near] = prob
                if b in (1, 2):
                    attended[t, (b - 1) * 128 : b * 128, h * HD : (h + 1) * HD] = dot(
                        prob, joint[t, near, v_cols]
                    ).astype(BF)

        @pl.when(t == 0)
        def _():
            gp.hop(2)

        @pl.when(t == 1)
        def _():
            gp.hop(3)
            gu.across()

        @pl.when(t == 2)
        def _():
            gd.forward()

        return carry

    lax.fori_loop(0, 4, attend, 0)
    resid_one[...] = tokens[...].astype(F32)

    def output(t, carry):
        resid_one[...] += dot(attended[t], whole(full_a[t])[:, CUT:], ((1,), (1,)))
        return carry

    lax.fori_loop(0, 4, output, 0)
    xhat, _ = norm_parts(resid_one[...])
    norm_two[...] = (xhat * gain_second).astype(BF)
    line_all.wait()
    stores[7].start()
    class_square = jnp.zeros((class_all.shape[1], 1), F32)
    for t in range(4):
        value = class_all[t].astype(F32)
        class_square += jnp.sum(value * value, axis=-1, keepdims=True)
    class_inverse = lax.rsqrt(class_square + epsilon_unit)
    for t in range(4):
        class_low[t] = (class_all[t].astype(F32) * class_inverse).astype(BF)
    gu.last()
    gp.forward()

    def expand(t, carry):
        value, derivative = gelu_parts(dot(norm_two[...], whole(full_u[t])))
        hidden[t] = value.astype(BF)
        slope[t] = derivative.astype(BF)
        return carry

    lax.fori_loop(0, 4, expand, 0)
    gd.across()
    gp.across()
    gd.last()
    total[...] = resid_one[...]

    def contract(t, carry):
        total[...] += dot(hidden[t], whole(full_d[t]), ((1,), (1,)))
        return carry

    lax.fori_loop(0, 4, contract, 0)
    resid_low[...] = total[...].astype(BF)
    gp.last()

    square = jnp.zeros((own, 1), F32)
    pieces = []
    for t in range(4):
        value = dot(resid_low[...], whole(full_p[t]))
        square += jnp.sum(value * value, axis=-1, keepdims=True)
        pieces.append(value)
    inverse = lax.rsqrt(square + epsilon_unit)
    products = jnp.zeros((class_low.shape[1], own), F32)
    for t in range(4):
        pieces[t] = pieces[t] * inverse
        unit_low[t] = pieces[t].astype(BF)
        products += dot(class_low[t], unit_low[t], ((1,), (1,)))
    products = products[:classes]
    centred = products - jnp.mean(products, axis=0, keepdims=True)
    spread = jnp.mean(centred * centred, axis=0, keepdims=True)
    mask_inverse = lax.rsqrt(spread + epsilon_norm)
    centred = centred * mask_inverse
    masks[...] = centred
    stores[0].start()
    d_masks = mask_grad[...]
    d_products = mask_inverse * (
        d_masks
        - jnp.mean(d_masks, axis=0, keepdims=True)
        - centred * jnp.mean(d_masks * centred, axis=0, keepdims=True)
    )
    d_products = d_products.astype(BF)
    along = jnp.zeros((own, 1), F32)
    d_pieces = []
    for t in range(4):
        value = dot(d_products, class_low[t, :classes], ((0,), (0,)))
        along += jnp.sum(value * pieces[t], axis=-1, keepdims=True)
        d_pieces.append(value)
    flipped = resid_low[...].T
    for t in range(4):
        d_pieces[t] = (inverse * (d_pieces[t] - pieces[t] * along)).astype(BF)
        grad_p[t] = dot(flipped, d_pieces[t]).astype(BF).reshape(grad_p.shape[1:])
    sp.start()
    d_total = jnp.zeros((own, width), F32)
    for t in range(4):
        d_total += dot(d_pieces[t], whole(full_p[t]), ((1,), (1,)))
    d_resid[...] = d_total
    branch = d_total.astype(BF)
    flipped = branch.T
    sp.planes()
    sp.spread()

    def down(t, carry):
        grad_d[t] = dot(flipped, hidden[t]).astype(BF).reshape(grad_d.shape[1:])
        return carry

    lax.fori_loop(0, 4, down, 0)
    sd.start()
    class_row[z] = class_weight[...].astype(BF)
    line_row.start()
    flipped = norm_two[...].T

    def up(t, carry):
        back = dot(branch, whole(full_d[t])) * slope[t].astype(F32)
        back = back.astype(BF)
        slope[t] = back
        grad_u[t] = dot(flipped, back).astype(BF).reshape(grad_u.shape[1:])

        @pl.when(t == 1)
        def _():
            sd.planes()
            sd.spread()

        return carry

    lax.fori_loop(0, 4, up, 0)
    for transfer in (ge, ga, gc, gu, gd, gp):
        transfer.drain()
    su.start()
    total[...] = jnp.zeros_like(total)

    def narrow_back(t, carry):
        total[...] += dot(slope[t], whole(full_u[t]), ((1,), (1,)))
        return carry

    lax.fori_loop(0, 4, narrow_back, 0)
    su.planes()
    xhat, inverse = norm_parts(resid_one[...])
    gain_two_sum = jnp.sum(total[...] * xhat, axis=0, keepdims=True)
    d_resid[...] += norm_back(total[...] * gain_second, xhat, inverse)
    halo.drain()
    window[mine] = d_resid[...].astype(BF)
    back_halo = Halo(place, window, own, halo_sems.at[1])
    back_halo.start()
    sp.lines()
    class_wide[...] = jnp.zeros_like(class_wide)
    for t in range(4):
        class_wide[0:classes, t * narrow : (t + 1) * narrow] = dot(d_products, unit_low[t])
    grad_c[...] = jnp.zeros_like(grad_c)
    tiles = width // TILE_COLS
    for i in range(class_wide.shape[0] // TILE_ROWS * tiles):
        r, q = i // tiles, i % tiles
        grad_c[i // 8, (i // 4) % 2, (i // 2) % 2, i % 2] = class_wide[
            r * TILE_ROWS : (r + 1) * TILE_ROWS, q * TILE_COLS : (q + 1) * TILE_COLS
        ].astype(BF)
    sc.start()
    flipped = window[mine].T

    def outer(t, carry):
        block = dot(flipped, attended[t]).astype(BF)
        grad_a[t, :, :, :, :, CUT:] = block.reshape((2, 2, 2, piece, width - CUT))
        return carry

    lax.fori_loop(0, 4, outer, 0)
    sc.planes()
    sc.spread()
    back_halo.wait()

    def attended_back(t, carry):
        value = dot(window[...], whole(full_a[t])[:, CUT:]).astype(BF)
        slope[t, :, 0:narrow] = value[0:own]
        slope[t, :, 256 : 256 + narrow] = value[own:span]
        return carry

    lax.fori_loop(0, 4, attended_back, 0)
    sd.lines()
    su.spread()
    line_row.wait()
    stores[8].start()
    stack[...] = jnp.zeros_like(stack)

    def attend_back(t, carry):
        for h in range(HEAD_SET):
            q_cols = slice(h * SPAN, h * SPAN + HD)
            k_cols = slice(h * SPAN + HD, h * SPAN + 2 * HD)
            v_cols = slice(h * SPAN + 2 * HD, h * SPAN + 3 * HD)
            for b in range(4):
                rows = slice(b * 128, (b + 1) * 128)
                low_key, high_key = max(b - 1, 0) * 128, min(b + 2, 4) * 128
                near = slice(low_key, high_key)
                prob = probs[t, h, rows, near].astype(F32)
                d_cols = slice(b // 2 * 256 + h * HD, b // 2 * 256 + (h + 1) * HD)
                d_rows = slice(b % 2 * 128, (b % 2 + 1) * 128)
                d_prob = dot(slope[t, d_rows, d_cols], joint[t, near, v_cols], ((1,), (1,)))
                delta = jnp.sum(prob * d_prob, axis=-1, keepdims=True)
                d_scores = (prob * (d_prob - delta)).astype(BF)
                first, last = max(low_key, HALO), min(high_key, HALO + own)
                stack[rows, first - HALO : last - HALO] = d_scores[
                    :, first - low_key : last - low_key
                ]
                if b in (1, 2):
                    hidden[t, (b - 1) * 128 : b * 128, q_cols] = (
                        dot(d_scores, joint[t, near, k_cols]) * HD**-0.5
                    ).astype(BF)
            hidden[t, :, k_cols] = (
                dot(stack[...], joint[t, :, q_cols], ((0,), (0,))) * HD**-0.5
            ).astype(BF)
            d_value = jnp.zeros((own, HD), F32)
            for half in range(2):
                d_value += dot(
                    probs[t, h, half * own : (half + 1) * own, mine],
                    slope[t, :, half * 256 + h * HD : half * 256 + (h + 1) * HD],
                    ((0,), (0,)),
                )
            hidden[t, :, v_cols] = d_value.astype(BF)

        @pl.when(t == 0)
        def _():
            sp.points()
            sc.lines()

        @pl.when(t == 2)
        def _():
            sc.points()
            sd.points()

        return carry

    lax.fori_loop(0, 4, attend_back, 0)
    flipped = norm_one[mine].T

    def attend_grad(t, carry):
        block = dot(flipped, hidden[t, :, :CUT]).astype(BF)
        grad_a[t, :, :, :, :, :CUT] = block.reshape((2, 2, 2, piece, CUT))
        return carry

    lax.fori_loop(0, 4, attend_grad, 0)
    for chunk in sa:
        chunk.start()
    su.lines()
    sa[0].planes()
    sa[0].spread()
    sa[1].planes()
    sa[1].spread()
    class_sum[z, row, col, core] = sc.result().astype(BF)
    gs.start()
    gs.line()
    sa[2].planes()
    total[...] = jnp.zeros_like(total)

    def joint_back(t, carry):
        total[...] += dot(hidden[t, :, :CUT], whole(full_a[t])[:, :CUT], ((1,), (1,)))
        return carry

    lax.fori_loop(0, 4, joint_back, 0)
    gs.hop(1)
    su.points()
    xhat, inverse = norm_parts(tokens[...].astype(F32))
    gain_one_sum = jnp.sum(total[...] * xhat, axis=0, keepdims=True)
    d_resid[...] += norm_back(total[...] * gain_first, xhat, inverse)
    stores[1].start()
    grad_n[...] = jnp.zeros_like(grad_n)
    for d in range(8):
        cols = slice(d * piece, (d + 1) * piece)
        for t in range(4):
            spot = (t, d // 4, (d // 2) % 2, d % 2)
            grad_n[spot + (slice(0, 1), slice(0, piece))] = gain_one_sum[:, cols]
            grad_n[spot + (slice(1, 2), slice(0, piece))] = gain_two_sum[:, cols]
    sn.start()
    sa[0].lines()
    sa[2].spread()
    gs.hop(2)
    sn.planes()
    sn.spread()
    share_p[...] = sp.result()
    stores[2].start()
    gs.hop(3)
    sa[1].lines()
    sa[0].points()
    gs.forward()
    sn.lines()
    share_d[...] = sd.result()
    stores[3].start()
    sa[1].points()
    sa[2].lines()
    sn.points()
    gs.across()
    share_u[...] = su.result()
    stores[4].start()
    gs.last()
    stores[9].start()
    sa[2].points()
    share_n[...] = sn.result()
    stores[6].start()
    for chunk, part in zip(sa, parts):
        share_a[part] = chunk.result()
    stores[5].start()
    for transfer in (gs, sp, sd, su, sn, sc, *sa, line_row, line_all, back_halo):
        transfer.drain()
    for store in stores:
        store.wait()


def vmem_specs(count):
    return [pl.BlockSpec(memory_space=pltpu.VMEM)] * count


def any_specs(count):
    return [pl.BlockSpec(memory_space=pl.ANY)] * count


def step_call(tokens, segments, mask_grad, params):
    own, width = tokens.shape
    gain_one, attend, output, gain_two, up, down, patch, classed, embed = params
    classes = embed.shape[0]
    rows_e = -(-(classes + 2) // 32) * 32
    piece, high, narrow = up.shape[0], up.shape[1], patch.shape[1]
    span = own + 2 * HALO
    low = lambda *shape: pltpu.VMEM(shape, BF)
    wide = lambda *shape: pltpu.VMEM(shape, F32)
    shape = jax.ShapeDtypeStruct
    operands = (tokens, segments, mask_grad, gain_one[None], attend, output, gain_two[None])
    operands += tuple(params[4:])
    outs = [
        shape((classes, own), F32),
        shape((own, width), F32),
        shape((piece, narrow), F32),
        shape((piece, high), F32),
        shape((piece, high), F32),
        shape((piece, width), F32),
        shape((8, 128), F32),
        shape((4, rows_e, narrow), BF),
        shape((4, piece, narrow), BF),
        shape((4, 2, 2, 2, TILE_ROWS, TILE_COLS), BF),
    ]
    scratch = [pltpu.VMEM(v.shape, v.dtype) for v in operands]
    scratch += [pltpu.VMEM(v.shape, v.dtype) for v in outs]
    scratch += [
        low(4, 2, 2, 2, piece, width),
        low(4, 2, 2, 2, piece, high),
        low(4, 2, 2, 2, piece, high),
        low(4, 2, 2, 2, piece, narrow),
        low(2, 2, 2, piece, narrow),
        low(2, 2, 2, rows_e, piece),
        low(4, 2, 2, 2, piece, high),
        low(4, 2, 2, 2, piece, high),
        low(4, 2, 2, 2, piece, narrow),
        wide(4, 2, 2, 2, 8, 128),
        low(4, 2, 2, 2, TILE_ROWS, TILE_COLS),
        low(4, span, CUT),
        low(4, own, narrow),
        wide(own, width),
        low(own, width),
        low(4, own, high),
        low(4, own, high),
        wide(own, width),
        low(span, width),
        low(span, width),
        low(rows_e, width),
        wide(rows_e, piece),
        low(own, width),
        low(4, own, narrow),
        low(4, rows_e, narrow),
        low(4, HEAD_SET, span, span),
        low(span, own),
        wide(1, segments.shape[1] + 2 * HALO),
        wide(span, 1),
        wide(1, span),
        wide(rows_e, width),
        low(3, piece, width),
    ]
    for rows, cols, dtype in (
        (piece, narrow, BF),
        (piece, high, BF),
        (piece, high, BF),
        (8, 128, F32),
        (TILE_ROWS, TILE_COLS, BF),
    ):
        scratch += scatter_buffers(rows, cols, dtype)
    scratch += [
        pltpu.SemaphoreType.DMA((7, 23)),
        pltpu.SemaphoreType.DMA((7, 23)),
        pltpu.SemaphoreType.DMA((8, 8)),
        pltpu.SemaphoreType.DMA((8, 8)),
        pltpu.SemaphoreType.DMA((4, 3)),
        pltpu.SemaphoreType.DMA((2, 4)),
        pltpu.SemaphoreType.DMA((len(operands),)),
        pltpu.SemaphoreType.DMA((len(outs),)),
    ]
    return pl.pallas_call(
        step_kernel,
        out_shape=outs,
        in_specs=any_specs(len(operands)),
        out_specs=any_specs(len(outs)),
        scratch_shapes=scratch,
        compiler_params=pltpu.CompilerParams(
            collective_id=0, has_side_effects=True, vmem_limit_bytes=VMEM_LIMIT
        ),
    )(*operands)


def update_kernel(*refs):
    inputs, outputs, held = refs[:37], refs[37:57], refs[57:94]
    class_back, sum_wide, in_sems, out_sems = refs[94:]
    masks, token_grad, share_p, share_d, share_u, share_a, share_n = held[:7]
    class_all, class_row, class_sum = held[7:10]
    params, means, squares = held[10:19], held[19:28], held[28:37]
    loads = loader(inputs, held, in_sems)
    stores = loader(held[:2] + squares + means, outputs, out_sems)
    order = (0, 3, 6, 4, 5, 2, 1, 8, 7)
    for n in (6, 0, 1, 2, 4, 3, 5, 7, 8, 9):
        loads[n].start()
    for n in order:
        for k in (10, 19, 28):
            loads[k + n].start()
    for n in range(10):
        loads[n].wait()
        if n < 2:
            stores[n].start()

    def update(n, gradient):
        scale = block_scale if n < 6 else 1.0
        decay = 0.0 if n in (0, 3) else weight_decay
        for k in (10, 19, 28):
            if k + n != 18:
                loads[k + n].wait()
        squares[n][...], means[n][...] = adamw_update(
            params[n][...], gradient, means[n][...], squares[n][...], scale, decay
        )
        stores[2 + n].start()
        stores[11 + n].start()

    piece = share_p.shape[0]
    update(0, share_n[0:1, 0:piece])
    update(3, share_n[1:2, 0:piece])
    update(6, share_p[...])
    update(4, share_u[...])
    update(5, share_d[...])
    update(2, share_a[:, CUT:].T)
    update(1, share_a[:, :CUT])

    classes = params[8].shape[0]
    narrow = class_all.shape[2]
    tiles = sum_wide.shape[1] // TILE_COLS
    for i in range(sum_wide.shape[0] // TILE_ROWS * tiles):
        r, q = i // tiles, i % tiles
        sum_wide[
            r * TILE_ROWS : (r + 1) * TILE_ROWS, q * TILE_COLS : (q + 1) * TILE_COLS
        ] = class_sum[i // 8, (i // 4) % 2, (i // 2) % 2, i % 2].astype(F32)
    square = jnp.zeros((classes, 1), F32)
    for t in range(4):
        value = class_all[t, :classes].astype(F32)
        square += jnp.sum(value * value, axis=-1, keepdims=True)
    inverse = lax.rsqrt(square + epsilon_unit)
    along = jnp.zeros((classes, 1), F32)
    for t in range(4):
        unit = class_all[t, :classes].astype(F32) * inverse
        d_unit = sum_wide[:classes, t * narrow : (t + 1) * narrow]
        along += jnp.sum(unit * d_unit, axis=-1, keepdims=True)
    share_embed = jnp.zeros((classes, piece), F32)
    loads[18].wait()
    embed_low = params[8][...].astype(BF)
    for t in range(4):
        unit = class_all[t, :classes].astype(F32) * inverse
        d_unit = sum_wide[:classes, t * narrow : (t + 1) * narrow]
        value = (inverse * (d_unit - unit * along)).astype(BF)
        class_back[t] = value
        share_embed += dot(value, class_row[t], ((1,), (1,)))
    update(8, share_embed)
    update(7, dot(embed_low, class_back[lax.axis_index("tensor")], ((0,), (0,))))
    for store in stores:
        store.wait()


def update_call(results, params, means, squares):
    flat = lambda arrays: [a[None] if a.ndim == 1 else a for a in arrays]
    params, means, squares = flat(params), flat(means), flat(squares)
    classes, narrow = params[8].shape[0], params[7].shape[1]
    rows_e, width = results[7].shape[1], results[1].shape[1]
    operands = (*results, *params, *means, *squares)
    shape = jax.ShapeDtypeStruct
    outs = [shape(r.shape, F32) for r in results[:2]]
    outs += [shape(p.shape, F32) for p in params] * 2
    return pl.pallas_call(
        update_kernel,
        out_shape=outs,
        in_specs=any_specs(len(operands)),
        out_specs=any_specs(len(outs)),
        scratch_shapes=[pltpu.VMEM(v.shape, v.dtype) for v in operands]
        + [
            pltpu.VMEM((4, classes, narrow), BF),
            pltpu.VMEM((rows_e, width), F32),
            pltpu.SemaphoreType.DMA((len(operands),)),
            pltpu.SemaphoreType.DMA((len(outs),)),
        ],
        compiler_params=pltpu.CompilerParams(vmem_limit_bytes=VMEM_LIMIT),
    )(*operands)


def finish(masks, token_grad, grads, params, means, squares):
    scales = (block_scale,) * 6 + (1.0,) * 3
    decays = (0.0, weight_decay, weight_decay, 0.0) + (weight_decay,) * 5
    new = [adamw_update(*v) for v in zip(params, grads, means, squares, scales, decays)]
    return (masks, token_grad) + tuple(n[0] for n in new) + tuple(n[1] for n in new)


def gather_plain(shards, embed):
    def full(s):
        return lax.all_gather(lax.all_gather(s, "dp", axis=0), "tensor", axis=0)

    return [full(s) for s in shards] + [lax.all_gather(embed, "dp", axis=0)]


def scatter_plain(grads):
    def share(g):
        part = lax.psum_scatter(g, "dp", scatter_dimension=1, tiled=True)
        return lax.psum_scatter(part, "tensor", scatter_dimension=0, tiled=True)[0]

    return [share(g).astype(F32) for g in grads]


def with_halo(rows, parts):
    forward = [(i, i + 1) for i in range(parts - 1)]
    backward = [(i + 1, i) for i in range(parts - 1)]
    before = lax.ppermute(rows[-HALO:], "tensor", forward)
    after = lax.ppermute(rows[:HALO], "tensor", backward)
    return jnp.concatenate((before, rows, after), axis=0)


def local_plain(
    parts,
    tokens,
    segments,
    mask_grad,
    gain_one,
    attend_weight,
    output_weight,
    gain_two,
    up_weight,
    down_weight,
    patch_weight,
    class_weight,
    class_embed,
    *moments,
):
    means, squares = moments[:9], moments[9:]
    own = tokens.shape[0]
    width = tokens.shape[1]
    classes = class_embed.shape[0]
    dp_index = lax.axis_index("dp")
    tensor_index = lax.axis_index("tensor")
    low = lambda v: v.astype(BF)

    shard_a = jnp.concatenate((low(attend_weight), low(output_weight).T), axis=1)
    shard_u = low(up_weight)
    shard_d = low(down_weight).T
    shard_p = jnp.concatenate((low(patch_weight), low(class_weight)), axis=1)
    rows_e = -(-(classes + 2) // 32) * 32
    shard_e = jnp.zeros((rows_e, class_embed.shape[1]), BF)
    shard_e = shard_e.at[:classes].set(low(class_embed))
    shard_e = shard_e.at[classes].set(low(gain_one)).at[classes + 1].set(low(gain_two))
    full_a, full_u, full_d, full_p, full_e = gather_plain(
        (shard_a, shard_u, shard_d, shard_p), shard_e
    )
    full_a, full_u, full_d, full_p = (
        v.reshape(v.shape[0], width, v.shape[-1]) for v in (full_a, full_u, full_d, full_p)
    )
    embed_rows = full_e.transpose(1, 0, 2).reshape(rows_e, width)
    embed = embed_rows[:classes]
    gain_first = embed_rows[classes].astype(F32)[None]
    gain_second = embed_rows[classes + 1].astype(F32)[None]

    cut = attend_weight.shape[1]
    heads = cut // (3 * HD)
    w_attend, w_output = full_a[:, :, :cut], full_a[:, :, cut:]
    narrow = patch_weight.shape[1]
    w_patch, w_class = full_p[:, :, :narrow], full_p[:, :, narrow:]
    w_patch = w_patch.transpose(1, 0, 2).reshape(width, -1)
    w_class = w_class.transpose(1, 0, 2).reshape(width, -1)

    window = with_halo(tokens, parts)
    token_wide = window.astype(F32)
    xhat_one, inverse_one = norm_parts(token_wide)
    norm_one = low(xhat_one * gain_first)
    joint = jnp.einsum("sd,tdn->stn", norm_one, w_attend, preferred_element_type=F32)
    joint = low(joint).reshape(own + 2 * HALO, parts * heads, 3, HD)
    queries, keys, values = joint[:, :, 0], joint[:, :, 1], joint[:, :, 2]
    padded = jnp.pad(segments[0], HALO, constant_values=-1)
    seg = lax.dynamic_slice_in_dim(padded, tensor_index * own, own + 2 * HALO, 0)
    scores = jnp.einsum("qhd,khd->hqk", queries, keys, preferred_element_type=F32) * HD**-0.5
    scores = jnp.where(seg[None, :, None] == seg[None, None, :], scores, masked_score)
    exponent = jnp.exp(scores - jnp.max(scores, axis=-1, keepdims=True))
    prob = exponent / jnp.sum(exponent, axis=-1, keepdims=True)
    prob_low = low(prob)
    mine = slice(HALO, HALO + own)
    attended = jnp.einsum(
        "hqk,khd->qhd", prob_low[:, mine], values, preferred_element_type=F32
    )
    attended = low(attended).reshape(own, parts, heads * HD)
    resid_one = token_wide[mine] + jnp.einsum(
        "stn,tdn->sd", attended, w_output, preferred_element_type=F32
    )
    xhat_two, inverse_two = norm_parts(resid_one)
    norm_two = low(xhat_two * gain_second)
    hidden_pre = jnp.einsum("sd,tdn->stn", norm_two, full_u, preferred_element_type=F32)
    hidden, gelu_back = jax.vjp(lambda v: jax.nn.gelu(v, approximate=False), hidden_pre)
    hidden = low(hidden)
    resid_two = resid_one + jnp.einsum(
        "stn,tdn->sd", hidden, full_d, preferred_element_type=F32
    )
    resid_low = low(resid_two)
    patch_feat = dot(resid_low, w_patch)
    patch_wide, patch_inverse = unit_parts(patch_feat)
    patch_unit = low(patch_wide)
    class_feat = dot(embed, w_class)
    class_wide, class_inverse = unit_parts(class_feat)
    class_unit = low(class_wide)
    products = dot(patch_unit, class_unit, ((1,), (1,)))
    masks, mask_inverse = norm_parts(products)
    d_products = low(norm_back(mask_grad, masks, mask_inverse))
    d_class_unit = lax.psum(dot(d_products, patch_unit, ((0,), (0,))), ("dp", "tensor"))
    d_patch_unit = dot(d_products, class_unit)
    d_patch_feat = low(unit_back(d_patch_unit, patch_wide, patch_inverse))
    grad_patch = dot(resid_low, d_patch_feat, ((0,), (0,)))
    d_resid_two = dot(d_patch_feat, w_patch, ((1,), (1,)))
    d_branch_two = low(d_resid_two)
    d_hidden = jnp.einsum("sd,tdn->stn", d_branch_two, full_d, preferred_element_type=F32)
    grad_down = jnp.einsum("sd,stn->tdn", d_branch_two, hidden, preferred_element_type=F32)
    d_hidden_pre = low(gelu_back(d_hidden)[0])
    grad_up = jnp.einsum("sd,stn->tdn", norm_two, d_hidden_pre, preferred_element_type=F32)
    d_norm_two = jnp.einsum("stn,tdn->sd", d_hidden_pre, full_u, preferred_element_type=F32)
    d_resid_one = d_resid_two + norm_back(d_norm_two * gain_second, xhat_two, inverse_two)
    grad_gain_two = jnp.sum(d_norm_two * xhat_two, axis=0)
    d_branch_one = with_halo(low(d_resid_one), parts)
    d_attended = low(
        jnp.einsum("sd,tdn->stn", d_branch_one, w_output, preferred_element_type=F32)
    )
    grad_output = jnp.einsum(
        "sd,stn->tdn", d_branch_one[mine], attended, preferred_element_type=F32
    )
    d_attended = d_attended.reshape(own + 2 * HALO, parts * heads, HD)
    d_prob = jnp.einsum("qhd,khd->hqk", d_attended, values, preferred_element_type=F32)
    delta = jnp.sum(prob * d_prob, axis=-1, keepdims=True)
    d_scores = low(prob * (d_prob - delta))
    d_query = jnp.einsum(
        "hqk,khd->qhd", d_scores[:, mine], keys, preferred_element_type=F32
    )
    d_key = jnp.einsum(
        "hqk,qhd->khd", d_scores[:, :, mine], queries, preferred_element_type=F32
    )
    d_value = jnp.einsum(
        "hqk,qhd->khd", prob_low[:, :, mine], d_attended, preferred_element_type=F32
    )
    d_joint = low(
        jnp.stack((d_query * HD**-0.5, d_key * HD**-0.5, d_value), axis=2)
    ).reshape(own, parts, cut)
    grad_attend = jnp.einsum(
        "sd,stn->tdn", norm_one[mine], d_joint, preferred_element_type=F32
    )
    d_norm_one = jnp.einsum("stn,tdn->sd", d_joint, w_attend, preferred_element_type=F32)
    token_grad = d_resid_one + norm_back(
        d_norm_one * gain_first, xhat_one[mine], inverse_one[mine]
    )
    grad_gain_one = jnp.sum(d_norm_one * xhat_one[mine], axis=0)

    grad_patch = grad_patch.reshape(width, parts, narrow).transpose(1, 0, 2)
    share_p, share_d, share_u, share_a = scatter_plain(
        [
            grad_patch,
            grad_down,
            grad_up,
            jnp.concatenate((grad_attend, grad_output), axis=2),
        ]
    )
    gains = lax.psum((grad_gain_one, grad_gain_two), ("dp", "tensor"))
    step = gain_one.shape[0]
    share_one, share_two = (lax.dynamic_slice_in_dim(g, dp_index * step, step, 0) for g in gains)
    d_class_feat = low(unit_back(d_class_unit, class_wide, class_inverse))
    d_class_own = lax.dynamic_slice_in_dim(d_class_feat, tensor_index * narrow, narrow, 1)
    share_class = dot(low(class_embed), d_class_own, ((0,), (0,)))
    class_rows = lax.dynamic_slice_in_dim(w_class, dp_index * step, step, 0)
    share_embed = dot(d_class_feat, class_rows, ((1,), (1,)))
    return finish(
        masks,
        token_grad,
        (
            share_one,
            share_a[:, :cut],
            share_a[:, cut:].T,
            share_two,
            share_u,
            share_d.T,
            share_p,
            share_class,
            share_embed,
        ),
        (
            gain_one,
            attend_weight,
            output_weight,
            gain_two,
            up_weight,
            down_weight,
            patch_weight,
            class_weight,
            class_embed,
        ),
        means,
        squares,
    )


def local_kernels(tokens, segments, mask_grad, *arrays):
    def turned(group):
        return (*group[:5], group[5].T, *group[6:])

    params, means, squares = (turned(arrays[n : n + 9]) for n in (0, 9, 18))
    results = step_call(tokens, segments, mask_grad.T, params)
    masks, token_grad, *new = update_call(results, params, means, squares)
    new = [n.reshape(p.shape) for n, p in zip(new, params * 2)]
    return (masks.T, token_grad, *turned(new[:9]), *turned(new[9:]))


def solution(mesh):
    parts = mesh.shape["tensor"]
    custom = mesh.shape["dp"] == 8 and parts == 4
    params = (
        P("dp"),
        P("dp", "tensor"),
        P("tensor", "dp"),
        P("dp"),
        P("dp", "tensor"),
        P("tensor", "dp"),
        P("dp", "tensor"),
        P("dp", "tensor"),
        P(None, "dp"),
    )
    rows = P(("dp", "tensor"), None)
    return jax.shard_map(
        local_kernels if custom else functools.partial(local_plain, parts),
        mesh=mesh,
        in_specs=(rows, P("dp", None), rows) + params * 3,
        out_specs=(rows, rows) + params * 2,
        check_vma=False,
    )
```

```python
import functools

import jax
import jax.numpy as jnp
from jax import lax
from jax.experimental import pallas as pl
from jax.experimental.pallas import tpu as pltpu
from jax.sharding import PartitionSpec as P

HD = 64
HALO = 128
BF = jnp.bfloat16
F32 = jnp.float32
MESH = pl.DeviceIdType.MESH
VMEM_LIMIT = 64 * 1024 * 1024 - 512 * 1024

epsilon_norm = 1e-05
epsilon_unit = 1e-06
masked_score = -1000000000.0
first_decay = 0.9
second_decay = 0.999
first_fix = 0.99997343860112
second_fix = 0.09520785288629
adam_epsilon = 1e-08
block_scale = 0.65
weight_decay = 0.05


def dot(left, right, dims=((1,), (0,))):
    return lax.dot_general(left, right, (dims, ((), ())), preferred_element_type=F32)


def layer_norm(values, gain):
    center = values - jnp.mean(values, axis=-1, keepdims=True)
    spread = jnp.mean(center * center, axis=-1, keepdims=True)
    return center * lax.rsqrt(spread + epsilon_norm) * gain


def norm_parts(values):
    center = values - jnp.mean(values, axis=-1, keepdims=True)
    spread = jnp.mean(center * center, axis=-1, keepdims=True)
    inverse = lax.rsqrt(spread + epsilon_norm)
    return center * inverse, inverse


def norm_back(gradient, xhat, inverse):
    return inverse * (
        gradient
        - jnp.mean(gradient, axis=-1, keepdims=True)
        - xhat * jnp.mean(gradient * xhat, axis=-1, keepdims=True)
    )


def unit_parts(values):
    inverse = lax.rsqrt(jnp.sum(values * values, axis=-1, keepdims=True) + epsilon_unit)
    return values * inverse, inverse


def unit_back(gradient, unit, inverse):
    return inverse * (gradient - unit * jnp.sum(unit * gradient, axis=-1, keepdims=True))


def adamw_update(current, gradient, mean_old, square_old, step_scale, decay_rate):
    mean_new = first_decay * mean_old + (1.0 - first_decay) * gradient
    square_new = second_decay * square_old + (1.0 - second_decay) * gradient * gradient
    moved = mean_new / first_fix / (jnp.sqrt(square_new / second_fix) + adam_epsilon)
    return (step_scale * (moved + decay_rate * current), mean_new)


class Place:
    def __init__(self):
        dp, z = lax.axis_index("dp"), lax.axis_index("tensor")
        self.dp, self.z = dp, z
        self.core, self.col, self.row = dp % 2, (dp // 2) % 2, dp // 4
        self.x = (dp + 2 * (1 - 2 * self.col), z)
        self.y = (dp + 4 * (1 - 2 * self.row), z)
        self.sibling = (dp + 1 - 2 * self.core, z)

    def along(self, j):
        return (self.dp, (self.z + j) % 4)


def greet(place):
    barrier = pltpu.get_barrier_semaphore()
    targets = [place.x, place.y, place.sibling] + [place.along(j) for j in (1, 2, 3)]
    for target in targets:
        pl.semaphore_signal(barrier, inc=1, device_id=target, device_id_type=MESH)
    pl.semaphore_wait(barrier, 6)


def remote(source, target_ref, sends, receives, device):
    return pltpu.make_async_remote_copy(
        src_ref=source,
        dst_ref=target_ref,
        send_sem=sends,
        recv_sem=receives,
        device_id=device,
        device_id_type=MESH,
    )


class Line:
    def __init__(self, place, full, sends, receives):
        self.copies = [
            remote(
                full.at[place.z], full.at[place.z], sends.at[k], receives.at[k], place.along(k + 1)
            )
            for k in range(3)
        ]

    def start(self):
        for copy in self.copies:
            copy.start()

    def wait(self):
        for copy in self.copies:
            copy.wait_recv()

    def drain(self):
        for copy in self.copies:
            copy.wait_send()


class Gather:
    def __init__(self, place, full, sends, receives, w):
        self.place, self.full, self.w = place, full, w
        self.sends, self.receives = sends, receives
        self.flat = len(full.shape) == 5

    def copy(self, k):
        place, full = self.place, self.full
        row, col, core, z = place.row, place.col, place.core, place.z
        if k < 3:
            view, target = full.at[z - k, row, col, core], place.along(1)
        elif k >= 20:
            view, target = full.at[z + k - 20, row, col, core], place.along(3)
        elif k < 15:
            j = (k - 3) // 3
            if self.flat:
                view = full.at[row, col, core]
            else:
                view = full.at[(z + j) % 4, row, col, core]
            target = (place.x, place.y, place.sibling)[(k - 3) % 3]
        elif k < 17:
            spot = (row, 1 - col, core) if k == 15 else (1 - row, col, core)
            if self.flat:
                half = full.shape[3] // 2
                view = full.at[spot + (pl.ds((k - 15) * half, half),)]
            else:
                view = full.at[(pl.ds((k - 15) * 2, 2),) + spot]
            target = place.y if k == 15 else place.x
        else:
            spot = ((row, 1 - col, core), (1 - row, col, core), (1 - row, 1 - col, core))[k - 17]
            view = full.at[spot] if self.flat else full.at[(slice(None),) + spot]
            target = place.sibling
        return remote(view, view, self.sends.at[self.w, k], self.receives.at[self.w, k], target)

    def pieces(self):
        return range(1 if self.flat else 4)

    def start(self):
        for k in (3, 4, 5):
            self.copy(k).start()

    def line(self):
        z = self.place.z

        @pl.when(z < 3)
        def _():
            self.copy(0).start()

        @pl.when(z > 0)
        def _():
            self.copy(20).start()

    def hop(self, h):
        z = self.place.z

        @pl.when(z >= h)
        def _():
            self.copy(h - 1).wait_recv()
            if h < 3:

                @pl.when(z < 3)
                def _():
                    self.copy(h).start()

            for k in range(3):
                self.copy(3 + 3 * (4 - h) + k).start()

        @pl.when(z + h <= 3)
        def _():
            self.copy(19 + h).wait_recv()
            if h < 3:

                @pl.when(z > 0)
                def _():
                    self.copy(20 + h).start()

            for k in range(3):
                self.copy(3 + 3 * h + k).start()

    def forward(self):
        for j in self.pieces():
            self.copy(3 + 3 * j).wait_recv()
        self.copy(15).start()
        self.copy(17).start()
        for j in self.pieces():
            self.copy(4 + 3 * j).wait_recv()
        self.copy(16).start()
        self.copy(18).start()

    def across(self):
        self.copy(15).wait_recv()
        self.copy(16).wait_recv()
        self.copy(19).start()

    def last(self):
        for j in self.pieces():
            self.copy(5 + 3 * j).wait_recv()
        for k in (17, 18, 19):
            self.copy(k).wait_recv()

    def drain(self):
        z = self.place.z
        if not self.flat:
            for k in range(3):

                @pl.when((z < 3) & (z >= k))
                def _(k=k):
                    self.copy(k).wait_send()

                @pl.when((z > 0) & (z + k <= 3))
                def _(k=k):
                    self.copy(20 + k).wait_send()

        for j in self.pieces():
            for k in range(3):
                self.copy(3 + 3 * j + k).wait_send()
        for k in range(15, 20):
            self.copy(k).wait_send()


class PlaneGather:
    def __init__(self, place, full, sends, receives, w):
        self.place, self.full, self.w = place, full, w
        self.sends, self.receives = sends, receives

    def copy(self, k):
        place, full = self.place, self.full
        row, col, core, z = place.row, place.col, place.core, place.z
        half = full.shape[4] // 2
        if k < 3:
            view, target = full.at[z, row, col, core], (place.x, place.y, place.sibling)[k]
        elif k == 3:
            view, target = full.at[z, row, 1 - col, core, 0:half], place.y
        elif k == 4:
            view, target = full.at[z, 1 - row, col, core, half : 2 * half], place.x
        elif k < 8:
            spot = ((row, 1 - col), (1 - row, col), (1 - row, 1 - col))[k - 5]
            view, target = full.at[z, spot[0], spot[1], core], place.sibling
        elif k < 11:
            view, target = full.at[z - (k - 8), :, :, core], place.along(1)
        elif k < 14:
            view, target = full.at[z + k - 11, :, :, core], place.along(3)
        else:
            view, target = full.at[(z + k - 13) % 4, :, :, core], place.sibling
        return remote(view, view, self.sends.at[self.w, k], self.receives.at[self.w, k], target)

    def start(self):
        for k in range(3):
            self.copy(k).start()

    def forward(self):
        self.copy(0).wait_recv()
        self.copy(3).start()
        self.copy(5).start()
        self.copy(1).wait_recv()
        self.copy(4).start()
        self.copy(6).start()

    def across(self):
        z = self.place.z
        self.copy(3).wait_recv()
        self.copy(4).wait_recv()

        @pl.when(z < 3)
        def _():
            self.copy(8).start()

        @pl.when(z > 0)
        def _():
            self.copy(11).start()

        self.copy(7).start()

    def hop(self, h):
        z = self.place.z

        @pl.when(z >= h)
        def _():
            self.copy(7 + h).wait_recv()
            if h < 3:

                @pl.when(z < 3)
                def _():
                    self.copy(8 + h).start()

            self.copy(13 + 4 - h).start()

        @pl.when(z + h <= 3)
        def _():
            self.copy(10 + h).wait_recv()
            if h < 3:

                @pl.when(z > 0)
                def _():
                    self.copy(11 + h).start()

            self.copy(13 + h).start()

    def last(self):
        for k in (2, 5, 6, 7, 14, 15, 16):
            self.copy(k).wait_recv()

    def drain(self):
        z = self.place.z
        for k in (0, 1, 2, 3, 4, 5, 6, 7, 14, 15, 16):
            self.copy(k).wait_send()
        for k in range(3):

            @pl.when((z < 3) & (z >= k))
            def _(k=k):
                self.copy(8 + k).wait_send()

            @pl.when((z > 0) & (z + k <= 3))
            def _(k=k):
                self.copy(11 + k).wait_send()


class Scatter:
    def __init__(self, place, grad, buffers, sends, receives, w):
        self.place, self.grad, self.w = place, grad, w
        self.sends, self.receives = sends, receives
        self.r1, self.r2a, self.r2b, self.r3a, self.r3b, self.r4 = buffers

    def copy(self, k):
        place, r1 = self.place, self.r1
        row, col, core = place.row, place.col, place.core
        if k in (0, 8):
            half = slice(0, 2) if k == 0 else slice(2, 4)
            pair = (self.grad.at[half, :, :, 1 - core], r1.at[half], place.sibling)
        elif k == 1:
            pair = (r1.at[0:2, :, 1 - col], self.r2a, place.x)
        elif k == 2:
            pair = (r1.at[2:4, 1 - row], self.r2b, place.y)
        elif k == 3:
            pair = (r1.at[0:2, 1 - row, col], self.r3a, place.y)
        elif k == 4:
            pair = (r1.at[2:4, row, 1 - col], self.r3b, place.x)
        else:
            peer = place.along(k - 4)
            pair = (r1.at[peer[1], row, col], self.r4.at[k - 5], peer)
        return remote(
            pair[0], pair[1], self.sends.at[self.w, k], self.receives.at[self.w, k], pair[2]
        )

    def add(self, index, other):
        ref = self.r1
        ref[index] = (ref[index].astype(F32) + other.astype(F32)).astype(ref.dtype)

    def start(self, halves=(0, 1)):
        for half in halves:
            self.copy(8 * half).start()

    def planes(self, halves=(0, 1)):
        core = self.place.core
        for half in halves:
            self.copy(8 * half).wait_recv()

            def step(i, carry):
                t, y = 2 * half + i // 2, i % 2
                self.add((t, y), self.grad[t, y, :, core])
                return carry

            lax.fori_loop(0, 4, step, 0)

    def spread(self, halves=(0, 1)):
        for half in halves:
            self.copy(1 + half).start()

    def lines(self):
        col, row = self.place.col, self.place.row
        self.copy(1).wait_recv()
        for t in range(2):
            for y in range(2):
                self.add((t, y, col), self.r2a[t, y])
        self.copy(3).start()
        self.copy(2).wait_recv()
        for t in range(2):
            for x in range(2):
                self.add((2 + t, row, x), self.r2b[t, x])
        self.copy(4).start()

    def points(self):
        col, row = self.place.col, self.place.row
        self.copy(3).wait_recv()
        for t in range(2):
            self.add((t, row, col), self.r3a[t])
        self.copy(4).wait_recv()
        for t in range(2):
            self.add((2 + t, row, col), self.r3b[t])
        for k in (5, 6, 7):
            self.copy(k).start()

    def result(self):
        place = self.place
        for k in (5, 6, 7):
            self.copy(k).wait_recv()
        total = self.r1[place.z, place.row, place.col].astype(F32)
        for j in range(3):
            total = total + self.r4[j].astype(F32)
        return total

    def drain(self):
        for k in range(9):
            self.copy(k).wait_send()


class LineScatter:
    def __init__(self, place, grad, buffers, sends, receives, w):
        self.place, self.grad, self.w = place, grad, w
        self.sends, self.receives = sends, receives
        self.r1, self.r2a, self.r2b, self.r3a, self.r3b, self.r4 = buffers

    def copy(self, k):
        place, r1 = self.place, self.r1
        row, col, core, z = place.row, place.col, place.core, place.z
        half = r1.shape[3] // 2
        if k == 0:
            pair = (self.grad.at[:, :, :, 1 - core], r1, place.sibling)
        elif k == 1:
            pair = (r1.at[z, :, 1 - col, 0:half], self.r2a, place.x)
        elif k == 2:
            pair = (r1.at[z, 1 - row, :, half : 2 * half], self.r2b, place.y)
        elif k == 3:
            pair = (r1.at[z, 1 - row, col, 0:half], self.r3a, place.y)
        elif k == 4:
            pair = (r1.at[z, row, 1 - col, half : 2 * half], self.r3b, place.x)
        else:
            peer = place.along(k - 4)
            pair = (r1.at[peer[1]], self.r4.at[k - 5], peer)
        return remote(
            pair[0], pair[1], self.sends.at[self.w, k], self.receives.at[self.w, k], pair[2]
        )

    def add(self, index, other):
        ref = self.r1
        ref[index] = (ref[index].astype(F32) + other.astype(F32)).astype(ref.dtype)

    def start(self):
        self.copy(0).start()

    def planes(self):
        core = self.place.core
        self.copy(0).wait_recv()

        def step(i, carry):
            t, y = i // 2, i % 2
            self.add((t, y), self.grad[t, y, :, core])
            return carry

        lax.fori_loop(0, 8, step, 0)
        for k in (5, 6, 7):
            self.copy(k).start()

    def depth(self):
        z = self.place.z
        for k in (5, 6, 7):
            self.copy(k).wait_recv()
        for y in range(2):
            for x in range(2):
                value = self.r1[z, y, x].astype(F32)
                for j in range(3):
                    value = value + self.r4[j, y, x].astype(F32)
                self.r1[z, y, x] = value.astype(self.r1.dtype)
        self.copy(1).start()
        self.copy(2).start()

    def lines(self):
        place, half = self.place, self.r1.shape[3] // 2
        self.copy(1).wait_recv()
        for y in range(2):
            self.add((place.z, y, place.col, slice(0, half)), self.r2a[y])
        self.copy(3).start()
        self.copy(2).wait_recv()
        for x in range(2):
            self.add((place.z, place.row, x, slice(half, 2 * half)), self.r2b[x])
        self.copy(4).start()

    def result(self, out):
        place, half = self.place, self.r1.shape[3] // 2
        for k, part in ((3, slice(0, half)), (4, slice(half, 2 * half))):
            self.copy(k).wait_recv()
            other = self.r3a if k == 3 else self.r3b
            mine = self.r1[place.z, place.row, place.col, part]
            out[part] = mine.astype(F32) + other[...].astype(F32)

    def drain(self):
        for k in range(8):
            self.copy(k).wait_send()


def scatter_buffers(rows, cols, dtype):
    return [
        pltpu.VMEM((4, 2, 2, rows, cols), dtype),
        pltpu.VMEM((2, 2, rows, cols), dtype),
        pltpu.VMEM((2, 2, rows, cols), dtype),
        pltpu.VMEM((2, rows, cols), dtype),
        pltpu.VMEM((2, rows, cols), dtype),
        pltpu.VMEM((3, rows, cols), dtype),
    ]


HEAD_SET = 3
SPAN = 3 * HD
CUT = HEAD_SET * SPAN
TILE_ROWS, TILE_COLS = 16, 256


def whole(value):
    return value.reshape(-1, value.shape[-1])


def gelu_parts(values):
    cumulative = 0.5 * (1.0 + lax.erf(values * 0.7071067811865476))
    density = 0.3989422804014327 * jnp.exp(-0.5 * values * values)
    return values * cumulative, cumulative + values * density


class Halo:
    def __init__(self, place, window, own, semaphores):
        edge = HALO + own
        self.place, self.window, self.edge = place, window, edge
        self.down = remote(
            window.at[pl.ds(HALO, HALO)],
            window.at[pl.ds(edge, HALO)],
            semaphores.at[0],
            semaphores.at[1],
            place.along(3),
        )
        self.up = remote(
            window.at[pl.ds(own, HALO)],
            window.at[pl.ds(0, HALO)],
            semaphores.at[2],
            semaphores.at[3],
            place.along(1),
        )

    def start(self):
        z, window = self.place.z, self.window
        blank = jnp.zeros((HALO, window.shape[1]), window.dtype)

        @pl.when(z > 0)
        def _():
            self.down.start()

        @pl.when(z < 3)
        def _():
            self.up.start()

        @pl.when(z == 0)
        def _():
            window[0:HALO] = blank

        @pl.when(z == 3)
        def _():
            window[self.edge : self.edge + HALO] = blank

    def wait(self):
        z = self.place.z

        @pl.when(z < 3)
        def _():
            self.down.wait_recv()

        @pl.when(z > 0)
        def _():
            self.up.wait_recv()

    def drain(self):
        z = self.place.z

        @pl.when(z > 0)
        def _():
            self.down.wait_send()

        @pl.when(z < 3)
        def _():
            self.up.wait_send()


def loader(inputs, places, semaphores):
    return [
        pltpu.make_async_copy(source, target, semaphores.at[n])
        for n, (source, target) in enumerate(zip(inputs, places))
    ]


def step_kernel(*refs):
    inputs, outputs, held = refs[:12], refs[12:22], refs[22:34]
    (
        tokens,
        segments,
        mask_grad,
        gain_one,
        attend_weight,
        output_weight,
        gain_two,
        up_weight,
        down_weight,
        patch_weight,
        class_weight,
        class_embed,
    ) = held
    results = refs[34:44]
    (
        masks,
        d_resid,
        share_p,
        share_d,
        share_u,
        share_a,
        share_n,
        class_all,
        class_row,
        class_sum,
    ) = results
    (
        full_a,
        full_u,
        full_d,
        full_p,
        full_c,
        full_e,
        grad_d,
        grad_u,
        grad_p,
        grad_n,
        grad_c,
        joint,
        attended,
        resid_one,
        norm_two,
        hidden,
        slope,
        total,
        window,
        norm_one,
        embed,
        embed_wide,
        resid_low,
        unit_low,
        class_low,
        probs,
        stack,
        seg_wide,
        seg_col,
        seg_row,
        class_wide,
        r4_a,
    ) = refs[44:76]
    buffers = refs[76:106]
    (
        gather_sends,
        gather_receives,
        scatter_sends,
        scatter_receives,
        line_sems,
        halo_sems,
        in_sems,
        out_sems,
    ) = refs[106:]
    loads = loader(inputs, held, in_sems)
    stores = loader(results, outputs, out_sems)
    for n in (11, 3, 6, 0, 4, 5, 10, 7, 8, 9, 1, 2):
        loads[n].start()

    place = Place()
    z, row, col, core = place.z, place.row, place.col, place.core
    own, width = tokens.shape
    span = own + 2 * HALO
    piece = width // 8
    narrow = patch_weight.shape[1]
    classes = class_embed.shape[0]
    mine = slice(HALO, HALO + own)
    ge, ga, gc, gu, gd, gp, gs = (
        (PlaneGather if full is full_p else Gather)(
            place, full, gather_sends, gather_receives, w
        )
        for w, full in enumerate((full_e, full_a, full_c, full_u, full_d, full_p, class_sum))
    )
    sp, sd, su, sn, sc = (
        (LineScatter if g is grad_p else Scatter)(
            place, g, buffers[6 * w : 6 * w + 6], scatter_sends, scatter_receives, w
        )
        for w, g in enumerate((grad_p, grad_d, grad_u, grad_n, grad_c))
    )
    grad_a = full_u
    third = piece // 3
    parts = [slice(n * third, (n + 1) * third) for n in range(3)]
    sa = [
        Scatter(
            place,
            grad_a.at[:, :, :, :, part],
            (
                full_d.at[:, :, :, 0, part],
                full_d.at[0:2, :, 0, 1, part],
                full_d.at[2:4, :, 0, 1, part],
                full_d.at[0:2, 0, 1, 1, part],
                full_d.at[2:4, 0, 1, 1, part],
                r4_a.at[:, part],
            ),
            scatter_sends,
            scatter_receives,
            5 + n,
        )
        for n, part in enumerate(parts)
    ]
    line_row = Line(place, class_row, line_sems.at[0], line_sems.at[1])
    line_all = Line(place, class_all, line_sems.at[2], line_sems.at[3])

    embed_wide[...] = jnp.zeros_like(embed_wide)
    for n in (11, 3, 6):
        loads[n].wait()
    embed_wide[0:classes] = class_embed[...]
    embed_wide[classes : classes + 1] = gain_one[...]
    embed_wide[classes + 1 : classes + 2] = gain_two[...]
    full_e[row, col, core] = embed_wide[...].astype(BF)
    greet(place)
    ge.start()
    loads[0].wait()
    window[mine] = tokens[...]
    halo = Halo(place, window, own, halo_sems.at[0])
    halo.start()
    loads[4].wait()
    loads[5].wait()
    full_a[z, row, col, core, :, 0:CUT] = attend_weight[...].astype(BF)
    full_a[z, row, col, core, :, CUT:] = output_weight[...].T.astype(BF)
    ga.start()
    ga.line()
    loads[10].wait()
    full_c[row, col, core] = class_weight[...].astype(BF)
    gc.start()
    loads[7].wait()
    full_u[z, row, col, core] = up_weight[...].astype(BF)
    gu.start()
    gu.line()
    loads[9].wait()
    full_p[z, row, col, core] = patch_weight[...].astype(BF)
    gp.start()
    loads[8].wait()
    full_d[z, row, col, core] = down_weight[...].astype(BF)
    gd.start()
    ga.hop(1)

    loads[1].wait()
    loads[2].wait()
    seg_wide[...] = jnp.full_like(seg_wide, -1.0)
    seg_wide[:, HALO : HALO + segments.shape[1]] = segments[...].astype(F32)
    seg_row[...] = seg_wide[:, pl.ds(pl.multiple_of(z * own, 128), span)]
    seg_col[...] = jnp.broadcast_to(seg_row[...], (8, span)).T[:, 0:1]
    gc.forward()
    gd.line()
    ge.forward()
    gu.hop(1)
    ge.across()
    ga.hop(2)
    ga.hop(3)
    ge.last()
    halo.wait()
    for d in range(8):
        embed[:, d * piece : (d + 1) * piece] = full_e[d // 4, (d // 2) % 2, d % 2]
    gains = embed[classes : classes + 2, :].astype(F32)
    gain_first, gain_second = gains[0:1], gains[1:2]

    def first_norm(i, carry):
        rows = pl.ds(pl.multiple_of(i * 128, 128), 128)
        xhat, _ = norm_parts(window[rows].astype(F32))
        norm_one[rows] = (xhat * gain_first).astype(BF)
        return carry

    lax.fori_loop(0, span // 128, first_norm, 0)
    gp.forward()
    gu.hop(2)
    gp.across()
    ga.forward()
    gc.across()
    gd.hop(1)
    gc.last()
    ga.across()
    class_all[z] = dot(embed[...], whole(full_c[...])).astype(BF)
    line_all.start()
    class_row[z] = class_weight[...].astype(BF)
    line_row.start()
    ga.last()
    gd.hop(2)
    def project(t, carry):
        joint[t] = dot(norm_one[...], whole(full_a[t])[:, :CUT]).astype(BF)
        return carry

    lax.fori_loop(0, 4, project, 0)
    gu.hop(3)
    gu.forward()
    gp.hop(1)
    gd.hop(3)
    probs[...] = jnp.zeros_like(probs)

    def attend(t, carry):
        for h in range(HEAD_SET):
            q_cols = slice(h * SPAN, h * SPAN + HD)
            k_cols = slice(h * SPAN + HD, h * SPAN + 2 * HD)
            v_cols = slice(h * SPAN + 2 * HD, h * SPAN + 3 * HD)
            for b in range(4):
                rows = slice(b * 128, (b + 1) * 128)
                near = slice(max(b - 1, 0) * 128, min(b + 2, 4) * 128)
                scores = dot(joint[t, rows, q_cols], joint[t, near, k_cols], ((1,), (1,)))
                match = seg_col[rows] == seg_row[:, near]
                scores = jnp.where(match, scores * HD**-0.5, masked_score)
                exponent = jnp.exp(scores - jnp.max(scores, axis=-1, keepdims=True))
                row_total = jnp.sum(exponent, axis=-1, keepdims=True)
                prob = (exponent / row_total).astype(BF)
                probs[t, h, rows, near] = prob
                if b in (1, 2):
                    attended[t, (b - 1) * 128 : b * 128, h * HD : (h + 1) * HD] = dot(
                        prob, joint[t, near, v_cols]
                    ).astype(BF)

        @pl.when(t == 0)
        def _():
            gp.hop(2)

        @pl.when(t == 1)
        def _():
            gu.across()
            gp.hop(3)

        @pl.when(t == 2)
        def _():
            gd.forward()

        @pl.when(t == 3)
        def _():
            gp.last()

        return carry

    lax.fori_loop(0, 4, attend, 0)
    resid_one[...] = tokens[...].astype(F32)

    def output(t, carry):
        resid_one[...] += dot(attended[t], whole(full_a[t])[:, CUT:], ((1,), (1,)))
        return carry

    lax.fori_loop(0, 4, output, 0)
    xhat, _ = norm_parts(resid_one[...])
    norm_two[...] = (xhat * gain_second).astype(BF)
    gu.last()
    def expand(t, carry):
        value, derivative = gelu_parts(dot(norm_two[...], whole(full_u[t])))
        hidden[t] = value.astype(BF)
        slope[t] = derivative.astype(BF)

        @pl.when(t == 3)
        def _():
            gd.across()
            gd.last()

        return carry

    lax.fori_loop(0, 4, expand, 0)
    total[...] = resid_one[...]

    def contract(t, carry):
        total[...] += dot(hidden[t], whole(full_d[t]), ((1,), (1,)))
        return carry

    lax.fori_loop(0, 4, contract, 0)
    resid_low[...] = total[...].astype(BF)
    line_all.wait()
    stores[7].start()
    line_row.wait()
    stores[8].start()
    class_square = jnp.zeros((class_all.shape[1], 1), F32)
    for t in range(4):
        value = class_all[t].astype(F32)
        class_square += jnp.sum(value * value, axis=-1, keepdims=True)
    class_inverse = lax.rsqrt(class_square + epsilon_unit)
    for t in range(4):
        class_low[t] = (class_all[t].astype(F32) * class_inverse).astype(BF)

    square = jnp.zeros((own, 1), F32)
    pieces = []
    for t in range(4):
        value = dot(resid_low[...], whole(full_p[t]))
        square += jnp.sum(value * value, axis=-1, keepdims=True)
        pieces.append(value)
    inverse = lax.rsqrt(square + epsilon_unit)
    products = jnp.zeros((class_low.shape[1], own), F32)
    for t in range(4):
        pieces[t] = pieces[t] * inverse
        unit_low[t] = pieces[t].astype(BF)
        products += dot(class_low[t], unit_low[t], ((1,), (1,)))
    products = products[:classes]
    centred = products - jnp.mean(products, axis=0, keepdims=True)
    spread = jnp.mean(centred * centred, axis=0, keepdims=True)
    mask_inverse = lax.rsqrt(spread + epsilon_norm)
    centred = centred * mask_inverse
    masks[...] = centred
    stores[0].start()
    d_masks = mask_grad[...]
    d_products = mask_inverse * (
        d_masks
        - jnp.mean(d_masks, axis=0, keepdims=True)
        - centred * jnp.mean(d_masks * centred, axis=0, keepdims=True)
    )
    d_products = d_products.astype(BF)
    along = jnp.zeros((own, 1), F32)
    d_pieces = []
    for t in range(4):
        value = dot(d_products, class_low[t, :classes], ((0,), (0,)))
        along += jnp.sum(value * pieces[t], axis=-1, keepdims=True)
        d_pieces.append(value)
    flipped = resid_low[...].T
    for t in range(4):
        d_pieces[t] = (inverse * (d_pieces[t] - pieces[t] * along)).astype(BF)
        grad_p[t] = dot(flipped, d_pieces[t]).astype(BF).reshape(grad_p.shape[1:])
    sp.start()
    d_total = jnp.zeros((own, width), F32)
    for t in range(4):
        d_total += dot(d_pieces[t], whole(full_p[t]), ((1,), (1,)))
    d_resid[...] = d_total
    branch = d_total.astype(BF)
    flipped = branch.T
    sp.planes()

    def down(t, carry):
        grad_d[t] = dot(flipped, hidden[t]).astype(BF).reshape(grad_d.shape[1:])

        @pl.when(t == 1)
        def _():
            sd.start((0,))

        @pl.when(t == 3)
        def _():
            sd.start((1,))
            sd.planes((0,))
            sd.spread((0,))

        return carry

    lax.fori_loop(0, 4, down, 0)
    flipped = norm_two[...].T

    def up(t, carry):
        back = dot(branch, whole(full_d[t])) * slope[t].astype(F32)
        back = back.astype(BF)
        slope[t] = back
        grad_u[t] = dot(flipped, back).astype(BF).reshape(grad_u.shape[1:])

        @pl.when(t == 0)
        def _():
            sd.planes((1,))
            sd.spread((1,))

        return carry

    lax.fori_loop(0, 4, up, 0)
    for transfer in (ge, ga, gc, gu, gd, gp):
        transfer.drain()
    su.start()
    total[...] = jnp.zeros_like(total)

    def narrow_back(t, carry):
        total[...] += dot(slope[t], whole(full_u[t]), ((1,), (1,)))
        return carry

    lax.fori_loop(0, 4, narrow_back, 0)
    su.planes()
    xhat, inverse = norm_parts(resid_one[...])
    gain_two_sum = jnp.sum(total[...] * xhat, axis=0, keepdims=True)
    d_resid[...] += norm_back(total[...] * gain_second, xhat, inverse)
    halo.drain()
    window[mine] = d_resid[...].astype(BF)
    back_halo = Halo(place, window, own, halo_sems.at[1])
    back_halo.start()
    class_wide[...] = jnp.zeros_like(class_wide)
    for t in range(4):
        class_wide[0:classes, t * narrow : (t + 1) * narrow] = dot(d_products, unit_low[t])
    grad_c[...] = jnp.zeros_like(grad_c)
    tiles = width // TILE_COLS
    for i in range(class_wide.shape[0] // TILE_ROWS * tiles):
        r, q = i // tiles, i % tiles
        grad_c[i // 8, (i // 4) % 2, (i // 2) % 2, i % 2] = class_wide[
            r * TILE_ROWS : (r + 1) * TILE_ROWS, q * TILE_COLS : (q + 1) * TILE_COLS
        ].astype(BF)
    sc.start()
    flipped = window[mine].T

    def outer(t, carry):
        block = dot(flipped, attended[t]).astype(BF)
        grad_a[t, :, :, :, :, CUT:] = block.reshape((2, 2, 2, piece, width - CUT))
        return carry

    lax.fori_loop(0, 4, outer, 0)
    sc.planes()
    sc.spread()
    back_halo.wait()

    def attended_back(t, carry):
        value = dot(window[...], whole(full_a[t])[:, CUT:]).astype(BF)
        slope[t, :, 0:narrow] = value[0:own]
        slope[t, :, 256 : 256 + narrow] = value[own:span]
        return carry

    lax.fori_loop(0, 4, attended_back, 0)
    sc.lines()
    sd.lines()
    su.spread()
    stack[...] = jnp.zeros_like(stack)

    def attend_back(t, carry):
        for h in range(HEAD_SET):
            q_cols = slice(h * SPAN, h * SPAN + HD)
            k_cols = slice(h * SPAN + HD, h * SPAN + 2 * HD)
            v_cols = slice(h * SPAN + 2 * HD, h * SPAN + 3 * HD)
            for b in range(4):
                rows = slice(b * 128, (b + 1) * 128)
                low_key, high_key = max(b - 1, 0) * 128, min(b + 2, 4) * 128
                near = slice(low_key, high_key)
                prob = probs[t, h, rows, near].astype(F32)
                d_cols = slice(b // 2 * 256 + h * HD, b // 2 * 256 + (h + 1) * HD)
                d_rows = slice(b % 2 * 128, (b % 2 + 1) * 128)
                d_prob = dot(slope[t, d_rows, d_cols], joint[t, near, v_cols], ((1,), (1,)))
                delta = jnp.sum(prob * d_prob, axis=-1, keepdims=True)
                d_scores = (prob * (d_prob - delta)).astype(BF)
                first, last = max(low_key, HALO), min(high_key, HALO + own)
                stack[rows, first - HALO : last - HALO] = d_scores[
                    :, first - low_key : last - low_key
                ]
                if b in (1, 2):
                    hidden[t, (b - 1) * 128 : b * 128, q_cols] = (
                        dot(d_scores, joint[t, near, k_cols]) * HD**-0.5
                    ).astype(BF)
            hidden[t, :, k_cols] = (
                dot(stack[...], joint[t, :, q_cols], ((0,), (0,))) * HD**-0.5
            ).astype(BF)
            d_value = jnp.zeros((own, HD), F32)
            for half in range(2):
                d_value += dot(
                    probs[t, h, half * own : (half + 1) * own, mine],
                    slope[t, :, half * 256 + h * HD : half * 256 + (h + 1) * HD],
                    ((0,), (0,)),
                )
            hidden[t, :, v_cols] = d_value.astype(BF)

        @pl.when(t == 0)
        def _():
            sc.points()
            sp.depth()

        @pl.when(t == 1)
        def _():
            class_sum[z, row, col, core] = sc.result().astype(BF)
            gs.start()
            gs.line()

        @pl.when(t == 2)
        def _():
            gs.hop(1)
            sd.points()

        @pl.when(t == 3)
        def _():
            gs.hop(2)

        return carry

    lax.fori_loop(0, 4, attend_back, 0)
    total[...] = jnp.zeros_like(total)

    def joint_back(t, carry):
        total[...] += dot(hidden[t, :, :CUT], whole(full_a[t])[:, :CUT], ((1,), (1,)))
        return carry

    lax.fori_loop(0, 4, joint_back, 0)
    xhat, inverse = norm_parts(tokens[...].astype(F32))
    gain_one_sum = jnp.sum(total[...] * xhat, axis=0, keepdims=True)
    grad_n[...] = jnp.zeros_like(grad_n)
    for d in range(8):
        cols = slice(d * piece, (d + 1) * piece)
        for t in range(4):
            spot = (t, d // 4, (d // 2) % 2, d % 2)
            grad_n[spot + (slice(0, 1), slice(0, piece))] = gain_one_sum[:, cols]
            grad_n[spot + (slice(1, 2), slice(0, piece))] = gain_two_sum[:, cols]
    sn.start()
    flipped = norm_one[mine].T

    def attend_grad(t, carry):
        block = dot(flipped, hidden[t, :, :CUT]).astype(BF)
        grad_a[t, :, :, :, :, :CUT] = block.reshape((2, 2, 2, piece, CUT))
        return carry

    lax.fori_loop(0, 4, attend_grad, 0)
    for chunk in sa:
        chunk.start()
    sn.planes()
    sn.spread()
    su.lines()
    sp.lines()
    sa[0].planes()
    sa[0].spread()
    sa[1].planes()
    sa[1].spread()
    gs.hop(3)
    sa[2].planes()
    d_resid[...] += norm_back(total[...] * gain_first, xhat, inverse)
    stores[1].start()
    sn.lines()
    su.points()
    sa[0].lines()
    sa[2].spread()
    sn.points()
    sp.result(share_p)
    stores[2].start()
    gs.forward()
    sa[1].lines()
    sa[0].points()
    gs.across()
    share_d[...] = sd.result()
    stores[3].start()
    share_n[...] = sn.result()
    stores[6].start()
    sa[2].lines()
    sa[1].points()
    gs.last()
    stores[9].start()
    share_u[...] = su.result()
    stores[4].start()
    sa[2].points()
    for chunk, part in zip(sa, parts):
        share_a[part] = chunk.result()
    stores[5].start()
    for transfer in (gs, sp, sd, su, sn, sc, *sa, line_row, line_all, back_halo):
        transfer.drain()
    for store in stores:
        store.wait()


def vmem_specs(count):
    return [pl.BlockSpec(memory_space=pltpu.VMEM)] * count


def any_specs(count):
    return [pl.BlockSpec(memory_space=pl.ANY)] * count


def step_call(tokens, segments, mask_grad, params):
    own, width = tokens.shape
    gain_one, attend, output, gain_two, up, down, patch, classed, embed = params
    classes = embed.shape[0]
    rows_e = -(-(classes + 2) // 32) * 32
    piece, high, narrow = up.shape[0], up.shape[1], patch.shape[1]
    span = own + 2 * HALO
    low = lambda *shape: pltpu.VMEM(shape, BF)
    wide = lambda *shape: pltpu.VMEM(shape, F32)
    shape = jax.ShapeDtypeStruct
    operands = (tokens, segments, mask_grad, gain_one[None], attend, output, gain_two[None])
    operands += tuple(params[4:])
    outs = [
        shape((classes, own), F32),
        shape((own, width), F32),
        shape((piece, narrow), F32),
        shape((piece, high), F32),
        shape((piece, high), F32),
        shape((piece, width), F32),
        shape((8, 128), F32),
        shape((4, rows_e, narrow), BF),
        shape((4, piece, narrow), BF),
        shape((4, 2, 2, 2, TILE_ROWS, TILE_COLS), BF),
    ]
    scratch = [pltpu.VMEM(v.shape, v.dtype) for v in operands]
    scratch += [pltpu.VMEM(v.shape, v.dtype) for v in outs]
    scratch += [
        low(4, 2, 2, 2, piece, width),
        low(4, 2, 2, 2, piece, high),
        low(4, 2, 2, 2, piece, high),
        low(4, 2, 2, 2, piece, narrow),
        low(2, 2, 2, piece, narrow),
        low(2, 2, 2, rows_e, piece),
        low(4, 2, 2, 2, piece, high),
        low(4, 2, 2, 2, piece, high),
        low(4, 2, 2, 2, piece, narrow),
        wide(4, 2, 2, 2, 8, 128),
        low(4, 2, 2, 2, TILE_ROWS, TILE_COLS),
        low(4, span, CUT),
        low(4, own, narrow),
        wide(own, width),
        low(own, width),
        low(4, own, high),
        low(4, own, high),
        wide(own, width),
        low(span, width),
        low(span, width),
        low(rows_e, width),
        wide(rows_e, piece),
        low(own, width),
        low(4, own, narrow),
        low(4, rows_e, narrow),
        low(4, HEAD_SET, span, span),
        low(span, own),
        wide(1, segments.shape[1] + 2 * HALO),
        wide(span, 1),
        wide(1, span),
        wide(rows_e, width),
        low(3, piece, width),
    ]
    scratch += [
        low(4, 2, 2, piece, narrow),
        low(2, piece // 2, narrow),
        low(2, piece // 2, narrow),
        low(piece // 2, narrow),
        low(piece // 2, narrow),
        low(3, 2, 2, piece, narrow),
    ]
    for rows, cols, dtype in (
        (piece, high, BF),
        (piece, high, BF),
        (8, 128, F32),
        (TILE_ROWS, TILE_COLS, BF),
    ):
        scratch += scatter_buffers(rows, cols, dtype)
    scratch += [
        pltpu.SemaphoreType.DMA((7, 23)),
        pltpu.SemaphoreType.DMA((7, 23)),
        pltpu.SemaphoreType.DMA((8, 9)),
        pltpu.SemaphoreType.DMA((8, 9)),
        pltpu.SemaphoreType.DMA((4, 3)),
        pltpu.SemaphoreType.DMA((2, 4)),
        pltpu.SemaphoreType.DMA((len(operands),)),
        pltpu.SemaphoreType.DMA((len(outs),)),
    ]
    return pl.pallas_call(
        step_kernel,
        out_shape=outs,
        in_specs=any_specs(len(operands)),
        out_specs=any_specs(len(outs)),
        scratch_shapes=scratch,
        compiler_params=pltpu.CompilerParams(
            collective_id=0, has_side_effects=True, vmem_limit_bytes=VMEM_LIMIT
        ),
    )(*operands)


def update_kernel(*refs):
    inputs, outputs, held = refs[:37], refs[37:57], refs[57:94]
    class_back, sum_wide, in_sems, out_sems = refs[94:]
    masks, token_grad, share_p, share_d, share_u, share_a, share_n = held[:7]
    class_all, class_row, class_sum = held[7:10]
    params, means, squares = held[10:19], held[19:28], held[28:37]
    loads = loader(inputs, held, in_sems)
    stores = loader(held[:2] + squares + means, outputs, out_sems)
    order = (0, 3, 6, 4, 5, 2, 1, 8, 7)
    for n in (6, 0, 1, 2, 4, 3, 5, 7, 8, 9):
        loads[n].start()
    for n in order:
        for k in (10, 19, 28):
            loads[k + n].start()
    for n in range(10):
        loads[n].wait()
        if n < 2:
            stores[n].start()

    def update(n, gradient):
        scale = block_scale if n < 6 else 1.0
        decay = 0.0 if n in (0, 3) else weight_decay
        for k in (10, 19, 28):
            if k + n != 18:
                loads[k + n].wait()
        squares[n][...], means[n][...] = adamw_update(
            params[n][...], gradient, means[n][...], squares[n][...], scale, decay
        )
        stores[2 + n].start()
        stores[11 + n].start()

    piece = share_p.shape[0]
    update(0, share_n[0:1, 0:piece])
    update(3, share_n[1:2, 0:piece])
    update(6, share_p[...])
    update(4, share_u[...])
    update(5, share_d[...])
    update(2, share_a[:, CUT:].T)
    update(1, share_a[:, :CUT])

    classes = params[8].shape[0]
    narrow = class_all.shape[2]
    tiles = sum_wide.shape[1] // TILE_COLS
    for i in range(sum_wide.shape[0] // TILE_ROWS * tiles):
        r, q = i // tiles, i % tiles
        sum_wide[
            r * TILE_ROWS : (r + 1) * TILE_ROWS, q * TILE_COLS : (q + 1) * TILE_COLS
        ] = class_sum[i // 8, (i // 4) % 2, (i // 2) % 2, i % 2].astype(F32)
    square = jnp.zeros((classes, 1), F32)
    for t in range(4):
        value = class_all[t, :classes].astype(F32)
        square += jnp.sum(value * value, axis=-1, keepdims=True)
    inverse = lax.rsqrt(square + epsilon_unit)
    along = jnp.zeros((classes, 1), F32)
    for t in range(4):
        unit = class_all[t, :classes].astype(F32) * inverse
        d_unit = sum_wide[:classes, t * narrow : (t + 1) * narrow]
        along += jnp.sum(unit * d_unit, axis=-1, keepdims=True)
    share_embed = jnp.zeros((classes, piece), F32)
    loads[18].wait()
    embed_low = params[8][...].astype(BF)
    for t in range(4):
        unit = class_all[t, :classes].astype(F32) * inverse
        d_unit = sum_wide[:classes, t * narrow : (t + 1) * narrow]
        value = (inverse * (d_unit - unit * along)).astype(BF)
        class_back[t] = value
        share_embed += dot(value, class_row[t], ((1,), (1,)))
    update(8, share_embed)
    update(7, dot(embed_low, class_back[lax.axis_index("tensor")], ((0,), (0,))))
    for store in stores:
        store.wait()


def update_call(results, params, means, squares):
    flat = lambda arrays: [a[None] if a.ndim == 1 else a for a in arrays]
    params, means, squares = flat(params), flat(means), flat(squares)
    classes, narrow = params[8].shape[0], params[7].shape[1]
    rows_e, width = results[7].shape[1], results[1].shape[1]
    operands = (*results, *params, *means, *squares)
    shape = jax.ShapeDtypeStruct
    outs = [shape(r.shape, F32) for r in results[:2]]
    outs += [shape(p.shape, F32) for p in params] * 2
    return pl.pallas_call(
        update_kernel,
        out_shape=outs,
        in_specs=any_specs(len(operands)),
        out_specs=any_specs(len(outs)),
        scratch_shapes=[pltpu.VMEM(v.shape, v.dtype) for v in operands]
        + [
            pltpu.VMEM((4, classes, narrow), BF),
            pltpu.VMEM((rows_e, width), F32),
            pltpu.SemaphoreType.DMA((len(operands),)),
            pltpu.SemaphoreType.DMA((len(outs),)),
        ],
        compiler_params=pltpu.CompilerParams(vmem_limit_bytes=VMEM_LIMIT),
    )(*operands)


def finish(masks, token_grad, grads, params, means, squares):
    scales = (block_scale,) * 6 + (1.0,) * 3
    decays = (0.0, weight_decay, weight_decay, 0.0) + (weight_decay,) * 5
    new = [adamw_update(*v) for v in zip(params, grads, means, squares, scales, decays)]
    return (masks, token_grad) + tuple(n[0] for n in new) + tuple(n[1] for n in new)


def gather_plain(shards, embed):
    def full(s):
        return lax.all_gather(lax.all_gather(s, "dp", axis=0), "tensor", axis=0)

    return [full(s) for s in shards] + [lax.all_gather(embed, "dp", axis=0)]


def scatter_plain(grads):
    def share(g):
        part = lax.psum_scatter(g, "dp", scatter_dimension=1, tiled=True)
        return lax.psum_scatter(part, "tensor", scatter_dimension=0, tiled=True)[0]

    return [share(g).astype(F32) for g in grads]


def with_halo(rows, parts):
    forward = [(i, i + 1) for i in range(parts - 1)]
    backward = [(i + 1, i) for i in range(parts - 1)]
    before = lax.ppermute(rows[-HALO:], "tensor", forward)
    after = lax.ppermute(rows[:HALO], "tensor", backward)
    return jnp.concatenate((before, rows, after), axis=0)


def local_plain(
    parts,
    tokens,
    segments,
    mask_grad,
    gain_one,
    attend_weight,
    output_weight,
    gain_two,
    up_weight,
    down_weight,
    patch_weight,
    class_weight,
    class_embed,
    *moments,
):
    means, squares = moments[:9], moments[9:]
    own = tokens.shape[0]
    width = tokens.shape[1]
    classes = class_embed.shape[0]
    dp_index = lax.axis_index("dp")
    tensor_index = lax.axis_index("tensor")
    low = lambda v: v.astype(BF)

    shard_a = jnp.concatenate((low(attend_weight), low(output_weight).T), axis=1)
    shard_u = low(up_weight)
    shard_d = low(down_weight).T
    shard_p = jnp.concatenate((low(patch_weight), low(class_weight)), axis=1)
    rows_e = -(-(classes + 2) // 32) * 32
    shard_e = jnp.zeros((rows_e, class_embed.shape[1]), BF)
    shard_e = shard_e.at[:classes].set(low(class_embed))
    shard_e = shard_e.at[classes].set(low(gain_one)).at[classes + 1].set(low(gain_two))
    full_a, full_u, full_d, full_p, full_e = gather_plain(
        (shard_a, shard_u, shard_d, shard_p), shard_e
    )
    full_a, full_u, full_d, full_p = (
        v.reshape(v.shape[0], width, v.shape[-1]) for v in (full_a, full_u, full_d, full_p)
    )
    embed_rows = full_e.transpose(1, 0, 2).reshape(rows_e, width)
    embed = embed_rows[:classes]
    gain_first = embed_rows[classes].astype(F32)[None]
    gain_second = embed_rows[classes + 1].astype(F32)[None]

    cut = attend_weight.shape[1]
    heads = cut // (3 * HD)
    w_attend, w_output = full_a[:, :, :cut], full_a[:, :, cut:]
    narrow = patch_weight.shape[1]
    w_patch, w_class = full_p[:, :, :narrow], full_p[:, :, narrow:]
    w_patch = w_patch.transpose(1, 0, 2).reshape(width, -1)
    w_class = w_class.transpose(1, 0, 2).reshape(width, -1)

    window = with_halo(tokens, parts)
    token_wide = window.astype(F32)
    xhat_one, inverse_one = norm_parts(token_wide)
    norm_one = low(xhat_one * gain_first)
    joint = jnp.einsum("sd,tdn->stn", norm_one, w_attend, preferred_element_type=F32)
    joint = low(joint).reshape(own + 2 * HALO, parts * heads, 3, HD)
    queries, keys, values = joint[:, :, 0], joint[:, :, 1], joint[:, :, 2]
    padded = jnp.pad(segments[0], HALO, constant_values=-1)
    seg = lax.dynamic_slice_in_dim(padded, tensor_index * own, own + 2 * HALO, 0)
    scores = jnp.einsum("qhd,khd->hqk", queries, keys, preferred_element_type=F32) * HD**-0.5
    scores = jnp.where(seg[None, :, None] == seg[None, None, :], scores, masked_score)
    exponent = jnp.exp(scores - jnp.max(scores, axis=-1, keepdims=True))
    prob = exponent / jnp.sum(exponent, axis=-1, keepdims=True)
    prob_low = low(prob)
    mine = slice(HALO, HALO + own)
    attended = jnp.einsum(
        "hqk,khd->qhd", prob_low[:, mine], values, preferred_element_type=F32
    )
    attended = low(attended).reshape(own, parts, heads * HD)
    resid_one = token_wide[mine] + jnp.einsum(
        "stn,tdn->sd", attended, w_output, preferred_element_type=F32
    )
    xhat_two, inverse_two = norm_parts(resid_one)
    norm_two = low(xhat_two * gain_second)
    hidden_pre = jnp.einsum("sd,tdn->stn", norm_two, full_u, preferred_element_type=F32)
    hidden, gelu_back = jax.vjp(lambda v: jax.nn.gelu(v, approximate=False), hidden_pre)
    hidden = low(hidden)
    resid_two = resid_one + jnp.einsum(
        "stn,tdn->sd", hidden, full_d, preferred_element_type=F32
    )
    resid_low = low(resid_two)
    patch_feat = dot(resid_low, w_patch)
    patch_wide, patch_inverse = unit_parts(patch_feat)
    patch_unit = low(patch_wide)
    class_feat = dot(embed, w_class)
    class_wide, class_inverse = unit_parts(class_feat)
    class_unit = low(class_wide)
    products = dot(patch_unit, class_unit, ((1,), (1,)))
    masks, mask_inverse = norm_parts(products)
    d_products = low(norm_back(mask_grad, masks, mask_inverse))
    d_class_unit = lax.psum(dot(d_products, patch_unit, ((0,), (0,))), ("dp", "tensor"))
    d_patch_unit = dot(d_products, class_unit)
    d_patch_feat = low(unit_back(d_patch_unit, patch_wide, patch_inverse))
    grad_patch = dot(resid_low, d_patch_feat, ((0,), (0,)))
    d_resid_two = dot(d_patch_feat, w_patch, ((1,), (1,)))
    d_branch_two = low(d_resid_two)
    d_hidden = jnp.einsum("sd,tdn->stn", d_branch_two, full_d, preferred_element_type=F32)
    grad_down = jnp.einsum("sd,stn->tdn", d_branch_two, hidden, preferred_element_type=F32)
    d_hidden_pre = low(gelu_back(d_hidden)[0])
    grad_up = jnp.einsum("sd,stn->tdn", norm_two, d_hidden_pre, preferred_element_type=F32)
    d_norm_two = jnp.einsum("stn,tdn->sd", d_hidden_pre, full_u, preferred_element_type=F32)
    d_resid_one = d_resid_two + norm_back(d_norm_two * gain_second, xhat_two, inverse_two)
    grad_gain_two = jnp.sum(d_norm_two * xhat_two, axis=0)
    d_branch_one = with_halo(low(d_resid_one), parts)
    d_attended = low(
        jnp.einsum("sd,tdn->stn", d_branch_one, w_output, preferred_element_type=F32)
    )
    grad_output = jnp.einsum(
        "sd,stn->tdn", d_branch_one[mine], attended, preferred_element_type=F32
    )
    d_attended = d_attended.reshape(own + 2 * HALO, parts * heads, HD)
    d_prob = jnp.einsum("qhd,khd->hqk", d_attended, values, preferred_element_type=F32)
    delta = jnp.sum(prob * d_prob, axis=-1, keepdims=True)
    d_scores = low(prob * (d_prob - delta))
    d_query = jnp.einsum(
        "hqk,khd->qhd", d_scores[:, mine], keys, preferred_element_type=F32
    )
    d_key = jnp.einsum(
        "hqk,qhd->khd", d_scores[:, :, mine], queries, preferred_element_type=F32
    )
    d_value = jnp.einsum(
        "hqk,qhd->khd", prob_low[:, :, mine], d_attended, preferred_element_type=F32
    )
    d_joint = low(
        jnp.stack((d_query * HD**-0.5, d_key * HD**-0.5, d_value), axis=2)
    ).reshape(own, parts, cut)
    grad_attend = jnp.einsum(
        "sd,stn->tdn", norm_one[mine], d_joint, preferred_element_type=F32
    )
    d_norm_one = jnp.einsum("stn,tdn->sd", d_joint, w_attend, preferred_element_type=F32)
    token_grad = d_resid_one + norm_back(
        d_norm_one * gain_first, xhat_one[mine], inverse_one[mine]
    )
    grad_gain_one = jnp.sum(d_norm_one * xhat_one[mine], axis=0)

    grad_patch = grad_patch.reshape(width, parts, narrow).transpose(1, 0, 2)
    share_p, share_d, share_u, share_a = scatter_plain(
        [
            grad_patch,
            grad_down,
            grad_up,
            jnp.concatenate((grad_attend, grad_output), axis=2),
        ]
    )
    gains = lax.psum((grad_gain_one, grad_gain_two), ("dp", "tensor"))
    step = gain_one.shape[0]
    share_one, share_two = (lax.dynamic_slice_in_dim(g, dp_index * step, step, 0) for g in gains)
    d_class_feat = low(unit_back(d_class_unit, class_wide, class_inverse))
    d_class_own = lax.dynamic_slice_in_dim(d_class_feat, tensor_index * narrow, narrow, 1)
    share_class = dot(low(class_embed), d_class_own, ((0,), (0,)))
    class_rows = lax.dynamic_slice_in_dim(w_class, dp_index * step, step, 0)
    share_embed = dot(d_class_feat, class_rows, ((1,), (1,)))
    return finish(
        masks,
        token_grad,
        (
            share_one,
            share_a[:, :cut],
            share_a[:, cut:].T,
            share_two,
            share_u,
            share_d.T,
            share_p,
            share_class,
            share_embed,
        ),
        (
            gain_one,
            attend_weight,
            output_weight,
            gain_two,
            up_weight,
            down_weight,
            patch_weight,
            class_weight,
            class_embed,
        ),
        means,
        squares,
    )


def local_kernels(tokens, segments, mask_grad, *arrays):
    def turned(group):
        return (*group[:5], group[5].T, *group[6:])

    params, means, squares = (turned(arrays[n : n + 9]) for n in (0, 9, 18))
    results = step_call(tokens, segments, mask_grad.T, params)
    masks, token_grad, *new = update_call(results, params, means, squares)
    new = [n.reshape(p.shape) for n, p in zip(new, params * 2)]
    return (masks.T, token_grad, *turned(new[:9]), *turned(new[9:]))


def solution(mesh):
    parts = mesh.shape["tensor"]
    custom = mesh.shape["dp"] == 8 and parts == 4
    params = (
        P("dp"),
        P("dp", "tensor"),
        P("tensor", "dp"),
        P("dp"),
        P("dp", "tensor"),
        P("tensor", "dp"),
        P("dp", "tensor"),
        P("dp", "tensor"),
        P(None, "dp"),
    )
    rows = P(("dp", "tensor"), None)
    return jax.shard_map(
        local_kernels if custom else functools.partial(local_plain, parts),
        mesh=mesh,
        in_specs=(rows, P("dp", None), rows) + params * 3,
        out_specs=(rows, rows) + params * 2,
        check_vma=False,
    )
```

```python
import functools

import jax
import jax.numpy as jnp
from jax import lax
from jax.experimental import pallas as pl
from jax.experimental.pallas import tpu as pltpu
from jax.sharding import PartitionSpec as P

HD = 64
HALO = 128
BF = jnp.bfloat16
F32 = jnp.float32
MESH = pl.DeviceIdType.MESH
VMEM_LIMIT = 64 * 1024 * 1024 - 512 * 1024

epsilon_norm = 1e-05
epsilon_unit = 1e-06
masked_score = -1000000000.0
first_decay = 0.9
second_decay = 0.999
first_fix = 0.99997343860112
second_fix = 0.09520785288629
adam_epsilon = 1e-08
block_scale = 0.65
weight_decay = 0.05


def dot(left, right, dims=((1,), (0,))):
    return lax.dot_general(left, right, (dims, ((), ())), preferred_element_type=F32)


def layer_norm(values, gain):
    center = values - jnp.mean(values, axis=-1, keepdims=True)
    spread = jnp.mean(center * center, axis=-1, keepdims=True)
    return center * lax.rsqrt(spread + epsilon_norm) * gain


def norm_parts(values):
    center = values - jnp.mean(values, axis=-1, keepdims=True)
    spread = jnp.mean(center * center, axis=-1, keepdims=True)
    inverse = lax.rsqrt(spread + epsilon_norm)
    return center * inverse, inverse


def norm_back(gradient, xhat, inverse):
    return inverse * (
        gradient
        - jnp.mean(gradient, axis=-1, keepdims=True)
        - xhat * jnp.mean(gradient * xhat, axis=-1, keepdims=True)
    )


def unit_parts(values):
    inverse = lax.rsqrt(jnp.sum(values * values, axis=-1, keepdims=True) + epsilon_unit)
    return values * inverse, inverse


def unit_back(gradient, unit, inverse):
    return inverse * (gradient - unit * jnp.sum(unit * gradient, axis=-1, keepdims=True))


def adamw_update(current, gradient, mean_old, square_old, step_scale, decay_rate):
    mean_new = first_decay * mean_old + (1.0 - first_decay) * gradient
    square_new = second_decay * square_old + (1.0 - second_decay) * gradient * gradient
    moved = mean_new / first_fix / (jnp.sqrt(square_new / second_fix) + adam_epsilon)
    return (step_scale * (moved + decay_rate * current), mean_new)


class Place:
    def __init__(self):
        dp, z = lax.axis_index("dp"), lax.axis_index("tensor")
        self.dp, self.z = dp, z
        self.core, self.col, self.row = dp % 2, (dp // 2) % 2, dp // 4
        self.x = (dp + 2 * (1 - 2 * self.col), z)
        self.y = (dp + 4 * (1 - 2 * self.row), z)
        self.sibling = (dp + 1 - 2 * self.core, z)

    def along(self, j):
        return (self.dp, (self.z + j) % 4)


def greet(place):
    barrier = pltpu.get_barrier_semaphore()
    targets = [place.x, place.y, place.sibling] + [place.along(j) for j in (1, 2, 3)]
    for target in targets:
        pl.semaphore_signal(barrier, inc=1, device_id=target, device_id_type=MESH)
    pl.semaphore_wait(barrier, 6)


def remote(source, target_ref, sends, receives, device):
    return pltpu.make_async_remote_copy(
        src_ref=source,
        dst_ref=target_ref,
        send_sem=sends,
        recv_sem=receives,
        device_id=device,
        device_id_type=MESH,
    )


class Line:
    def __init__(self, place, full, sends, receives):
        self.copies = [
            remote(
                full.at[place.z], full.at[place.z], sends.at[k], receives.at[k], place.along(k + 1)
            )
            for k in range(3)
        ]

    def start(self):
        for copy in self.copies:
            copy.start()

    def wait(self):
        for copy in self.copies:
            copy.wait_recv()

    def drain(self):
        for copy in self.copies:
            copy.wait_send()


class Gather:
    def __init__(self, place, full, sends, receives, w):
        self.place, self.full, self.w = place, full, w
        self.sends, self.receives = sends, receives
        self.flat = len(full.shape) == 5

    def copy(self, k):
        place, full = self.place, self.full
        row, col, core, z = place.row, place.col, place.core, place.z
        if k < 3:
            view, target = full.at[z - k, row, col, core], place.along(1)
        elif k >= 20:
            view, target = full.at[z + k - 20, row, col, core], place.along(3)
        elif k < 15:
            j = (k - 3) // 3
            if self.flat:
                view = full.at[row, col, core]
            else:
                view = full.at[(z + j) % 4, row, col, core]
            target = (place.x, place.y, place.sibling)[(k - 3) % 3]
        elif k < 17:
            spot = (row, 1 - col, core) if k == 15 else (1 - row, col, core)
            if self.flat:
                half = full.shape[3] // 2
                view = full.at[spot + (pl.ds((k - 15) * half, half),)]
            else:
                view = full.at[(pl.ds((k - 15) * 2, 2),) + spot]
            target = place.y if k == 15 else place.x
        else:
            spot = ((row, 1 - col, core), (1 - row, col, core), (1 - row, 1 - col, core))[k - 17]
            view = full.at[spot] if self.flat else full.at[(slice(None),) + spot]
            target = place.sibling
        return remote(view, view, self.sends.at[self.w, k], self.receives.at[self.w, k], target)

    def pieces(self):
        return range(1 if self.flat else 4)

    def start(self):
        for k in (3, 4, 5):
            self.copy(k).start()

    def line(self):
        z = self.place.z

        @pl.when(z < 3)
        def _():
            self.copy(0).start()

        @pl.when(z > 0)
        def _():
            self.copy(20).start()

    def hop(self, h):
        z = self.place.z

        @pl.when(z >= h)
        def _():
            self.copy(h - 1).wait_recv()
            if h < 3:

                @pl.when(z < 3)
                def _():
                    self.copy(h).start()

            for k in range(3):
                self.copy(3 + 3 * (4 - h) + k).start()

        @pl.when(z + h <= 3)
        def _():
            self.copy(19 + h).wait_recv()
            if h < 3:

                @pl.when(z > 0)
                def _():
                    self.copy(20 + h).start()

            for k in range(3):
                self.copy(3 + 3 * h + k).start()

    def forward(self):
        for j in self.pieces():
            self.copy(3 + 3 * j).wait_recv()
        self.copy(15).start()
        self.copy(17).start()
        for j in self.pieces():
            self.copy(4 + 3 * j).wait_recv()
        self.copy(16).start()
        self.copy(18).start()

    def across(self):
        self.copy(15).wait_recv()
        self.copy(16).wait_recv()
        self.copy(19).start()

    def last(self):
        for j in self.pieces():
            self.copy(5 + 3 * j).wait_recv()
        for k in (17, 18, 19):
            self.copy(k).wait_recv()

    def drain(self):
        z = self.place.z
        if not self.flat:
            for k in range(3):

                @pl.when((z < 3) & (z >= k))
                def _(k=k):
                    self.copy(k).wait_send()

                @pl.when((z > 0) & (z + k <= 3))
                def _(k=k):
                    self.copy(20 + k).wait_send()

        for j in self.pieces():
            for k in range(3):
                self.copy(3 + 3 * j + k).wait_send()
        for k in range(15, 20):
            self.copy(k).wait_send()


class PlaneGather:
    def __init__(self, place, full, sends, receives, w):
        self.place, self.full, self.w = place, full, w
        self.sends, self.receives = sends, receives

    def copy(self, k):
        place, full = self.place, self.full
        row, col, core, z = place.row, place.col, place.core, place.z
        half = full.shape[4] // 2
        if k < 3:
            view, target = full.at[z, row, col, core], (place.x, place.y, place.sibling)[k]
        elif k == 3:
            view, target = full.at[z, row, 1 - col, core, 0:half], place.y
        elif k == 4:
            view, target = full.at[z, 1 - row, col, core, half : 2 * half], place.x
        elif k < 8:
            spot = ((row, 1 - col), (1 - row, col), (1 - row, 1 - col))[k - 5]
            view, target = full.at[z, spot[0], spot[1], core], place.sibling
        elif k < 11:
            view, target = full.at[z - (k - 8), :, :, core], place.along(1)
        elif k < 14:
            view, target = full.at[z + k - 11, :, :, core], place.along(3)
        else:
            view, target = full.at[(z + k - 13) % 4, :, :, core], place.sibling
        return remote(view, view, self.sends.at[self.w, k], self.receives.at[self.w, k], target)

    def start(self):
        for k in range(3):
            self.copy(k).start()

    def forward(self):
        self.copy(0).wait_recv()
        self.copy(3).start()
        self.copy(5).start()
        self.copy(1).wait_recv()
        self.copy(4).start()
        self.copy(6).start()

    def across(self):
        z = self.place.z
        self.copy(3).wait_recv()
        self.copy(4).wait_recv()

        @pl.when(z < 3)
        def _():
            self.copy(8).start()

        @pl.when(z > 0)
        def _():
            self.copy(11).start()

        self.copy(7).start()

    def hop(self, h):
        z = self.place.z

        @pl.when(z >= h)
        def _():
            self.copy(7 + h).wait_recv()
            if h < 3:

                @pl.when(z < 3)
                def _():
                    self.copy(8 + h).start()

            self.copy(13 + 4 - h).start()

        @pl.when(z + h <= 3)
        def _():
            self.copy(10 + h).wait_recv()
            if h < 3:

                @pl.when(z > 0)
                def _():
                    self.copy(11 + h).start()

            self.copy(13 + h).start()

    def last(self):
        for k in (2, 5, 6, 7, 14, 15, 16):
            self.copy(k).wait_recv()

    def drain(self):
        z = self.place.z
        for k in (0, 1, 2, 3, 4, 5, 6, 7, 14, 15, 16):
            self.copy(k).wait_send()
        for k in range(3):

            @pl.when((z < 3) & (z >= k))
            def _(k=k):
                self.copy(8 + k).wait_send()

            @pl.when((z > 0) & (z + k <= 3))
            def _(k=k):
                self.copy(11 + k).wait_send()


class Scatter:
    def __init__(self, place, grad, buffers, sends, receives, w):
        self.place, self.grad, self.w = place, grad, w
        self.sends, self.receives = sends, receives
        self.r1, self.r2a, self.r2b, self.r3a, self.r3b, self.r4 = buffers

    def copy(self, k):
        place, r1 = self.place, self.r1
        row, col, core = place.row, place.col, place.core
        if k in (0, 8):
            half = slice(0, 2) if k == 0 else slice(2, 4)
            pair = (self.grad.at[half, :, :, 1 - core], r1.at[half], place.sibling)
        elif k == 1:
            pair = (r1.at[0:2, :, 1 - col], self.r2a, place.x)
        elif k == 2:
            pair = (r1.at[2:4, 1 - row], self.r2b, place.y)
        elif k == 3:
            pair = (r1.at[0:2, 1 - row, col], self.r3a, place.y)
        elif k == 4:
            pair = (r1.at[2:4, row, 1 - col], self.r3b, place.x)
        else:
            peer = place.along(k - 4)
            pair = (r1.at[peer[1], row, col], self.r4.at[k - 5], peer)
        return remote(
            pair[0], pair[1], self.sends.at[self.w, k], self.receives.at[self.w, k], pair[2]
        )

    def add(self, index, other):
        ref = self.r1
        ref[index] = (ref[index].astype(F32) + other.astype(F32)).astype(ref.dtype)

    def start(self, halves=(0, 1)):
        for half in halves:
            self.copy(8 * half).start()

    def planes(self, halves=(0, 1)):
        core = self.place.core
        for half in halves:
            self.copy(8 * half).wait_recv()

            def step(i, carry):
                t, y = 2 * half + i // 2, i % 2
                self.add((t, y), self.grad[t, y, :, core])
                return carry

            lax.fori_loop(0, 4, step, 0)

    def spread(self, halves=(0, 1)):
        for half in halves:
            self.copy(1 + half).start()

    def lines(self):
        col, row = self.place.col, self.place.row
        self.copy(1).wait_recv()
        for t in range(2):
            for y in range(2):
                self.add((t, y, col), self.r2a[t, y])
        self.copy(3).start()
        self.copy(2).wait_recv()
        for t in range(2):
            for x in range(2):
                self.add((2 + t, row, x), self.r2b[t, x])
        self.copy(4).start()

    def points(self):
        col, row = self.place.col, self.place.row
        self.copy(3).wait_recv()
        for t in range(2):
            self.add((t, row, col), self.r3a[t])
        self.copy(4).wait_recv()
        for t in range(2):
            self.add((2 + t, row, col), self.r3b[t])
        for k in (5, 6, 7):
            self.copy(k).start()

    def result(self):
        place = self.place
        for k in (5, 6, 7):
            self.copy(k).wait_recv()
        total = self.r1[place.z, place.row, place.col].astype(F32)
        for j in range(3):
            total = total + self.r4[j].astype(F32)
        return total

    def drain(self):
        for k in range(9):
            self.copy(k).wait_send()


class LineScatter:
    def __init__(self, place, grad, buffers, sends, receives, w):
        self.place, self.grad, self.w = place, grad, w
        self.sends, self.receives = sends, receives
        self.r1, self.r2a, self.r2b, self.r3a, self.r3b, self.r4 = buffers

    def copy(self, k):
        place, r1 = self.place, self.r1
        row, col, core, z = place.row, place.col, place.core, place.z
        half = r1.shape[3] // 2
        if k == 0:
            pair = (self.grad.at[:, :, :, 1 - core], r1, place.sibling)
        elif k == 1:
            pair = (r1.at[z, :, 1 - col, 0:half], self.r2a, place.x)
        elif k == 2:
            pair = (r1.at[z, 1 - row, :, half : 2 * half], self.r2b, place.y)
        elif k == 3:
            pair = (r1.at[z, 1 - row, col, 0:half], self.r3a, place.y)
        elif k == 4:
            pair = (r1.at[z, row, 1 - col, half : 2 * half], self.r3b, place.x)
        else:
            peer = place.along(k - 4)
            pair = (r1.at[peer[1]], self.r4.at[k - 5], peer)
        return remote(
            pair[0], pair[1], self.sends.at[self.w, k], self.receives.at[self.w, k], pair[2]
        )

    def add(self, index, other):
        ref = self.r1
        ref[index] = (ref[index].astype(F32) + other.astype(F32)).astype(ref.dtype)

    def start(self):
        self.copy(0).start()

    def planes(self):
        core = self.place.core
        self.copy(0).wait_recv()

        def step(i, carry):
            t, y = i // 2, i % 2
            self.add((t, y), self.grad[t, y, :, core])
            return carry

        lax.fori_loop(0, 8, step, 0)
        for k in (5, 6, 7):
            self.copy(k).start()

    def depth(self):
        z = self.place.z
        for k in (5, 6, 7):
            self.copy(k).wait_recv()
        for y in range(2):
            for x in range(2):
                value = self.r1[z, y, x].astype(F32)
                for j in range(3):
                    value = value + self.r4[j, y, x].astype(F32)
                self.r1[z, y, x] = value.astype(self.r1.dtype)
        self.copy(1).start()
        self.copy(2).start()

    def lines(self):
        place, half = self.place, self.r1.shape[3] // 2
        self.copy(1).wait_recv()
        for y in range(2):
            self.add((place.z, y, place.col, slice(0, half)), self.r2a[y])
        self.copy(3).start()
        self.copy(2).wait_recv()
        for x in range(2):
            self.add((place.z, place.row, x, slice(half, 2 * half)), self.r2b[x])
        self.copy(4).start()

    def result(self, out):
        place, half = self.place, self.r1.shape[3] // 2
        for k, part in ((3, slice(0, half)), (4, slice(half, 2 * half))):
            self.copy(k).wait_recv()
            other = self.r3a if k == 3 else self.r3b
            mine = self.r1[place.z, place.row, place.col, part]
            out[part] = mine.astype(F32) + other[...].astype(F32)

    def drain(self):
        for k in range(8):
            self.copy(k).wait_send()


def scatter_buffers(rows, cols, dtype):
    return [
        pltpu.VMEM((4, 2, 2, rows, cols), dtype),
        pltpu.VMEM((2, 2, rows, cols), dtype),
        pltpu.VMEM((2, 2, rows, cols), dtype),
        pltpu.VMEM((2, rows, cols), dtype),
        pltpu.VMEM((2, rows, cols), dtype),
        pltpu.VMEM((3, rows, cols), dtype),
    ]


HEAD_SET = 3
SPAN = 3 * HD
CUT = HEAD_SET * SPAN
TILE_ROWS, TILE_COLS = 16, 256


def whole(value):
    return value.reshape(-1, value.shape[-1])


def gelu_parts(values):
    cumulative = 0.5 * (1.0 + lax.erf(values * 0.7071067811865476))
    density = 0.3989422804014327 * jnp.exp(-0.5 * values * values)
    return values * cumulative, cumulative + values * density


class Halo:
    def __init__(self, place, window, own, semaphores):
        edge = HALO + own
        self.place, self.window, self.edge = place, window, edge
        self.down = remote(
            window.at[pl.ds(HALO, HALO)],
            window.at[pl.ds(edge, HALO)],
            semaphores.at[0],
            semaphores.at[1],
            place.along(3),
        )
        self.up = remote(
            window.at[pl.ds(own, HALO)],
            window.at[pl.ds(0, HALO)],
            semaphores.at[2],
            semaphores.at[3],
            place.along(1),
        )

    def start(self):
        z, window = self.place.z, self.window
        blank = jnp.zeros((HALO, window.shape[1]), window.dtype)

        @pl.when(z > 0)
        def _():
            self.down.start()

        @pl.when(z < 3)
        def _():
            self.up.start()

        @pl.when(z == 0)
        def _():
            window[0:HALO] = blank

        @pl.when(z == 3)
        def _():
            window[self.edge : self.edge + HALO] = blank

    def wait(self):
        z = self.place.z

        @pl.when(z < 3)
        def _():
            self.down.wait_recv()

        @pl.when(z > 0)
        def _():
            self.up.wait_recv()

    def drain(self):
        z = self.place.z

        @pl.when(z > 0)
        def _():
            self.down.wait_send()

        @pl.when(z < 3)
        def _():
            self.up.wait_send()


def loader(inputs, places, semaphores):
    return [
        pltpu.make_async_copy(source, target, semaphores.at[n])
        for n, (source, target) in enumerate(zip(inputs, places))
    ]


def step_kernel(*refs):
    inputs, outputs, held = refs[:12], refs[12:22], refs[22:34]
    (
        tokens,
        segments,
        mask_grad,
        gain_one,
        attend_weight,
        output_weight,
        gain_two,
        up_weight,
        down_weight,
        patch_weight,
        class_weight,
        class_embed,
    ) = held
    results = refs[34:44]
    (
        masks,
        d_resid,
        share_p,
        share_d,
        share_u,
        share_a,
        share_n,
        class_all,
        class_row,
        class_sum,
    ) = results
    (
        full_a,
        full_u,
        full_d,
        full_p,
        full_c,
        full_e,
        grad_d,
        grad_u,
        grad_p,
        grad_n,
        grad_c,
        joint,
        attended,
        resid_one,
        norm_two,
        hidden,
        slope,
        total,
        window,
        norm_one,
        embed,
        embed_wide,
        resid_low,
        unit_low,
        class_low,
        probs,
        stack,
        seg_wide,
        seg_col,
        seg_row,
        class_wide,
        r4_a,
    ) = refs[44:76]
    buffers = refs[76:106]
    (
        gather_sends,
        gather_receives,
        scatter_sends,
        scatter_receives,
        line_sems,
        halo_sems,
        in_sems,
        out_sems,
    ) = refs[106:]
    loads = loader(inputs, held, in_sems)
    stores = loader(results, outputs, out_sems)
    for n in (11, 3, 6, 0, 4, 5, 10, 7, 8, 9, 1, 2):
        loads[n].start()

    place = Place()
    z, row, col, core = place.z, place.row, place.col, place.core
    own, width = tokens.shape
    span = own + 2 * HALO
    piece = width // 8
    narrow = patch_weight.shape[1]
    classes = class_embed.shape[0]
    mine = slice(HALO, HALO + own)
    ge, ga, gc, gu, gd, gp, gs = (
        (PlaneGather if full is full_p else Gather)(
            place, full, gather_sends, gather_receives, w
        )
        for w, full in enumerate((full_e, full_a, full_c, full_u, full_d, full_p, class_sum))
    )
    sp, sd, su, sn, sc = (
        (LineScatter if g is grad_p else Scatter)(
            place, g, buffers[6 * w : 6 * w + 6], scatter_sends, scatter_receives, w
        )
        for w, g in enumerate((grad_p, grad_d, grad_u, grad_n, grad_c))
    )
    grad_a = full_u
    third = piece // 3
    parts = [slice(n * third, (n + 1) * third) for n in range(3)]
    sa = [
        Scatter(
            place,
            grad_a.at[:, :, :, :, part],
            (
                full_d.at[:, :, :, 0, part],
                full_d.at[0:2, :, 0, 1, part],
                full_d.at[2:4, :, 0, 1, part],
                full_d.at[0:2, 0, 1, 1, part],
                full_d.at[2:4, 0, 1, 1, part],
                r4_a.at[:, part],
            ),
            scatter_sends,
            scatter_receives,
            5 + n,
        )
        for n, part in enumerate(parts)
    ]
    line_row = Line(place, class_row, line_sems.at[0], line_sems.at[1])
    line_all = Line(place, class_all, line_sems.at[2], line_sems.at[3])

    embed_wide[...] = jnp.zeros_like(embed_wide)
    for n in (11, 3, 6):
        loads[n].wait()
    embed_wide[0:classes] = class_embed[...]
    embed_wide[classes : classes + 1] = gain_one[...]
    embed_wide[classes + 1 : classes + 2] = gain_two[...]
    full_e[row, col, core] = embed_wide[...].astype(BF)
    greet(place)
    ge.start()
    loads[0].wait()
    window[mine] = tokens[...]
    halo = Halo(place, window, own, halo_sems.at[0])
    halo.start()
    loads[4].wait()
    loads[5].wait()
    full_a[z, row, col, core, :, 0:CUT] = attend_weight[...].astype(BF)
    full_a[z, row, col, core, :, CUT:] = output_weight[...].T.astype(BF)
    ga.start()
    ga.line()
    loads[10].wait()
    full_c[row, col, core] = class_weight[...].astype(BF)
    gc.start()
    loads[7].wait()
    full_u[z, row, col, core] = up_weight[...].astype(BF)
    gu.start()
    gu.line()
    loads[9].wait()
    full_p[z, row, col, core] = patch_weight[...].astype(BF)
    gp.start()
    loads[8].wait()
    full_d[z, row, col, core] = down_weight[...].astype(BF)
    gd.start()
    ga.hop(1)

    loads[1].wait()
    loads[2].wait()
    seg_wide[...] = jnp.full_like(seg_wide, -1.0)
    seg_wide[:, HALO : HALO + segments.shape[1]] = segments[...].astype(F32)
    seg_row[...] = seg_wide[:, pl.ds(pl.multiple_of(z * own, 128), span)]
    seg_col[...] = jnp.broadcast_to(seg_row[...], (8, span)).T[:, 0:1]
    gc.forward()
    gd.line()
    ge.forward()
    gu.hop(1)
    ge.across()
    ga.hop(2)
    ga.hop(3)
    ge.last()
    halo.wait()
    for d in range(8):
        embed[:, d * piece : (d + 1) * piece] = full_e[d // 4, (d // 2) % 2, d % 2]
    gains = embed[classes : classes + 2, :].astype(F32)
    gain_first, gain_second = gains[0:1], gains[1:2]

    def first_norm(i, carry):
        rows = pl.ds(pl.multiple_of(i * 128, 128), 128)
        xhat, _ = norm_parts(window[rows].astype(F32))
        norm_one[rows] = (xhat * gain_first).astype(BF)
        return carry

    lax.fori_loop(0, span // 128, first_norm, 0)
    gp.forward()
    gu.hop(2)
    gp.across()
    ga.forward()
    gc.across()
    gd.hop(1)
    gc.last()
    ga.across()
    class_all[z] = dot(embed[...], whole(full_c[...])).astype(BF)
    line_all.start()
    class_row[z] = class_weight[...].astype(BF)
    line_row.start()
    ga.last()
    gd.hop(2)
    def project(t, carry):
        joint[t] = dot(norm_one[...], whole(full_a[t])[:, :CUT]).astype(BF)
        return carry

    lax.fori_loop(0, 4, project, 0)
    gu.hop(3)
    gu.forward()
    gp.hop(1)
    gd.hop(3)
    probs[...] = jnp.zeros_like(probs)

    def attend(t, carry):
        for h in range(HEAD_SET):
            q_cols = slice(h * SPAN, h * SPAN + HD)
            k_cols = slice(h * SPAN + HD, h * SPAN + 2 * HD)
            v_cols = slice(h * SPAN + 2 * HD, h * SPAN + 3 * HD)
            for b in range(4):
                rows = slice(b * 128, (b + 1) * 128)
                near = slice(max(b - 1, 0) * 128, min(b + 2, 4) * 128)
                scores = dot(joint[t, rows, q_cols], joint[t, near, k_cols], ((1,), (1,)))
                match = seg_col[rows] == seg_row[:, near]
                scores = jnp.where(match, scores * HD**-0.5, masked_score)
                exponent = jnp.exp(scores - jnp.max(scores, axis=-1, keepdims=True))
                row_total = jnp.sum(exponent, axis=-1, keepdims=True)
                prob = (exponent / row_total).astype(BF)
                probs[t, h, rows, near] = prob
                if b in (1, 2):
                    attended[t, (b - 1) * 128 : b * 128, h * HD : (h + 1) * HD] = dot(
                        prob, joint[t, near, v_cols]
                    ).astype(BF)

        @pl.when(t == 0)
        def _():
            gp.hop(2)

        @pl.when(t == 1)
        def _():
            gu.across()
            gp.hop(3)

        @pl.when(t == 2)
        def _():
            gd.forward()

        @pl.when(t == 3)
        def _():
            gp.last()

        return carry

    lax.fori_loop(0, 4, attend, 0)
    resid_one[...] = tokens[...].astype(F32)

    def output(t, carry):
        resid_one[...] += dot(attended[t], whole(full_a[t])[:, CUT:], ((1,), (1,)))
        return carry

    lax.fori_loop(0, 4, output, 0)
    xhat, _ = norm_parts(resid_one[...])
    norm_two[...] = (xhat * gain_second).astype(BF)
    gu.last()
    def expand(t, carry):
        value, derivative = gelu_parts(dot(norm_two[...], whole(full_u[t])))
        hidden[t] = value.astype(BF)
        slope[t] = derivative.astype(BF)

        @pl.when(t == 3)
        def _():
            gd.across()
            gd.last()

        return carry

    lax.fori_loop(0, 4, expand, 0)
    total[...] = resid_one[...]

    def contract(t, carry):
        total[...] += dot(hidden[t], whole(full_d[t]), ((1,), (1,)))
        return carry

    lax.fori_loop(0, 4, contract, 0)
    resid_low[...] = total[...].astype(BF)
    line_all.wait()
    stores[7].start()
    line_row.wait()
    stores[8].start()
    class_square = jnp.zeros((class_all.shape[1], 1), F32)
    for t in range(4):
        value = class_all[t].astype(F32)
        class_square += jnp.sum(value * value, axis=-1, keepdims=True)
    class_inverse = lax.rsqrt(class_square + epsilon_unit)
    for t in range(4):
        class_low[t] = (class_all[t].astype(F32) * class_inverse).astype(BF)

    square = jnp.zeros((own, 1), F32)
    pieces = []
    for t in range(4):
        value = dot(resid_low[...], whole(full_p[t]))
        square += jnp.sum(value * value, axis=-1, keepdims=True)
        pieces.append(value)
    inverse = lax.rsqrt(square + epsilon_unit)
    products = jnp.zeros((class_low.shape[1], own), F32)
    for t in range(4):
        pieces[t] = pieces[t] * inverse
        unit_low[t] = pieces[t].astype(BF)
        products += dot(class_low[t], unit_low[t], ((1,), (1,)))
    products = products[:classes]
    centred = products - jnp.mean(products, axis=0, keepdims=True)
    spread = jnp.mean(centred * centred, axis=0, keepdims=True)
    mask_inverse = lax.rsqrt(spread + epsilon_norm)
    centred = centred * mask_inverse
    masks[...] = centred
    stores[0].start()
    d_masks = mask_grad[...]
    d_products = mask_inverse * (
        d_masks
        - jnp.mean(d_masks, axis=0, keepdims=True)
        - centred * jnp.mean(d_masks * centred, axis=0, keepdims=True)
    )
    d_products = d_products.astype(BF)
    along = jnp.zeros((own, 1), F32)
    d_pieces = []
    for t in range(4):
        value = dot(d_products, class_low[t, :classes], ((0,), (0,)))
        along += jnp.sum(value * pieces[t], axis=-1, keepdims=True)
        d_pieces.append(value)
    flipped = resid_low[...].T
    for t in range(4):
        d_pieces[t] = (inverse * (d_pieces[t] - pieces[t] * along)).astype(BF)
        grad_p[t] = dot(flipped, d_pieces[t]).astype(BF).reshape(grad_p.shape[1:])
    sp.start()
    d_total = jnp.zeros((own, width), F32)
    for t in range(4):
        d_total += dot(d_pieces[t], whole(full_p[t]), ((1,), (1,)))
    d_resid[...] = d_total
    branch = d_total.astype(BF)
    flipped = branch.T
    sp.planes()

    def down(t, carry):
        grad_d[t] = dot(flipped, hidden[t]).astype(BF).reshape(grad_d.shape[1:])

        @pl.when(t == 1)
        def _():
            sd.start((0,))

        @pl.when(t == 3)
        def _():
            sd.start((1,))
            sd.planes((0,))
            sd.spread((0,))

        return carry

    lax.fori_loop(0, 4, down, 0)
    flipped = norm_two[...].T

    def up(t, carry):
        back = dot(branch, whole(full_d[t])) * slope[t].astype(F32)
        back = back.astype(BF)
        slope[t] = back
        grad_u[t] = dot(flipped, back).astype(BF).reshape(grad_u.shape[1:])

        @pl.when(t == 0)
        def _():
            sd.planes((1,))
            sd.spread((1,))

        return carry

    lax.fori_loop(0, 4, up, 0)
    for transfer in (ge, ga, gc, gu, gd, gp):
        transfer.drain()
    su.start()
    total[...] = jnp.zeros_like(total)

    def narrow_back(t, carry):
        total[...] += dot(slope[t], whole(full_u[t]), ((1,), (1,)))
        return carry

    lax.fori_loop(0, 4, narrow_back, 0)
    su.planes()
    xhat, inverse = norm_parts(resid_one[...])
    gain_two_sum = jnp.sum(total[...] * xhat, axis=0, keepdims=True)
    d_resid[...] += norm_back(total[...] * gain_second, xhat, inverse)
    halo.drain()
    window[mine] = d_resid[...].astype(BF)
    back_halo = Halo(place, window, own, halo_sems.at[1])
    back_halo.start()
    class_wide[...] = jnp.zeros_like(class_wide)
    for t in range(4):
        class_wide[0:classes, t * narrow : (t + 1) * narrow] = dot(d_products, unit_low[t])
    grad_c[...] = jnp.zeros_like(grad_c)
    tiles = width // TILE_COLS
    for i in range(class_wide.shape[0] // TILE_ROWS * tiles):
        r, q = i // tiles, i % tiles
        grad_c[i // 8, (i // 4) % 2, (i // 2) % 2, i % 2] = class_wide[
            r * TILE_ROWS : (r + 1) * TILE_ROWS, q * TILE_COLS : (q + 1) * TILE_COLS
        ].astype(BF)
    sc.start()
    flipped = window[mine].T

    def outer(t, carry):
        block = dot(flipped, attended[t]).astype(BF)
        grad_a[t, :, :, :, :, CUT:] = block.reshape((2, 2, 2, piece, width - CUT))
        return carry

    lax.fori_loop(0, 4, outer, 0)
    sc.planes()
    sc.spread()
    back_halo.wait()

    def attended_back(t, carry):
        value = dot(window[...], whole(full_a[t])[:, CUT:]).astype(BF)
        slope[t, :, 0:narrow] = value[0:own]
        slope[t, :, 256 : 256 + narrow] = value[own:span]
        return carry

    lax.fori_loop(0, 4, attended_back, 0)
    sc.lines()
    sd.lines()
    su.spread()
    stack[...] = jnp.zeros_like(stack)

    def attend_back(t, carry):
        for h in range(HEAD_SET):
            q_cols = slice(h * SPAN, h * SPAN + HD)
            k_cols = slice(h * SPAN + HD, h * SPAN + 2 * HD)
            v_cols = slice(h * SPAN + 2 * HD, h * SPAN + 3 * HD)
            for b in range(4):
                rows = slice(b * 128, (b + 1) * 128)
                low_key, high_key = max(b - 1, 0) * 128, min(b + 2, 4) * 128
                near = slice(low_key, high_key)
                prob = probs[t, h, rows, near].astype(F32)
                d_cols = slice(b // 2 * 256 + h * HD, b // 2 * 256 + (h + 1) * HD)
                d_rows = slice(b % 2 * 128, (b % 2 + 1) * 128)
                d_prob = dot(slope[t, d_rows, d_cols], joint[t, near, v_cols], ((1,), (1,)))
                delta = jnp.sum(prob * d_prob, axis=-1, keepdims=True)
                d_scores = (prob * (d_prob - delta)).astype(BF)
                first, last = max(low_key, HALO), min(high_key, HALO + own)
                stack[rows, first - HALO : last - HALO] = d_scores[
                    :, first - low_key : last - low_key
                ]
                if b in (1, 2):
                    hidden[t, (b - 1) * 128 : b * 128, q_cols] = (
                        dot(d_scores, joint[t, near, k_cols]) * HD**-0.5
                    ).astype(BF)
            hidden[t, :, k_cols] = (
                dot(stack[...], joint[t, :, q_cols], ((0,), (0,))) * HD**-0.5
            ).astype(BF)
            d_value = jnp.zeros((own, HD), F32)
            for half in range(2):
                d_value += dot(
                    probs[t, h, half * own : (half + 1) * own, mine],
                    slope[t, :, half * 256 + h * HD : half * 256 + (h + 1) * HD],
                    ((0,), (0,)),
                )
            hidden[t, :, v_cols] = d_value.astype(BF)

        @pl.when(t == 0)
        def _():
            sc.points()
            sp.depth()

        @pl.when(t == 1)
        def _():
            class_sum[z, row, col, core] = sc.result().astype(BF)
            gs.start()
            gs.line()

        @pl.when(t == 2)
        def _():
            gs.hop(1)
            sd.points()

        @pl.when(t == 3)
        def _():
            gs.hop(2)

        return carry

    lax.fori_loop(0, 4, attend_back, 0)
    total[...] = jnp.zeros_like(total)

    def joint_back(t, carry):
        total[...] += dot(hidden[t, :, :CUT], whole(full_a[t])[:, :CUT], ((1,), (1,)))
        return carry

    lax.fori_loop(0, 4, joint_back, 0)
    xhat, inverse = norm_parts(tokens[...].astype(F32))
    gain_one_sum = jnp.sum(total[...] * xhat, axis=0, keepdims=True)
    grad_n[...] = jnp.zeros_like(grad_n)
    for d in range(8):
        cols = slice(d * piece, (d + 1) * piece)
        for t in range(4):
            spot = (t, d // 4, (d // 2) % 2, d % 2)
            grad_n[spot + (slice(0, 1), slice(0, piece))] = gain_one_sum[:, cols]
            grad_n[spot + (slice(1, 2), slice(0, piece))] = gain_two_sum[:, cols]
    sn.start()
    flipped = norm_one[mine].T

    def attend_grad(t, carry):
        block = dot(flipped, hidden[t, :, :CUT]).astype(BF)
        grad_a[t, :, :, :, :, :CUT] = block.reshape((2, 2, 2, piece, CUT))
        return carry

    lax.fori_loop(0, 4, attend_grad, 0)
    for chunk in sa:
        chunk.start()
    sn.planes()
    sn.spread()
    su.lines()
    sp.lines()
    sa[0].planes()
    sa[0].spread()
    sa[1].planes()
    sa[1].spread()
    gs.hop(3)
    sa[2].planes()
    d_resid[...] += norm_back(total[...] * gain_first, xhat, inverse)
    stores[1].start()
    sn.lines()
    su.points()
    sa[0].lines()
    sa[2].spread()
    sn.points()
    sp.result(share_p)
    stores[2].start()
    gs.forward()
    sa[1].lines()
    sa[0].points()
    gs.across()
    share_d[...] = sd.result()
    stores[3].start()
    share_n[...] = sn.result()
    stores[6].start()
    sa[2].lines()
    sa[1].points()
    gs.last()
    stores[9].start()
    share_u[...] = su.result()
    stores[4].start()
    sa[2].points()
    for chunk, part in zip(sa, parts):
        share_a[part] = chunk.result()
    stores[5].start()
    for transfer in (gs, sp, sd, su, sn, sc, *sa, line_row, line_all, back_halo):
        transfer.drain()
    for store in stores:
        store.wait()


def vmem_specs(count):
    return [pl.BlockSpec(memory_space=pltpu.VMEM)] * count


def any_specs(count):
    return [pl.BlockSpec(memory_space=pl.ANY)] * count


def step_call(tokens, segments, mask_grad, params):
    own, width = tokens.shape
    gain_one, attend, output, gain_two, up, down, patch, classed, embed = params
    classes = embed.shape[0]
    rows_e = -(-(classes + 2) // 32) * 32
    piece, high, narrow = up.shape[0], up.shape[1], patch.shape[1]
    span = own + 2 * HALO
    low = lambda *shape: pltpu.VMEM(shape, BF)
    wide = lambda *shape: pltpu.VMEM(shape, F32)
    shape = jax.ShapeDtypeStruct
    operands = (tokens, segments, mask_grad, gain_one[None], attend, output, gain_two[None])
    operands += tuple(params[4:])
    outs = [
        shape((classes, own), F32),
        shape((own, width), F32),
        shape((piece, narrow), F32),
        shape((piece, high), F32),
        shape((piece, high), F32),
        shape((piece, width), F32),
        shape((8, 128), F32),
        shape((4, rows_e, narrow), BF),
        shape((4, piece, narrow), BF),
        shape((4, 2, 2, 2, TILE_ROWS, TILE_COLS), BF),
    ]
    scratch = [pltpu.VMEM(v.shape, v.dtype) for v in operands]
    scratch += [pltpu.VMEM(v.shape, v.dtype) for v in outs]
    scratch += [
        low(4, 2, 2, 2, piece, width),
        low(4, 2, 2, 2, piece, high),
        low(4, 2, 2, 2, piece, high),
        low(4, 2, 2, 2, piece, narrow),
        low(2, 2, 2, piece, narrow),
        low(2, 2, 2, rows_e, piece),
        low(4, 2, 2, 2, piece, high),
        low(4, 2, 2, 2, piece, high),
        low(4, 2, 2, 2, piece, narrow),
        wide(4, 2, 2, 2, 8, 128),
        low(4, 2, 2, 2, TILE_ROWS, TILE_COLS),
        low(4, span, CUT),
        low(4, own, narrow),
        wide(own, width),
        low(own, width),
        low(4, own, high),
        low(4, own, high),
        wide(own, width),
        low(span, width),
        low(span, width),
        low(rows_e, width),
        wide(rows_e, piece),
        low(own, width),
        low(4, own, narrow),
        low(4, rows_e, narrow),
        low(4, HEAD_SET, span, span),
        low(span, own),
        wide(1, segments.shape[1] + 2 * HALO),
        wide(span, 1),
        wide(1, span),
        wide(rows_e, width),
        low(3, piece, width),
    ]
    scratch += [
        low(4, 2, 2, piece, narrow),
        low(2, piece // 2, narrow),
        low(2, piece // 2, narrow),
        low(piece // 2, narrow),
        low(piece // 2, narrow),
        low(3, 2, 2, piece, narrow),
    ]
    for rows, cols, dtype in (
        (piece, high, BF),
        (piece, high, BF),
        (8, 128, F32),
        (TILE_ROWS, TILE_COLS, BF),
    ):
        scratch += scatter_buffers(rows, cols, dtype)
    scratch += [
        pltpu.SemaphoreType.DMA((7, 23)),
        pltpu.SemaphoreType.DMA((7, 23)),
        pltpu.SemaphoreType.DMA((8, 9)),
        pltpu.SemaphoreType.DMA((8, 9)),
        pltpu.SemaphoreType.DMA((4, 3)),
        pltpu.SemaphoreType.DMA((2, 4)),
        pltpu.SemaphoreType.DMA((len(operands),)),
        pltpu.SemaphoreType.DMA((len(outs),)),
    ]
    return pl.pallas_call(
        step_kernel,
        out_shape=outs,
        in_specs=any_specs(len(operands)),
        out_specs=any_specs(len(outs)),
        scratch_shapes=scratch,
        compiler_params=pltpu.CompilerParams(
            collective_id=0, has_side_effects=True, vmem_limit_bytes=VMEM_LIMIT
        ),
    )(*operands)


def update_kernel(*refs):
    inputs, outputs, held = refs[:37], refs[37:57], refs[57:94]
    class_back, sum_wide, in_sems, out_sems = refs[94:]
    masks, token_grad, share_p, share_d, share_u, share_a, share_n = held[:7]
    class_all, class_row, class_sum = held[7:10]
    params, means, squares = held[10:19], held[19:28], held[28:37]
    loads = loader(inputs, held, in_sems)
    stores = loader(held[:2] + squares + means, outputs, out_sems)
    order = (8, 7, 4, 5, 1, 2, 6, 0, 3)
    for n in (7, 8, 9, 18, 0, 1, 6, 2, 4, 3, 5):
        loads[n].start()
    for n in order:
        for k in (10, 19, 28):
            if k + n != 18:
                loads[k + n].start()
    for n in (7, 8, 9):
        loads[n].wait()

    def update(n, gradient):
        scale = block_scale if n < 6 else 1.0
        decay = 0.0 if n in (0, 3) else weight_decay
        for k in (10, 19, 28):
            if k + n != 18:
                loads[k + n].wait()
        squares[n][...], means[n][...] = adamw_update(
            params[n][...], gradient, means[n][...], squares[n][...], scale, decay
        )
        stores[2 + n].start()
        stores[11 + n].start()

    piece = share_p.shape[0]
    classes = params[8].shape[0]
    narrow = class_all.shape[2]
    tiles = sum_wide.shape[1] // TILE_COLS
    for i in range(sum_wide.shape[0] // TILE_ROWS * tiles):
        r, q = i // tiles, i % tiles
        sum_wide[
            r * TILE_ROWS : (r + 1) * TILE_ROWS, q * TILE_COLS : (q + 1) * TILE_COLS
        ] = class_sum[i // 8, (i // 4) % 2, (i // 2) % 2, i % 2].astype(F32)
    square = jnp.zeros((classes, 1), F32)
    for t in range(4):
        value = class_all[t, :classes].astype(F32)
        square += jnp.sum(value * value, axis=-1, keepdims=True)
    inverse = lax.rsqrt(square + epsilon_unit)
    along = jnp.zeros((classes, 1), F32)
    for t in range(4):
        unit = class_all[t, :classes].astype(F32) * inverse
        d_unit = sum_wide[:classes, t * narrow : (t + 1) * narrow]
        along += jnp.sum(unit * d_unit, axis=-1, keepdims=True)
    share_embed = jnp.zeros((classes, piece), F32)
    loads[18].wait()
    embed_low = params[8][...].astype(BF)
    for t in range(4):
        unit = class_all[t, :classes].astype(F32) * inverse
        d_unit = sum_wide[:classes, t * narrow : (t + 1) * narrow]
        value = (inverse * (d_unit - unit * along)).astype(BF)
        class_back[t] = value
        share_embed += dot(value, class_row[t], ((1,), (1,)))
    update(8, share_embed)
    update(7, dot(embed_low, class_back[lax.axis_index("tensor")], ((0,), (0,))))
    for n in range(7):
        loads[n].wait()
        if n < 2:
            stores[n].start()
    update(4, share_u[...])
    update(5, share_d[...])
    update(1, share_a[:, :CUT])
    update(2, share_a[:, CUT:].T)
    update(6, share_p[...])
    update(0, share_n[0:1, 0:piece])
    update(3, share_n[1:2, 0:piece])

    for store in stores:
        store.wait()


def update_call(results, params, means, squares):
    flat = lambda arrays: [a[None] if a.ndim == 1 else a for a in arrays]
    params, means, squares = flat(params), flat(means), flat(squares)
    classes, narrow = params[8].shape[0], params[7].shape[1]
    rows_e, width = results[7].shape[1], results[1].shape[1]
    operands = (*results, *params, *means, *squares)
    shape = jax.ShapeDtypeStruct
    outs = [shape(r.shape, F32) for r in results[:2]]
    outs += [shape(p.shape, F32) for p in params] * 2
    return pl.pallas_call(
        update_kernel,
        out_shape=outs,
        in_specs=any_specs(len(operands)),
        out_specs=any_specs(len(outs)),
        scratch_shapes=[pltpu.VMEM(v.shape, v.dtype) for v in operands]
        + [
            pltpu.VMEM((4, classes, narrow), BF),
            pltpu.VMEM((rows_e, width), F32),
            pltpu.SemaphoreType.DMA((len(operands),)),
            pltpu.SemaphoreType.DMA((len(outs),)),
        ],
        compiler_params=pltpu.CompilerParams(vmem_limit_bytes=VMEM_LIMIT),
    )(*operands)


def finish(masks, token_grad, grads, params, means, squares):
    scales = (block_scale,) * 6 + (1.0,) * 3
    decays = (0.0, weight_decay, weight_decay, 0.0) + (weight_decay,) * 5
    new = [adamw_update(*v) for v in zip(params, grads, means, squares, scales, decays)]
    return (masks, token_grad) + tuple(n[0] for n in new) + tuple(n[1] for n in new)


def gather_plain(shards, embed):
    def full(s):
        return lax.all_gather(lax.all_gather(s, "dp", axis=0), "tensor", axis=0)

    return [full(s) for s in shards] + [lax.all_gather(embed, "dp", axis=0)]


def scatter_plain(grads):
    def share(g):
        part = lax.psum_scatter(g, "dp", scatter_dimension=1, tiled=True)
        return lax.psum_scatter(part, "tensor", scatter_dimension=0, tiled=True)[0]

    return [share(g).astype(F32) for g in grads]


def with_halo(rows, parts):
    forward = [(i, i + 1) for i in range(parts - 1)]
    backward = [(i + 1, i) for i in range(parts - 1)]
    before = lax.ppermute(rows[-HALO:], "tensor", forward)
    after = lax.ppermute(rows[:HALO], "tensor", backward)
    return jnp.concatenate((before, rows, after), axis=0)


def local_plain(
    parts,
    tokens,
    segments,
    mask_grad,
    gain_one,
    attend_weight,
    output_weight,
    gain_two,
    up_weight,
    down_weight,
    patch_weight,
    class_weight,
    class_embed,
    *moments,
):
    means, squares = moments[:9], moments[9:]
    own = tokens.shape[0]
    width = tokens.shape[1]
    classes = class_embed.shape[0]
    dp_index = lax.axis_index("dp")
    tensor_index = lax.axis_index("tensor")
    low = lambda v: v.astype(BF)

    shard_a = jnp.concatenate((low(attend_weight), low(output_weight).T), axis=1)
    shard_u = low(up_weight)
    shard_d = low(down_weight).T
    shard_p = jnp.concatenate((low(patch_weight), low(class_weight)), axis=1)
    rows_e = -(-(classes + 2) // 32) * 32
    shard_e = jnp.zeros((rows_e, class_embed.shape[1]), BF)
    shard_e = shard_e.at[:classes].set(low(class_embed))
    shard_e = shard_e.at[classes].set(low(gain_one)).at[classes + 1].set(low(gain_two))
    full_a, full_u, full_d, full_p, full_e = gather_plain(
        (shard_a, shard_u, shard_d, shard_p), shard_e
    )
    full_a, full_u, full_d, full_p = (
        v.reshape(v.shape[0], width, v.shape[-1]) for v in (full_a, full_u, full_d, full_p)
    )
    embed_rows = full_e.transpose(1, 0, 2).reshape(rows_e, width)
    embed = embed_rows[:classes]
    gain_first = embed_rows[classes].astype(F32)[None]
    gain_second = embed_rows[classes + 1].astype(F32)[None]

    cut = attend_weight.shape[1]
    heads = cut // (3 * HD)
    w_attend, w_output = full_a[:, :, :cut], full_a[:, :, cut:]
    narrow = patch_weight.shape[1]
    w_patch, w_class = full_p[:, :, :narrow], full_p[:, :, narrow:]
    w_patch = w_patch.transpose(1, 0, 2).reshape(width, -1)
    w_class = w_class.transpose(1, 0, 2).reshape(width, -1)

    window = with_halo(tokens, parts)
    token_wide = window.astype(F32)
    xhat_one, inverse_one = norm_parts(token_wide)
    norm_one = low(xhat_one * gain_first)
    joint = jnp.einsum("sd,tdn->stn", norm_one, w_attend, preferred_element_type=F32)
    joint = low(joint).reshape(own + 2 * HALO, parts * heads, 3, HD)
    queries, keys, values = joint[:, :, 0], joint[:, :, 1], joint[:, :, 2]
    padded = jnp.pad(segments[0], HALO, constant_values=-1)
    seg = lax.dynamic_slice_in_dim(padded, tensor_index * own, own + 2 * HALO, 0)
    scores = jnp.einsum("qhd,khd->hqk", queries, keys, preferred_element_type=F32) * HD**-0.5
    scores = jnp.where(seg[None, :, None] == seg[None, None, :], scores, masked_score)
    exponent = jnp.exp(scores - jnp.max(scores, axis=-1, keepdims=True))
    prob = exponent / jnp.sum(exponent, axis=-1, keepdims=True)
    prob_low = low(prob)
    mine = slice(HALO, HALO + own)
    attended = jnp.einsum(
        "hqk,khd->qhd", prob_low[:, mine], values, preferred_element_type=F32
    )
    attended = low(attended).reshape(own, parts, heads * HD)
    resid_one = token_wide[mine] + jnp.einsum(
        "stn,tdn->sd", attended, w_output, preferred_element_type=F32
    )
    xhat_two, inverse_two = norm_parts(resid_one)
    norm_two = low(xhat_two * gain_second)
    hidden_pre = jnp.einsum("sd,tdn->stn", norm_two, full_u, preferred_element_type=F32)
    hidden, gelu_back = jax.vjp(lambda v: jax.nn.gelu(v, approximate=False), hidden_pre)
    hidden = low(hidden)
    resid_two = resid_one + jnp.einsum(
        "stn,tdn->sd", hidden, full_d, preferred_element_type=F32
    )
    resid_low = low(resid_two)
    patch_feat = dot(resid_low, w_patch)
    patch_wide, patch_inverse = unit_parts(patch_feat)
    patch_unit = low(patch_wide)
    class_feat = dot(embed, w_class)
    class_wide, class_inverse = unit_parts(class_feat)
    class_unit = low(class_wide)
    products = dot(patch_unit, class_unit, ((1,), (1,)))
    masks, mask_inverse = norm_parts(products)
    d_products = low(norm_back(mask_grad, masks, mask_inverse))
    d_class_unit = lax.psum(dot(d_products, patch_unit, ((0,), (0,))), ("dp", "tensor"))
    d_patch_unit = dot(d_products, class_unit)
    d_patch_feat = low(unit_back(d_patch_unit, patch_wide, patch_inverse))
    grad_patch = dot(resid_low, d_patch_feat, ((0,), (0,)))
    d_resid_two = dot(d_patch_feat, w_patch, ((1,), (1,)))
    d_branch_two = low(d_resid_two)
    d_hidden = jnp.einsum("sd,tdn->stn", d_branch_two, full_d, preferred_element_type=F32)
    grad_down = jnp.einsum("sd,stn->tdn", d_branch_two, hidden, preferred_element_type=F32)
    d_hidden_pre = low(gelu_back(d_hidden)[0])
    grad_up = jnp.einsum("sd,stn->tdn", norm_two, d_hidden_pre, preferred_element_type=F32)
    d_norm_two = jnp.einsum("stn,tdn->sd", d_hidden_pre, full_u, preferred_element_type=F32)
    d_resid_one = d_resid_two + norm_back(d_norm_two * gain_second, xhat_two, inverse_two)
    grad_gain_two = jnp.sum(d_norm_two * xhat_two, axis=0)
    d_branch_one = with_halo(low(d_resid_one), parts)
    d_attended = low(
        jnp.einsum("sd,tdn->stn", d_branch_one, w_output, preferred_element_type=F32)
    )
    grad_output = jnp.einsum(
        "sd,stn->tdn", d_branch_one[mine], attended, preferred_element_type=F32
    )
    d_attended = d_attended.reshape(own + 2 * HALO, parts * heads, HD)
    d_prob = jnp.einsum("qhd,khd->hqk", d_attended, values, preferred_element_type=F32)
    delta = jnp.sum(prob * d_prob, axis=-1, keepdims=True)
    d_scores = low(prob * (d_prob - delta))
    d_query = jnp.einsum(
        "hqk,khd->qhd", d_scores[:, mine], keys, preferred_element_type=F32
    )
    d_key = jnp.einsum(
        "hqk,qhd->khd", d_scores[:, :, mine], queries, preferred_element_type=F32
    )
    d_value = jnp.einsum(
        "hqk,qhd->khd", prob_low[:, :, mine], d_attended, preferred_element_type=F32
    )
    d_joint = low(
        jnp.stack((d_query * HD**-0.5, d_key * HD**-0.5, d_value), axis=2)
    ).reshape(own, parts, cut)
    grad_attend = jnp.einsum(
        "sd,stn->tdn", norm_one[mine], d_joint, preferred_element_type=F32
    )
    d_norm_one = jnp.einsum("stn,tdn->sd", d_joint, w_attend, preferred_element_type=F32)
    token_grad = d_resid_one + norm_back(
        d_norm_one * gain_first, xhat_one[mine], inverse_one[mine]
    )
    grad_gain_one = jnp.sum(d_norm_one * xhat_one[mine], axis=0)

    grad_patch = grad_patch.reshape(width, parts, narrow).transpose(1, 0, 2)
    share_p, share_d, share_u, share_a = scatter_plain(
        [
            grad_patch,
            grad_down,
            grad_up,
            jnp.concatenate((grad_attend, grad_output), axis=2),
        ]
    )
    gains = lax.psum((grad_gain_one, grad_gain_two), ("dp", "tensor"))
    step = gain_one.shape[0]
    share_one, share_two = (lax.dynamic_slice_in_dim(g, dp_index * step, step, 0) for g in gains)
    d_class_feat = low(unit_back(d_class_unit, class_wide, class_inverse))
    d_class_own = lax.dynamic_slice_in_dim(d_class_feat, tensor_index * narrow, narrow, 1)
    share_class = dot(low(class_embed), d_class_own, ((0,), (0,)))
    class_rows = lax.dynamic_slice_in_dim(w_class, dp_index * step, step, 0)
    share_embed = dot(d_class_feat, class_rows, ((1,), (1,)))
    return finish(
        masks,
        token_grad,
        (
            share_one,
            share_a[:, :cut],
            share_a[:, cut:].T,
            share_two,
            share_u,
            share_d.T,
            share_p,
            share_class,
            share_embed,
        ),
        (
            gain_one,
            attend_weight,
            output_weight,
            gain_two,
            up_weight,
            down_weight,
            patch_weight,
            class_weight,
            class_embed,
        ),
        means,
        squares,
    )


def local_kernels(tokens, segments, mask_grad, *arrays):
    def turned(group):
        return (*group[:5], group[5].T, *group[6:])

    params, means, squares = (turned(arrays[n : n + 9]) for n in (0, 9, 18))
    results = step_call(tokens, segments, mask_grad.T, params)
    masks, token_grad, *new = update_call(results, params, means, squares)
    new = [n.reshape(p.shape) for n, p in zip(new, params * 2)]
    return (masks.T, token_grad, *turned(new[:9]), *turned(new[9:]))


def solution(mesh):
    parts = mesh.shape["tensor"]
    custom = mesh.shape["dp"] == 8 and parts == 4
    params = (
        P("dp"),
        P("dp", "tensor"),
        P("tensor", "dp"),
        P("dp"),
        P("dp", "tensor"),
        P("tensor", "dp"),
        P("dp", "tensor"),
        P("dp", "tensor"),
        P(None, "dp"),
    )
    rows = P(("dp", "tensor"), None)
    return jax.shard_map(
        local_kernels if custom else functools.partial(local_plain, parts),
        mesh=mesh,
        in_specs=(rows, P("dp", None), rows) + params * 3,
        out_specs=(rows, rows) + params * 2,
        check_vma=False,
    )
```
